32 devices in a mesh: slab: 8 (over y, x, core), grp: 4 (over z).
Axes of the slice: x: 2, y: 2, z: 4, core: 2. Of those that a mesh axis runs over, the one named last changes fastest.
Arguments:
- resid7: float32 [512, 4096], P(None, ('slab', 'grp')), may hold values from -6 to 6
- interp73: float32 [8, 4], replicated, may hold values from -2 to 2
- interp31: float32 [4, 2], replicated, may hold values from -4 to 4
- elem_ops: float32 [8, 8, 4096], P(None, None, 'slab'), as said below
- conn: int32 [8, 4096], P(None, 'slab'), may hold values from 0 to 1121, as said below
- faces: int32 [2, 8, 561], P(None, 'slab'), may hold values from 0 to 1121, as said below
Outputs:
- correction3: float32 [64, 4096], P(None, ('slab', 'grp'))
The draws below stay inside these ranges and needn't reach their ends.
Inputs may be any that keep to these rules, and one draw needn't show every extreme that they name: `conn`: the 512 columns of a slab describe a block of 32 x 16 x 1 hexahedra stacked along the long direction; column e lists the corners of one element, the corner at offsets (i, j, k) along (long, second, first direction) in row 4 i + 2 j + k; the slab's nodes are numbered 0 to 1121 in some order and every one of them is a corner of some element. faces[0, s] lists the 561 nodes of slab s on its face toward slab s - 1, faces[1, s] those on its face toward slab s + 1, all distinct; faces[1, s, f] and faces[0, s + 1, f] are the same point of the mesh. `elem_ops`: each element's matrix is symmetric, and each diagonal entry is positive and larger than the sum of magnitudes of the other entries of its row.
All inputs are finite; a program needn't handle non-finite values.
Results may differ from the reference program's by a relative error of at most 0.0003.
Values sent between devices are 32-bit elements; how exact they have to be, the bound alone decides.
A program may use at most 64 MiB of HBM per device.

```python
import math
import jax
import jax.numpy as jnp
from jax import lax

EX = 32
EY = 16
SWEEPS = 2
EG = 512
EZ = 1
NG = 1122
FACE = 561
ELEMS = 4096
N_SLAB = 8


def pin_ends(perm):
    top_at = jnp.argmax(perm == NG - 1)
    first = perm[0]
    perm = perm.at[top_at].set(first).at[0].set(NG - 1)
    target = EZ * FACE
    low_at = jnp.argmax(perm == 0)
    moved = perm[target]
    perm = perm.at[low_at].set(moved).at[target].set(0)
    return perm.astype(jnp.int32)


def slab_layout(key):
    base = jax.random.fold_in(key, 11)
    node_keys = jax.random.split(jax.random.fold_in(base, 1), N_SLAB)
    elem_keys = jax.random.split(jax.random.fold_in(base, 2), N_SLAB)
    node_perm = jax.vmap(lambda one: pin_ends(jax.random.permutation(one, NG).astype(jnp.int32)))(node_keys)
    elem_perm = jax.vmap(lambda one: jax.random.permutation(one, EG))(elem_keys).astype(jnp.int32)
    along_x = elem_perm % EX
    along_y = elem_perm // EX % EY
    along_z = elem_perm // (EX * EY)
    corner = jnp.arange(8, dtype=jnp.int32)
    off_z = (corner // 4)[None, :, None]
    off_y = (corner // 2 % 2)[None, :, None]
    off_x = (corner % 2)[None, :, None]
    lexical = ((along_z[:, None, :] + off_z) * (EY + 1) + along_y[:, None, :] + off_y) * (EX + 1) + along_x[:, None, :] + off_x
    corners = jax.vmap(lambda perm, where: perm[where])(node_perm, lexical)
    plane = jnp.arange(FACE, dtype=jnp.int32)
    lower = node_perm[:, plane]
    upper = node_perm[:, plane + EZ * FACE]
    return (corners.transpose(1, 0, 2).reshape(8, N_SLAB * EG), jnp.stack([lower, upper]))


def draw_conn(key, part):
    return slab_layout(key)[0]


def draw_faces(key, part):
    return slab_layout(key)[1]


def draw_elem_ops(key, part):
    first, second, third = jax.random.split(jax.random.fold_in(key, 5), 3)
    low_scale = 0.02
    raw = jax.random.uniform(first, (8, 8, ELEMS), jnp.float32, minval=-0.5, maxval=0.5)
    sym = 0.5 * (raw + jnp.swapaxes(raw, 0, 1))
    identity = jnp.eye(8, dtype=jnp.float32)[:, :, None]
    diagonal = 4.0 + jax.random.uniform(second, (8, ELEMS), jnp.float32)
    scale = jnp.exp(jax.random.uniform(third, (ELEMS,), jnp.float32, minval=math.log(low_scale), maxval=math.log(0.2)))
    return scale[None, None, :] * (sym * (1.0 - identity) + identity * diagonal[:, None, :])


def shard_levels(stream_key, extent, cuts, smallest, top_value):
    factor_of, own = 1.0, jax.random.fold_in(stream_key, 6)
    for dim, parts in cuts:
        draws = jnp.exp(jax.random.uniform(jax.random.fold_in(own, dim), (parts,), jnp.float32, smallest / len(cuts), top_value / len(cuts)))
        factor_of = factor_of * jnp.repeat(draws, extent[dim] // parts).reshape([-1 if axis == dim else 1 for axis in range(len(extent))])
    return factor_of


def normal_values(key, extent, deviation, most, cuts=(), kind=jnp.bfloat16):
    values = jax.random.normal(key, extent, jnp.float32) * deviation
    if len(cuts) > 0:
        values = shard_levels(key, extent, cuts, -0.22, 0.18) * values
    return jnp.clip(values, min=-most, max=most).astype(kind)


def setup_inputs(seed: int = 0) -> dict:
    key_of = jax.random.split(jax.random.key(seed), 7)
    return {
        "resid7": normal_values(key_of[0], (512, ELEMS), 1.0, 6.0, ((1, 32),), jnp.float32),
        "interp73": normal_values(key_of[1], (8, 4), 8 ** -0.5, 2.0, (), jnp.float32),
        "interp31": normal_values(key_of[2], (4, 2), 2 ** -0.5, 4.0, (), jnp.float32),
        "elem_ops": draw_elem_ops(jax.random.fold_in(key_of[6], 71), 0),
        "conn": draw_conn(jax.random.fold_in(key_of[6], 71), 0),
        "faces": draw_faces(jax.random.fold_in(key_of[6], 71), 0),
    }


lam_low = 0.3
lam_high = 1.9


def restrict(block, interp73, interp31):
    hi = lax.Precision.HIGHEST
    width = block.shape[1]
    cube = block.reshape(8, 8, 8, width)
    cube = jnp.einsum("kc,ijkm->ijcm", interp73, cube, precision=hi)
    cube = jnp.einsum("jb,ijcm->ibcm", interp73, cube, precision=hi)
    cube = jnp.einsum("ia,ibcm->abcm", interp73, cube, precision=hi)
    cube = jnp.einsum("kc,ijkm->ijcm", interp31, cube, precision=hi)
    cube = jnp.einsum("jb,ijcm->ibcm", interp31, cube, precision=hi)
    cube = jnp.einsum("ia,ibcm->abcm", interp31, cube, precision=hi)
    return cube.reshape(8, width)


def prolong(coarse, interp31):
    hi = lax.Precision.HIGHEST
    width = coarse.shape[1]
    cube = coarse.reshape(2, 2, 2, width)
    cube = jnp.einsum("ck,ijkm->ijcm", interp31, cube, precision=hi)
    cube = jnp.einsum("bj,ijcm->ibcm", interp31, cube, precision=hi)
    cube = jnp.einsum("ai,ibcm->abcm", interp31, cube, precision=hi)
    return cube.reshape(64, width)


def reference(resid7, interp73, interp31, elem_ops, conn, faces):
    hi = lax.Precision.HIGHEST

    def reduce_slab(index):
        block = lax.dynamic_slice_in_dim(resid7, index * EG, EG, 1)
        return restrict(block, interp73, interp31)

    coarse_res = lax.map(reduce_slab, jnp.arange(N_SLAB, dtype=jnp.int32))
    conn_slab = conn.reshape(8, N_SLAB, EG).transpose(1, 0, 2)
    ops_slab = elem_ops.reshape(8, 8, N_SLAB, EG).transpose(2, 0, 1, 3)
    lower = faces[0]
    upper = faces[1]

    def assemble(values):
        return jax.vmap(lambda vals, ids: jax.ops.segment_sum(vals.reshape(-1), ids.reshape(-1), num_segments=NG))(values, conn_slab)

    def share(nodes):
        bottom = jnp.take_along_axis(nodes, lower, 1)
        top = jnp.take_along_axis(nodes, upper, 1)
        zero_row = jnp.zeros((1, FACE), jnp.float32)
        below = jnp.concatenate([zero_row, top[:-1]], axis=0)
        above = jnp.concatenate([bottom[1:], zero_row], axis=0)
        return jax.vmap(lambda node, low, upp, bel, abo: node.at[low].add(bel).at[upp].add(abo))(nodes, lower, upper, below, above)

    def pick(field):
        return jax.vmap(lambda values, ids: values[ids])(field, conn_slab)

    def operate(field):
        local = jnp.einsum("spqe,sqe->spe", ops_slab, pick(field), precision=hi)
        return share(assemble(local))

    rhs = share(assemble(coarse_res))
    diag = share(assemble(jnp.einsum("sppe->spe", ops_slab)))
    theta = 0.5 * (lam_high + lam_low)
    delta = 0.5 * (lam_high - lam_low)
    sigma = theta / delta
    inverse = 1.0 / diag
    direction = inverse * rhs / theta
    solution = direction
    remain = rhs
    rho = 1.0 / sigma
    for sweep in range(SWEEPS):
        remain = remain - operate(direction)
        rho_new = 1.0 / (2.0 * sigma - rho)
        direction = (rho_new * rho) * direction + (2.0 * rho_new / delta) * inverse * remain
        solution = solution + direction
        rho = rho_new
    picked = pick(solution).transpose(1, 0, 2).reshape(8, ELEMS)
    return prolong(picked, interp31)
```

```python
import functools

import jax
import jax.numpy as jnp
from jax import lax
from jax.experimental import pallas as pl
from jax.experimental.pallas import tpu as pltpu
from jax.sharding import PartitionSpec as P

EX = 32
EY = 16
SWEEPS = 2


lam_low = 0.3
lam_high = 1.9


def extended(array, sides, width):
    for axis, dim in sides:
        count, length = (lax.axis_size(axis), array.shape[dim])
        up = [(i, (i + 1) % count) for i in range(count - 1)]
        down = [(j, i) for i, j in up]
        last = lax.slice_in_dim(array, length - width, length, axis=dim)
        first = lax.slice_in_dim(array, 0, width, axis=dim)
        before = lax.ppermute(last, axis, up)
        after = lax.ppermute(first, axis, down)
        array = jnp.concatenate([before, array, after], axis=dim)
    return array


def restrict_high(block, interp73):
    hi = lax.Precision.HIGHEST
    width = block.shape[1]
    cube = block.reshape(8, 8, 8, width)
    cube = jnp.einsum("kc,ijkm->ijcm", interp73, cube, precision=hi)
    cube = jnp.einsum("jb,ijcm->ibcm", interp73, cube, precision=hi)
    cube = jnp.einsum("ia,ibcm->abcm", interp73, cube, precision=hi)
    return cube.reshape(64, width)


def restrict_low(block, interp31):
    hi = lax.Precision.HIGHEST
    width = block.shape[1]
    cube = block.reshape(4, 4, 4, width)
    cube = jnp.einsum("kc,ijkm->ijcm", interp31, cube, precision=hi)
    cube = jnp.einsum("jb,ijcm->ibcm", interp31, cube, precision=hi)
    cube = jnp.einsum("ia,ibcm->abcm", interp31, cube, precision=hi)
    return cube.reshape(8, width)


def prolong(coarse, interp31):
    hi = lax.Precision.HIGHEST
    width = coarse.shape[1]
    cube = coarse.reshape(2, 2, 2, width)
    cube = jnp.einsum("ck,ijkm->ijcm", interp31, cube, precision=hi)
    cube = jnp.einsum("bj,ijcm->ibcm", interp31, cube, precision=hi)
    cube = jnp.einsum("ai,ibcm->abcm", interp31, cube, precision=hi)
    return cube.reshape(64, width)


def assemble(values, conn_ids, count):
    layers = values.shape[0]
    flat = values.reshape(layers, -1).T
    summed = jax.ops.segment_sum(flat, conn_ids.reshape(-1), num_segments=count)
    return summed.T


def element_term(operators, conn_ids, field):
    return jnp.einsum("pqe,qe->pe", operators, field[conn_ids], precision=lax.Precision.HIGHEST)


def share(nodes, faces):
    lower = faces[0, 0]
    upper = faces[1, 0]
    planes = jnp.stack([nodes[:, lower], nodes[:, upper]], axis=1)
    padded = extended(planes, (("slab", 1),), 1)
    return nodes.at[:, lower].add(padded[:, 0]).at[:, upper].add(padded[:, 3])


def local(resid7, interp73, interp31, elem_ops, conn, faces):
    own = resid7.shape[1]
    slab_elems = conn.shape[1]
    layers = slab_elems // (EX * EY)
    count = (EX + 1) * (EY + 1) * (layers + 1)
    start = lax.axis_index("grp") * own
    own_conn = lax.dynamic_slice_in_dim(conn, start, own, 1)
    middle_res = restrict_high(resid7, interp73)
    blocks = lax.all_gather(middle_res, "grp", axis=1, tiled=True)
    slab_res = restrict_low(blocks, interp31)
    pair = jnp.stack([slab_res, jnp.einsum("ppe->pe", elem_ops)])
    both_nodes = assemble(pair, conn, count)
    shared = share(both_nodes, faces)
    rhs = shared[0]
    diag = shared[1]
    theta = 0.5 * (lam_high + lam_low)
    delta = 0.5 * (lam_high - lam_low)
    sigma = theta / delta
    inverse = 1.0 / diag
    direction = inverse * rhs / theta
    solution = direction
    remain = rhs
    rho = 1.0 / sigma
    for sweep in range(SWEEPS):
        nodes = assemble(element_term(elem_ops, conn, direction)[None], conn, count)
        remain = remain - share(nodes, faces)[0]
        rho_new = 1.0 / (2.0 * sigma - rho)
        direction = rho_new * rho * direction + 2.0 * rho_new / delta * inverse * remain
        solution = solution + direction
        rho = rho_new
    return prolong(solution[own_conn], interp31)


STRIDE = EX + 1
POINTS = (EX + 1) * (EY + 1)
LANES = (POINTS + 127) // 128 * 128
LINE = EX * EY
BLOCKS = LINE // 128
REACH = SWEEPS + 1
TURNS = ((0, 1), (1, -1), (1, 0), (1, 1))
ROWS = 2 * (len(TURNS) + 1) + 2 * len(TURNS) + 1
MESH = pl.DeviceIdType.MESH
VMEM = pl.BlockSpec(memory_space=pltpu.VMEM)
SMEM = pl.BlockSpec(memory_space=pltpu.SMEM)


def rows_of(shape):
    return lax.broadcasted_iota(jnp.int32, shape, 0)


def spread(row, count=8):
    return jnp.broadcast_to(row, (count, row.shape[1]))


def stack_rows(rows):
    sub = rows_of((8, rows[0].shape[1]))
    out = spread(rows[0])
    for at in range(1, 8):
        out = jnp.where(sub == at, spread(rows[at]), out)
    return out


def parts_of(value):
    hi = value.astype(jnp.bfloat16).astype(jnp.float32)
    left = value - hi
    mid = left.astype(jnp.bfloat16).astype(jnp.float32)
    return jnp.concatenate([hi, mid, left - mid], axis=0).astype(jnp.bfloat16)


def join_parts(value):
    third = value.shape[0] // 3
    return value[:third] + value[third : 2 * third] + value[2 * third :]


def gather_sums(corners):
    sub = rows_of(corners.shape)
    odd, second = ((sub & 1) == 1, (sub & 2) == 2)
    part = jnp.where(odd, pltpu.roll(corners, 1, 1), corners)
    part = part + jnp.where(odd, pltpu.roll(part, 1, 0), pltpu.roll(part, 7, 0))
    part = jnp.where(second, pltpu.roll(part, STRIDE, 1), part)
    return part + jnp.where(second, pltpu.roll(part, 2, 0), pltpu.roll(part, 6, 0))


def aligned(value):
    sub = rows_of(value.shape)
    part = jnp.where((sub & 1) == 1, pltpu.roll(value, 1, 1), value)
    return jnp.where((sub & 2) == 2, pltpu.roll(part, STRIDE, 1), part)


def stencil_rows(columns):
    sub = rows_of(columns[0].shape)
    odd, second = ((sub & 1) == 1, (sub & 2) == 2)

    def over_x(part):
        return part + jnp.where(odd, pltpu.roll(part, 1, 0), pltpu.roll(part, 7, 0))

    def over_y(part):
        return part + jnp.where(second, pltpu.roll(part, 2, 0), pltpu.roll(part, 6, 0))

    c0, c1, c2, c3 = columns
    centre = over_y(over_x(jnp.where(second, jnp.where(odd, c3, c2), jnp.where(odd, c1, c0))))
    along_x = over_y(jnp.where(second, jnp.where(odd, c2, c3), jnp.where(odd, c0, c1)))
    along_y = over_x(jnp.where(second, jnp.where(odd, c1, c0), jnp.where(odd, c3, c2)))
    forward = [(along_x, 0), (c2, 1), (along_y, 0), (c3, 0)]
    backward = [(along_x, 1), (c1, 2), (along_y, 2), (c0, 3)]
    return (centre, 0), forward, backward


def corner_values(nodes):
    sub = rows_of(nodes.shape)
    part = jnp.where((sub & 2) == 2, pltpu.roll(nodes, LANES - STRIDE, 1), nodes)
    return jnp.where((sub & 1) == 1, pltpu.roll(part, LANES - 1, 1), part)


def before(ids, mine, theirs):
    column = jnp.broadcast_to(ids[theirs : theirs + 1], (128, LINE)).T
    row = spread(ids[mine : mine + 1])
    place = rows_of((8, LINE)).astype(jnp.float32)
    total = jnp.zeros((8, LINE), jnp.float32)
    for at in range(LINE // 8):
        one = column[8 * at : 8 * at + 8]
        same = jnp.concatenate([one] * BLOCKS, axis=1) == row
        total = total + jnp.where(same, place + (8.0 * at + 1.0), 0.0)
    return jnp.sum(total, axis=0, keepdims=True)


def positions(conn):
    ids = conn.astype(jnp.float32)
    own = lax.broadcasted_iota(jnp.int32, (1, LINE), 1)
    rows = []
    for theirs in (1, 2):
        found = before(ids, 0, theirs).astype(jnp.int32)
        packed = jnp.where(found > 0, found - 1 + LINE, own)
        rows += [packed[:, 128 * b : 128 * b + 128] for b in range(BLOCKS)]
    state = stack_rows(rows)
    sub = rows_of((8, 128))
    for _ in range((EX - 1).bit_length()):
        target = state & (LINE - 1)
        lane, block = (target & 127, target >> 7)
        got = jnp.zeros((8, 128), jnp.int32)
        for b in range(BLOCKS):
            table = jnp.where(sub < BLOCKS, spread(state[b : b + 1]), spread(state[BLOCKS + b : BLOCKS + b + 1]))
            got = jnp.where(block == b, jnp.take_along_axis(table, lane, axis=1), got)
        state = got + (state - target)
    steps = state >> (LINE.bit_length() - 1)
    return steps + STRIDE * pltpu.roll(steps, 4, 0)


def one_hot(row):
    return jnp.where(rows_of((LANES, row.shape[1])) == spread(row, LANES), 1.0, 0.0).astype(jnp.bfloat16)


def cycle_kernel(slabs, groups, conn_hbm, ops_hbm, res_hbm, i73_hbm, i31_hbm, out_ref, conn_ref, ops_ref, res_ref, i73_ref, i31_ref, load_sem, sums_ref, coef_ref, stencil_ref, hello, sum_send, sum_recv, coef_send, coef_recv):
    slab, group = (lax.axis_index("slab"), lax.axis_index("grp"))
    offsets = [o for o in range(-REACH, REACH + 1) if o != 0]
    below, above = (jnp.minimum(slab, REACH), jnp.minimum(slabs - 1 - slab, REACH))
    every = below + above + 1

    def exists(o):
        return slab >= -o if o < 0 else slab < slabs - o

    loads = [
        pltpu.make_async_copy(source, target, load_sem.at[at])
        for at, (source, target) in enumerate(((conn_hbm, conn_ref), (i73_hbm, i73_ref), (i31_hbm, i31_ref), (res_hbm, res_ref), (ops_hbm, ops_ref)))
    ]
    for load in loads:
        load.start()
    sums_ref[...] = jnp.zeros(sums_ref.shape, jnp.float32)
    coef_ref[...] = jnp.zeros(coef_ref.shape, jnp.float32)

    def tell(semaphore, first, last, some):
        def visit(z, carry):
            pl.semaphore_signal(semaphore, inc=1, device_id=(slab, z), device_id_type=MESH)
            for o in offsets:

                @pl.when(exists(o))
                def _():
                    pl.semaphore_signal(semaphore, inc=1, device_id=(slab + o, z), device_id_type=MESH)

            return carry

        lax.fori_loop(first, last, visit, 0)
        for o in some:

            @pl.when(exists(o))
            def _():
                pl.semaphore_signal(semaphore, inc=1, device_id=(slab + o, group), device_id_type=MESH)

    barrier = pltpu.get_barrier_semaphore()
    tell(barrier, group + 1, groups, [o for o in offsets if o > 0])

    for load in loads:
        load.wait()
    place = positions(conn_ref[...])
    coef = [[sum(i73_ref[m, i] * i31_ref[a, m] for m in range(4)) for a in range(2)] for i in range(8)]
    along_j = [[None] * 8, [None] * 8]
    for j in range(8):
        for a in range(2):
            along_j[a][j] = sum(coef[i][a] * res_ref[64 * i + 8 * j : 64 * i + 8 * j + 8, :] for i in range(8))
    sub_tile = rows_of((8, 128))
    last = []
    for c in range(2):
        column = jnp.full((8, 128), coef[0][c], jnp.float32)
        for k in range(1, 8):
            column = jnp.where(sub_tile == k, coef[k][c], column)
        last.append(column)
    rows = []
    for a in range(2):
        for b in range(2):
            line = sum(coef[j][b] * along_j[a][j] for j in range(8))
            for c in range(2):
                rows.append(jnp.sum(last[c] * line, axis=0, keepdims=True))
    low_res = stack_rows(rows)

    mine = spread(place[0:1])
    for b in range(1, BLOCKS):
        mine = jnp.where(group == b, spread(place[b : b + 1]), mine)
    own_hot = one_hot(mine[0:1])
    own = join_parts(lax.dot_general(parts_of(low_res), own_hot, (((1,), (1,)), ((), ())), preferred_element_type=jnp.float32))
    nodes = gather_sums(own)
    for plane in range(2):
        sums_ref[plane, group, REACH : REACH + 1, :] = nodes[4 * plane : 4 * plane + 1]

    def sum_copy(z, o):
        return pltpu.make_async_remote_copy(
            src_ref=sums_ref.at[:, group, pl.ds(REACH, 1), :],
            dst_ref=sums_ref.at[:, group, pl.ds(REACH - o, 1), :],
            send_sem=sum_send.at[REACH + o],
            recv_sem=sum_recv.at[REACH - o],
            device_id=(slab + o, z),
            device_id_type=MESH,
        )

    def sums_from(o):
        count = groups if o else groups - 1
        return pltpu.make_async_remote_copy(
            src_ref=sums_ref.at[:, pl.ds(0, count), pl.ds(REACH, 1), :],
            dst_ref=sums_ref.at[:, pl.ds(0, count), pl.ds(REACH + o, 1), :],
            send_sem=sum_send.at[REACH + o],
            recv_sem=sum_recv.at[REACH + o],
            device_id=(slab, group),
            device_id_type=MESH,
        )

    def coef_copy(o):
        first = {1: 0, 2: 0 if o < 0 else 4, 3: 4 if o < 0 else 14}[abs(o)]
        count = {1: ROWS, 2: 15, 3: 1}[abs(o)]
        return pltpu.make_async_remote_copy(
            src_ref=coef_ref.at[pl.ds(first, count), pl.ds(REACH, 1), :],
            dst_ref=coef_ref.at[pl.ds(first, count), pl.ds(REACH - o, 1), :],
            send_sem=coef_send.at[REACH + o],
            recv_sem=coef_recv.at[REACH - o],
            device_id=(slab + o, group),
            device_id_type=MESH,
        )

    def send_sums(z, carry):
        sum_copy(z, 0).start()
        for o in offsets:

            @pl.when(exists(o))
            def _():
                sum_copy(z, o).start()

        return carry

    lower = group * every + below

    @pl.when(lower > 0)
    def _():
        pl.semaphore_wait(barrier, lower)

    tell(hello.at[group], 0, group, [o for o in offsets if o < 0])
    lax.fori_loop(0, group, send_sums, 0)
    for o in offsets:
        if o < 0:

            @pl.when(exists(o))
            def _():
                sum_copy(group, o).start()

    hot = jnp.concatenate([one_hot(place[b : b + 1]) for b in range(BLOCKS)], axis=1)
    ops = parts_of(ops_ref[...].reshape(64, LINE))
    lex = join_parts(lax.dot_general(ops, hot, (((1,), (1,)), ((), ())), preferred_element_type=jnp.float32))
    moved = [aligned(lex[8 * q : 8 * q + 8]) for q in range(8)]
    sub = rows_of((8, LANES))
    flat, flat_turns, _ = stencil_rows([jnp.where(sub < 4, moved[q], moved[q + 4]) for q in range(4)])
    centre, forward, backward = stencil_rows(moved[4:])
    rows = [(value, row) for value, row in flat_turns] + [flat, centre] + forward + backward
    rows += [(value, row + 4) for value, row in [flat] + flat_turns]
    for at, (value, row) in enumerate(rows):
        coef_ref[at, REACH : REACH + 1, :] = value[row : row + 1]
    for o in offsets:
        if o < 0:

            @pl.when(exists(o))
            def _():
                coef_copy(o).start()

    @pl.when(above > 0)
    def _():
        pl.semaphore_wait(hello.at[group], above)

    for o in offsets:
        if o > 0:

            @pl.when(exists(o))
            def _():
                sum_copy(group, o).start()
                coef_copy(o).start()

    def to_higher(z, carry):
        pl.semaphore_wait(hello.at[z], every)
        return send_sums(z, carry)

    lax.fori_loop(group + 1, groups, to_higher, 0)

    fine = []
    for k in range(2):
        column = jnp.full((8, 128), i31_ref[k, 0], jnp.float32)
        for c in range(1, 4):
            column = jnp.where((sub_tile & 3) == c, i31_ref[k, c], column)
        fine.append(column)
    weights = [jnp.where(sub_tile < 4, i31_ref[j, 2 * h], i31_ref[j, 2 * h + 1]) * fine[k] for h in range(2) for j in range(2) for k in range(2)]

    for o in offsets:

        @pl.when(exists(o))
        def _():
            coef_copy(-o).wait_recv()

    turns = len(TURNS)
    up_first = ROWS - turns
    steps = [STRIDE * dy + dx for dy, dx in TURNS]
    stencil_ref[0] = coef_ref[turns] + pltpu.roll(coef_ref[up_first - 1], 1, 0)
    middle = turns + 1
    stencil_ref[1] = pltpu.roll(coef_ref[middle], 1, 0)
    stencil_ref[2] = coef_ref[middle]
    for at, step in enumerate(steps):
        plane = coef_ref[at] + pltpu.roll(coef_ref[up_first + at], 1, 0)
        ahead, back = (coef_ref[middle + 1 + at], coef_ref[middle + 1 + turns + at])
        stencil_ref[3 + 6 * at] = plane
        stencil_ref[4 + 6 * at] = pltpu.roll(ahead, 1, 0)
        stencil_ref[5 + 6 * at] = pltpu.roll(back, LANES - step, 1)
        stencil_ref[6 + 6 * at] = pltpu.roll(plane, step, 1)
        stencil_ref[7 + 6 * at] = pltpu.roll(back, 1, 0)
        stencil_ref[8 + 6 * at] = pltpu.roll(ahead, step, 1)

    def operate(field):
        total = [stencil_ref[at] * field for at in range(3)]
        for at, step in enumerate(steps):
            for side, shift in enumerate((LANES - step, step)):
                value = pltpu.roll(field, shift, 1)
                for part in range(3):
                    total[part] = total[part] + stencil_ref[3 + 6 * at + 3 * side + part] * value
        return total[0] + pltpu.roll(total[1], 7, 0) + pltpu.roll(total[2], 1, 0)

    diag = stencil_ref[0]
    inverse = 1.0 / jnp.where(diag > 0.0, diag, 1.0)

    sums_from(0).wait_recv()
    for o in offsets:

        @pl.when(exists(o))
        def _():
            sums_from(o).wait_recv()

    low, high = (sums_ref[0, 0], sums_ref[1, 0])
    for z in range(1, groups):
        low, high = (low + sums_ref[0, z], high + sums_ref[1, z])
    remain = low + pltpu.roll(high, 1, 0)
    theta = 0.5 * (lam_high + lam_low)
    delta = 0.5 * (lam_high - lam_low)
    sigma = theta / delta
    direction = inverse * remain * (1.0 / theta)
    answer = direction
    rho = 1.0 / sigma
    for sweep in range(SWEEPS):
        remain = remain - operate(direction)
        rho_new = 1.0 / (2.0 * sigma - rho)
        direction = rho_new * rho * direction + 2.0 * rho_new / delta * inverse * remain
        answer = answer + direction
        rho = rho_new

    planes = jnp.where(sub < 4, spread(answer[REACH : REACH + 1]), spread(answer[REACH + 1 : REACH + 2]))
    picked = join_parts(jnp.dot(parts_of(corner_values(planes)), own_hot, preferred_element_type=jnp.float32))
    for h in range(2):
        for a in range(4):
            value = i31_ref[0, a] * picked[0:4] + i31_ref[1, a] * picked[4:8]
            block = sum(weights[4 * h + q] * spread(value[q : q + 1]) for q in range(4))
            out_ref[8 * (2 * a + h) : 8 * (2 * a + h) + 8, :] = block

    sums_from(0).wait_send()
    for o in offsets:

        @pl.when(exists(o))
        def _():
            sums_from(o).wait_send()
            coef_copy(o).wait_send()


def one_layer(resid7, interp73, interp31, elem_ops, conn):
    slabs, groups = (lax.axis_size("slab"), lax.axis_size("grp"))
    dma = pltpu.SemaphoreType.DMA
    span = 2 * REACH + 1
    return pl.pallas_call(
        functools.partial(cycle_kernel, slabs, groups),
        out_shape=pltpu.VMEM((64, 128), jnp.float32),
        in_specs=[pl.BlockSpec(memory_space=pl.ANY)] * 5,
        out_specs=VMEM,
        scratch_shapes=[
            pltpu.VMEM((8, LINE), jnp.int32),
            pltpu.VMEM((8, 8, LINE), jnp.float32),
            pltpu.VMEM((512, 128), jnp.float32),
            pltpu.SMEM((4, 8), jnp.float32),
            pltpu.SMEM((2, 4), jnp.float32),
            dma((5,)),
            pltpu.VMEM((2, groups, 8, LANES), jnp.float32),
            pltpu.VMEM((ROWS, 8, LANES), jnp.float32),
            pltpu.VMEM((3 + 6 * len(TURNS), 8, LANES), jnp.float32),
            pltpu.SemaphoreType.REGULAR((groups,)),
            dma((span,)),
            dma((span,)),
            dma((span,)),
            dma((span,)),
        ],
        compiler_params=pltpu.CompilerParams(collective_id=0, has_side_effects=True),
    )(conn, elem_ops, resid7, interp73.T, interp31.T)


def dispatch(resid7, interp73, interp31, elem_ops, conn, faces):
    if conn.shape[1] == LINE and resid7.shape[1] == 128 and lax.axis_size("grp") > 1:
        return one_layer(resid7, interp73, interp31, elem_ops, conn)
    return local(resid7, interp73, interp31, elem_ops, conn, faces)


def solution(mesh):
    in_specs = (
        P(None, ("slab", "grp")),
        P(),
        P(),
        P(None, None, "slab"),
        P(None, "slab"),
        P(None, "slab", None),
    )
    out_specs = P(None, ("slab", "grp"))
    return jax.shard_map(dispatch, mesh=mesh, in_specs=in_specs, out_specs=out_specs, check_vma=False)
```

```python
import functools

import jax
import jax.numpy as jnp
from jax import lax
from jax.experimental import pallas as pl
from jax.experimental.pallas import tpu as pltpu
from jax.sharding import PartitionSpec as P

EX = 32
EY = 16
SWEEPS = 2


lam_low = 0.3
lam_high = 1.9


def extended(array, sides, width):
    for axis, dim in sides:
        count, length = (lax.axis_size(axis), array.shape[dim])
        up = [(i, (i + 1) % count) for i in range(count - 1)]
        down = [(j, i) for i, j in up]
        last = lax.slice_in_dim(array, length - width, length, axis=dim)
        first = lax.slice_in_dim(array, 0, width, axis=dim)
        before = lax.ppermute(last, axis, up)
        after = lax.ppermute(first, axis, down)
        array = jnp.concatenate([before, array, after], axis=dim)
    return array


def restrict_high(block, interp73):
    hi = lax.Precision.HIGHEST
    width = block.shape[1]
    cube = block.reshape(8, 8, 8, width)
    cube = jnp.einsum("kc,ijkm->ijcm", interp73, cube, precision=hi)
    cube = jnp.einsum("jb,ijcm->ibcm", interp73, cube, precision=hi)
    cube = jnp.einsum("ia,ibcm->abcm", interp73, cube, precision=hi)
    return cube.reshape(64, width)


def restrict_low(block, interp31):
    hi = lax.Precision.HIGHEST
    width = block.shape[1]
    cube = block.reshape(4, 4, 4, width)
    cube = jnp.einsum("kc,ijkm->ijcm", interp31, cube, precision=hi)
    cube = jnp.einsum("jb,ijcm->ibcm", interp31, cube, precision=hi)
    cube = jnp.einsum("ia,ibcm->abcm", interp31, cube, precision=hi)
    return cube.reshape(8, width)


def prolong(coarse, interp31):
    hi = lax.Precision.HIGHEST
    width = coarse.shape[1]
    cube = coarse.reshape(2, 2, 2, width)
    cube = jnp.einsum("ck,ijkm->ijcm", interp31, cube, precision=hi)
    cube = jnp.einsum("bj,ijcm->ibcm", interp31, cube, precision=hi)
    cube = jnp.einsum("ai,ibcm->abcm", interp31, cube, precision=hi)
    return cube.reshape(64, width)


def assemble(values, conn_ids, count):
    layers = values.shape[0]
    flat = values.reshape(layers, -1).T
    summed = jax.ops.segment_sum(flat, conn_ids.reshape(-1), num_segments=count)
    return summed.T


def element_term(operators, conn_ids, field):
    return jnp.einsum("pqe,qe->pe", operators, field[conn_ids], precision=lax.Precision.HIGHEST)


def share(nodes, faces):
    lower = faces[0, 0]
    upper = faces[1, 0]
    planes = jnp.stack([nodes[:, lower], nodes[:, upper]], axis=1)
    padded = extended(planes, (("slab", 1),), 1)
    return nodes.at[:, lower].add(padded[:, 0]).at[:, upper].add(padded[:, 3])


def local(resid7, interp73, interp31, elem_ops, conn, faces):
    own = resid7.shape[1]
    slab_elems = conn.shape[1]
    layers = slab_elems // (EX * EY)
    count = (EX + 1) * (EY + 1) * (layers + 1)
    start = lax.axis_index("grp") * own
    own_conn = lax.dynamic_slice_in_dim(conn, start, own, 1)
    middle_res = restrict_high(resid7, interp73)
    blocks = lax.all_gather(middle_res, "grp", axis=1, tiled=True)
    slab_res = restrict_low(blocks, interp31)
    pair = jnp.stack([slab_res, jnp.einsum("ppe->pe", elem_ops)])
    both_nodes = assemble(pair, conn, count)
    shared = share(both_nodes, faces)
    rhs = shared[0]
    diag = shared[1]
    theta = 0.5 * (lam_high + lam_low)
    delta = 0.5 * (lam_high - lam_low)
    sigma = theta / delta
    inverse = 1.0 / diag
    direction = inverse * rhs / theta
    solution = direction
    remain = rhs
    rho = 1.0 / sigma
    for sweep in range(SWEEPS):
        nodes = assemble(element_term(elem_ops, conn, direction)[None], conn, count)
        remain = remain - share(nodes, faces)[0]
        rho_new = 1.0 / (2.0 * sigma - rho)
        direction = rho_new * rho * direction + 2.0 * rho_new / delta * inverse * remain
        solution = solution + direction
        rho = rho_new
    return prolong(solution[own_conn], interp31)


STRIDE = EX + 1
POINTS = (EX + 1) * (EY + 1)
LANES = (POINTS + 127) // 128 * 128
LINE = EX * EY
BLOCKS = LINE // 128
REACH = SWEEPS + 1
TURNS = ((0, 1), (1, -1), (1, 0), (1, 1))
ROWS = 2 * (len(TURNS) + 1) + 2 * len(TURNS) + 1
MESH = pl.DeviceIdType.MESH
VMEM = pl.BlockSpec(memory_space=pltpu.VMEM)
SMEM = pl.BlockSpec(memory_space=pltpu.SMEM)


def rows_of(shape):
    return lax.broadcasted_iota(jnp.int32, shape, 0)


def spread(row, count=8):
    return jnp.broadcast_to(row, (count, row.shape[1]))


def stack_rows(rows):
    sub = rows_of((8, rows[0].shape[1]))
    out = spread(rows[0])
    for at in range(1, 8):
        out = jnp.where(sub == at, spread(rows[at]), out)
    return out


def parts_of(value):
    hi = value.astype(jnp.bfloat16).astype(jnp.float32)
    left = value - hi
    mid = left.astype(jnp.bfloat16).astype(jnp.float32)
    return jnp.concatenate([hi, mid, left - mid], axis=0).astype(jnp.bfloat16)


def join_parts(value):
    third = value.shape[0] // 3
    return value[:third] + value[third : 2 * third] + value[2 * third :]


def gather_sums(corners):
    sub = rows_of(corners.shape)
    odd, second = ((sub & 1) == 1, (sub & 2) == 2)
    part = jnp.where(odd, pltpu.roll(corners, 1, 1), corners)
    part = part + jnp.where(odd, pltpu.roll(part, 1, 0), pltpu.roll(part, 7, 0))
    part = jnp.where(second, pltpu.roll(part, STRIDE, 1), part)
    return part + jnp.where(second, pltpu.roll(part, 2, 0), pltpu.roll(part, 6, 0))


def aligned(value):
    sub = rows_of(value.shape)
    part = jnp.where((sub & 1) == 1, pltpu.roll(value, 1, 1), value)
    return jnp.where((sub & 2) == 2, pltpu.roll(part, STRIDE, 1), part)


def stencil_rows(columns):
    sub = rows_of(columns[0].shape)
    odd, second = ((sub & 1) == 1, (sub & 2) == 2)

    def over_x(part):
        return part + jnp.where(odd, pltpu.roll(part, 1, 0), pltpu.roll(part, 7, 0))

    def over_y(part):
        return part + jnp.where(second, pltpu.roll(part, 2, 0), pltpu.roll(part, 6, 0))

    c0, c1, c2, c3 = columns
    centre = over_y(over_x(jnp.where(second, jnp.where(odd, c3, c2), jnp.where(odd, c1, c0))))
    along_x = over_y(jnp.where(second, jnp.where(odd, c2, c3), jnp.where(odd, c0, c1)))
    along_y = over_x(jnp.where(second, jnp.where(odd, c1, c0), jnp.where(odd, c3, c2)))
    forward = [(along_x, 0), (c2, 1), (along_y, 0), (c3, 0)]
    backward = [(along_x, 1), (c1, 2), (along_y, 2), (c0, 3)]
    return (centre, 0), forward, backward


def corner_values(nodes):
    sub = rows_of(nodes.shape)
    part = jnp.where((sub & 2) == 2, pltpu.roll(nodes, LANES - STRIDE, 1), nodes)
    return jnp.where((sub & 1) == 1, pltpu.roll(part, LANES - 1, 1), part)


def before(ids, mine, theirs):
    column = jnp.broadcast_to(ids[theirs : theirs + 1], (128, LINE)).T
    row = spread(ids[mine : mine + 1])
    place = rows_of((8, LINE)).astype(jnp.float32)
    total = jnp.zeros((8, LINE), jnp.float32)
    for at in range(LINE // 8):
        one = column[8 * at : 8 * at + 8]
        same = jnp.concatenate([one] * BLOCKS, axis=1) == row
        total = total + jnp.where(same, place + (8.0 * at + 1.0), 0.0)
    return jnp.sum(total, axis=0, keepdims=True)


def positions(conn):
    ids = conn.astype(jnp.float32)
    own = lax.broadcasted_iota(jnp.int32, (1, LINE), 1)
    rows = []
    for theirs in (1, 2):
        found = before(ids, 0, theirs).astype(jnp.int32)
        packed = jnp.where(found > 0, found - 1 + LINE, own)
        rows += [packed[:, 128 * b : 128 * b + 128] for b in range(BLOCKS)]
    state = stack_rows(rows)
    sub = rows_of((8, 128))
    for _ in range((EX - 1).bit_length()):
        target = state & (LINE - 1)
        lane, block = (target & 127, target >> 7)
        got = jnp.zeros((8, 128), jnp.int32)
        for b in range(BLOCKS):
            table = jnp.where(sub < BLOCKS, spread(state[b : b + 1]), spread(state[BLOCKS + b : BLOCKS + b + 1]))
            got = jnp.where(block == b, jnp.take_along_axis(table, lane, axis=1), got)
        state = got + (state - target)
    steps = state >> (LINE.bit_length() - 1)
    return steps + STRIDE * pltpu.roll(steps, 4, 0)


def one_hot(row):
    return jnp.where(rows_of((LANES, row.shape[1])) == spread(row, LANES), 1.0, 0.0).astype(jnp.bfloat16)


def cycle_kernel(slabs, groups, conn_hbm, ops_hbm, res_hbm, i73_hbm, i31_hbm, out_ref, conn_ref, ops_ref, res_ref, i73_ref, i31_ref, load_sem, sums_ref, coef_ref, stencil_ref, hello, sum_sent, coef_sent, sum_recv, coef_recv):
    slab, group = (lax.axis_index("slab"), lax.axis_index("grp"))
    offsets = [o for o in range(-REACH, REACH + 1) if o != 0]
    below, above = (jnp.minimum(slab, REACH), jnp.minimum(slabs - 1 - slab, REACH))
    every = below + above + 1

    def exists(o):
        return slab >= -o if o < 0 else slab < slabs - o

    loads = [
        pltpu.make_async_copy(source, target, (sum_sent, coef_sent, load_sem.at[0], load_sem.at[1], load_sem.at[2])[at])
        for at, (source, target) in enumerate(((conn_hbm, conn_ref), (i73_hbm, i73_ref), (i31_hbm, i31_ref), (res_hbm, res_ref), (ops_hbm, ops_ref)))
    ]
    for load in loads:
        load.start()
    sums_ref[...] = jnp.zeros(sums_ref.shape, jnp.float32)
    coef_ref[...] = jnp.zeros(coef_ref.shape, jnp.float32)

    def tell(semaphore, first, last, some):
        def visit(z, carry):
            pl.semaphore_signal(semaphore, inc=1, device_id=(slab, z), device_id_type=MESH)
            for o in offsets:

                @pl.when(exists(o))
                def _():
                    pl.semaphore_signal(semaphore, inc=1, device_id=(slab + o, z), device_id_type=MESH)

            return carry

        lax.fori_loop(first, last, visit, 0)
        for o in some:

            @pl.when(exists(o))
            def _():
                pl.semaphore_signal(semaphore, inc=1, device_id=(slab + o, group), device_id_type=MESH)

    barrier = pltpu.get_barrier_semaphore()
    tell(barrier, group + 1, groups, offsets)

    loads[0].wait()
    place = positions(conn_ref[...])
    for load in loads[1:]:
        load.wait()
    coef = [[sum(i73_ref[m, i] * i31_ref[a, m] for m in range(4)) for a in range(2)] for i in range(8)]
    along_j = [[None] * 8, [None] * 8]
    for j in range(8):
        for a in range(2):
            along_j[a][j] = sum(coef[i][a] * res_ref[64 * i + 8 * j : 64 * i + 8 * j + 8, :] for i in range(8))
    sub_tile = rows_of((8, 128))
    last = []
    for c in range(2):
        column = jnp.full((8, 128), coef[0][c], jnp.float32)
        for k in range(1, 8):
            column = jnp.where(sub_tile == k, coef[k][c], column)
        last.append(column)
    rows = []
    for a in range(2):
        for b in range(2):
            line = sum(coef[j][b] * along_j[a][j] for j in range(8))
            for c in range(2):
                rows.append(jnp.sum(last[c] * line, axis=0, keepdims=True))
    low_res = stack_rows(rows)

    mine = spread(place[0:1])
    for b in range(1, BLOCKS):
        mine = jnp.where(group == b, spread(place[b : b + 1]), mine)
    own_hot = one_hot(mine[0:1])
    own = join_parts(lax.dot_general(parts_of(low_res), own_hot, (((1,), (1,)), ((), ())), preferred_element_type=jnp.float32))
    nodes = gather_sums(own)
    for plane in range(2):
        sums_ref[plane, group, REACH : REACH + 1, :] = nodes[4 * plane : 4 * plane + 1]

    def sides(o):
        return pl.ds(0, 2) if abs(o) < REACH else pl.ds(int(o > 0), 1)

    def sum_copy(z, o):
        return pltpu.make_async_remote_copy(
            src_ref=sums_ref.at[sides(o), group, pl.ds(REACH, 1), :],
            dst_ref=sums_ref.at[sides(o), group, pl.ds(REACH - o, 1), :],
            send_sem=sum_sent,
            recv_sem=sum_recv,
            device_id=(slab + o, z),
            device_id_type=MESH,
        )

    def whole(semaphore, rows_at):
        width = next(w for w in range(1, 9) if rows_at % w == 0 and rows_at // w <= stencil_ref.shape[0])
        view = stencil_ref.at[pl.ds(0, rows_at // width), pl.ds(0, width), :]
        return pltpu.make_async_remote_copy(src_ref=view, dst_ref=view, send_sem=semaphore, recv_sem=semaphore, device_id=(slab, group), device_id_type=MESH)

    def for_each_size(own, rows_of_offset, act):
        sizes = {}
        for at in range(slabs):
            total = own + sum(rows_of_offset(abs(o)) for o in offsets if 0 <= at + o < slabs)
            sizes.setdefault(total, []).append(at)
        for total, places in sizes.items():
            here = functools.reduce(jnp.logical_or, [slab == at for at in places])

            @pl.when(here)
            def _():
                act(total)

    def sum_rows(distance):
        return groups * (2 if distance < REACH else 1)

    def coef_rows(distance):
        return {1: ROWS, 2: ROWS - len(TURNS), 3: 1}[distance]

    def coef_copy(o):
        first = {1: 0, 2: 0 if o < 0 else 4, 3: 4 if o < 0 else 14}[abs(o)]
        count = coef_rows(abs(o))
        return pltpu.make_async_remote_copy(
            src_ref=coef_ref.at[pl.ds(first, count), pl.ds(REACH, 1), :],
            dst_ref=coef_ref.at[pl.ds(first, count), pl.ds(REACH - o, 1), :],
            send_sem=coef_sent,
            recv_sem=coef_recv,
            device_id=(slab + o, group),
            device_id_type=MESH,
        )

    def send_sums(z, carry):
        sum_copy(z, 0).start()
        for o in offsets:

            @pl.when(exists(o))
            def _():
                sum_copy(z, o).start()

        return carry

    greeted = group * every + below + above

    @pl.when(greeted > 0)
    def _():
        pl.semaphore_wait(barrier, greeted)

    tell(hello.at[group - 1], 0, group, [])
    lax.fori_loop(0, group, send_sums, 0)
    for o in offsets:

        @pl.when(exists(o))
        def _():
            sum_copy(group, o).start()

    hot = jnp.concatenate([one_hot(place[b : b + 1]) for b in range(BLOCKS)], axis=1)
    ops = parts_of(ops_ref[...].reshape(64, LINE))
    lex = join_parts(lax.dot_general(ops, hot, (((1,), (1,)), ((), ())), preferred_element_type=jnp.float32))
    moved = [aligned(lex[8 * q : 8 * q + 8]) for q in range(8)]
    sub = rows_of((8, LANES))
    flat, flat_turns, _ = stencil_rows([jnp.where(sub < 4, moved[q], moved[q + 4]) for q in range(4)])
    centre, forward, backward = stencil_rows(moved[4:])
    rows = [(value, row) for value, row in flat_turns] + [flat, centre] + forward + backward
    rows += [(value, row + 4) for value, row in [flat] + flat_turns]
    for at, (value, row) in enumerate(rows):
        coef_ref[at, REACH : REACH + 1, :] = value[row : row + 1]
    for o in offsets:

        @pl.when(exists(o))
        def _():
            coef_copy(o).start()

    def to_higher(z, carry):
        pl.semaphore_wait(hello.at[z - 1], every)
        return send_sums(z, carry)

    lax.fori_loop(group + 1, groups, to_higher, 0)

    fine = []
    for k in range(2):
        column = jnp.full((8, 128), i31_ref[k, 0], jnp.float32)
        for c in range(1, 4):
            column = jnp.where((sub_tile & 3) == c, i31_ref[k, c], column)
        fine.append(column)
    weights = [jnp.where(sub_tile < 4, i31_ref[j, 2 * h], i31_ref[j, 2 * h + 1]) * fine[k] for h in range(2) for j in range(2) for k in range(2)]

    for_each_size(0, coef_rows, lambda total: whole(coef_recv, total).wait_recv())

    turns = len(TURNS)
    up_first = ROWS - turns
    steps = [STRIDE * dy + dx for dy, dx in TURNS]
    stencil_ref[0] = coef_ref[turns] + pltpu.roll(coef_ref[up_first - 1], 1, 0)
    middle = turns + 1
    stencil_ref[1] = pltpu.roll(coef_ref[middle], 1, 0)
    stencil_ref[2] = coef_ref[middle]
    for at, step in enumerate(steps):
        plane = coef_ref[at] + pltpu.roll(coef_ref[up_first + at], 1, 0)
        ahead, back = (coef_ref[middle + 1 + at], coef_ref[middle + 1 + turns + at])
        stencil_ref[3 + 6 * at] = plane
        stencil_ref[4 + 6 * at] = pltpu.roll(ahead, 1, 0)
        stencil_ref[5 + 6 * at] = pltpu.roll(back, LANES - step, 1)
        stencil_ref[6 + 6 * at] = pltpu.roll(plane, step, 1)
        stencil_ref[7 + 6 * at] = pltpu.roll(back, 1, 0)
        stencil_ref[8 + 6 * at] = pltpu.roll(ahead, step, 1)

    def operate(field):
        total = [stencil_ref[at] * field for at in range(3)]
        for at, step in enumerate(steps):
            for side, shift in enumerate((LANES - step, step)):
                value = pltpu.roll(field, shift, 1)
                for part in range(3):
                    total[part] = total[part] + stencil_ref[3 + 6 * at + 3 * side + part] * value
        return total[0] + pltpu.roll(total[1], 7, 0) + pltpu.roll(total[2], 1, 0)

    diag = stencil_ref[0]
    inverse = 1.0 / jnp.where(diag > 0.0, diag, 1.0)

    for_each_size(2 * (groups - 1), sum_rows, lambda total: whole(sum_recv, total).wait_recv())

    low, high = (sums_ref[0, 0], sums_ref[1, 0])
    for z in range(1, groups):
        low, high = (low + sums_ref[0, z], high + sums_ref[1, z])
    remain = low + pltpu.roll(high, 1, 0)
    theta = 0.5 * (lam_high + lam_low)
    delta = 0.5 * (lam_high - lam_low)
    sigma = theta / delta
    direction = inverse * remain * (1.0 / theta)
    answer = direction
    rho = 1.0 / sigma
    for sweep in range(SWEEPS):
        remain = remain - operate(direction)
        rho_new = 1.0 / (2.0 * sigma - rho)
        direction = rho_new * rho * direction + 2.0 * rho_new / delta * inverse * remain
        answer = answer + direction
        rho = rho_new

    planes = jnp.where(sub < 4, spread(answer[REACH : REACH + 1]), spread(answer[REACH + 1 : REACH + 2]))
    picked = join_parts(jnp.dot(parts_of(corner_values(planes)), own_hot, preferred_element_type=jnp.float32))
    for h in range(2):
        for a in range(4):
            value = i31_ref[0, a] * picked[0:4] + i31_ref[1, a] * picked[4:8]
            block = sum(weights[4 * h + q] * spread(value[q : q + 1]) for q in range(4))
            out_ref[8 * (2 * a + h) : 8 * (2 * a + h) + 8, :] = block

    for_each_size(2 * (groups - 1), sum_rows, lambda total: whole(sum_sent, total).wait_send())
    for_each_size(0, coef_rows, lambda total: whole(coef_sent, total).wait_send())


def one_layer(resid7, interp73, interp31, elem_ops, conn):
    slabs, groups = (lax.axis_size("slab"), lax.axis_size("grp"))
    dma = pltpu.SemaphoreType.DMA
    return pl.pallas_call(
        functools.partial(cycle_kernel, slabs, groups),
        out_shape=pltpu.VMEM((64, 128), jnp.float32),
        in_specs=[pl.BlockSpec(memory_space=pl.ANY)] * 5,
        out_specs=VMEM,
        scratch_shapes=[
            pltpu.VMEM((8, LINE), jnp.int32),
            pltpu.VMEM((8, 8, LINE), jnp.float32),
            pltpu.VMEM((512, 128), jnp.float32),
            pltpu.SMEM((4, 8), jnp.float32),
            pltpu.SMEM((2, 4), jnp.float32),
            dma((3,)),
            pltpu.VMEM((2, groups, 8, LANES), jnp.float32),
            pltpu.VMEM((ROWS, 8, LANES), jnp.float32),
            pltpu.VMEM((3 + 6 * len(TURNS), 8, LANES), jnp.float32),
            pltpu.SemaphoreType.REGULAR((groups - 1,)),
            dma,
            dma,
            dma,
            dma,
        ],
        compiler_params=pltpu.CompilerParams(collective_id=0, has_side_effects=True),
    )(conn, elem_ops, resid7, interp73.T, interp31.T)


def dispatch(resid7, interp73, interp31, elem_ops, conn, faces):
    if conn.shape[1] == LINE and resid7.shape[1] == 128 and lax.axis_size("grp") > 1:
        return one_layer(resid7, interp73, interp31, elem_ops, conn)
    return local(resid7, interp73, interp31, elem_ops, conn, faces)


def solution(mesh):
    in_specs = (
        P(None, ("slab", "grp")),
        P(),
        P(),
        P(None, None, "slab"),
        P(None, "slab"),
        P(None, "slab", None),
    )
    out_specs = P(None, ("slab", "grp"))
    return jax.shard_map(dispatch, mesh=mesh, in_specs=in_specs, out_specs=out_specs, check_vma=False)
```

```python
import functools

import jax
import jax.numpy as jnp
from jax import lax
from jax.experimental import pallas as pl
from jax.experimental.pallas import tpu as pltpu
from jax.sharding import PartitionSpec as P

EX = 32
EY = 16
SWEEPS = 2


lam_low = 0.3
lam_high = 1.9


def extended(array, sides, width):
    for axis, dim in sides:
        count, length = (lax.axis_size(axis), array.shape[dim])
        up = [(i, (i + 1) % count) for i in range(count - 1)]
        down = [(j, i) for i, j in up]
        last = lax.slice_in_dim(array, length - width, length, axis=dim)
        first = lax.slice_in_dim(array, 0, width, axis=dim)
        before = lax.ppermute(last, axis, up)
        after = lax.ppermute(first, axis, down)
        array = jnp.concatenate([before, array, after], axis=dim)
    return array


def restrict_high(block, interp73):
    hi = lax.Precision.HIGHEST
    width = block.shape[1]
    cube = block.reshape(8, 8, 8, width)
    cube = jnp.einsum("kc,ijkm->ijcm", interp73, cube, precision=hi)
    cube = jnp.einsum("jb,ijcm->ibcm", interp73, cube, precision=hi)
    cube = jnp.einsum("ia,ibcm->abcm", interp73, cube, precision=hi)
    return cube.reshape(64, width)


def restrict_low(block, interp31):
    hi = lax.Precision.HIGHEST
    width = block.shape[1]
    cube = block.reshape(4, 4, 4, width)
    cube = jnp.einsum("kc,ijkm->ijcm", interp31, cube, precision=hi)
    cube = jnp.einsum("jb,ijcm->ibcm", interp31, cube, precision=hi)
    cube = jnp.einsum("ia,ibcm->abcm", interp31, cube, precision=hi)
    return cube.reshape(8, width)


def prolong(coarse, interp31):
    hi = lax.Precision.HIGHEST
    width = coarse.shape[1]
    cube = coarse.reshape(2, 2, 2, width)
    cube = jnp.einsum("ck,ijkm->ijcm", interp31, cube, precision=hi)
    cube = jnp.einsum("bj,ijcm->ibcm", interp31, cube, precision=hi)
    cube = jnp.einsum("ai,ibcm->abcm", interp31, cube, precision=hi)
    return cube.reshape(64, width)


def assemble(values, conn_ids, count):
    layers = values.shape[0]
    flat = values.reshape(layers, -1).T
    summed = jax.ops.segment_sum(flat, conn_ids.reshape(-1), num_segments=count)
    return summed.T


def element_term(operators, conn_ids, field):
    return jnp.einsum("pqe,qe->pe", operators, field[conn_ids], precision=lax.Precision.HIGHEST)


def share(nodes, faces):
    lower = faces[0, 0]
    upper = faces[1, 0]
    planes = jnp.stack([nodes[:, lower], nodes[:, upper]], axis=1)
    padded = extended(planes, (("slab", 1),), 1)
    return nodes.at[:, lower].add(padded[:, 0]).at[:, upper].add(padded[:, 3])


def local(resid7, interp73, interp31, elem_ops, conn, faces):
    own = resid7.shape[1]
    slab_elems = conn.shape[1]
    layers = slab_elems // (EX * EY)
    count = (EX + 1) * (EY + 1) * (layers + 1)
    start = lax.axis_index("grp") * own
    own_conn = lax.dynamic_slice_in_dim(conn, start, own, 1)
    middle_res = restrict_high(resid7, interp73)
    blocks = lax.all_gather(middle_res, "grp", axis=1, tiled=True)
    slab_res = restrict_low(blocks, interp31)
    pair = jnp.stack([slab_res, jnp.einsum("ppe->pe", elem_ops)])
    both_nodes = assemble(pair, conn, count)
    shared = share(both_nodes, faces)
    rhs = shared[0]
    diag = shared[1]
    theta = 0.5 * (lam_high + lam_low)
    delta = 0.5 * (lam_high - lam_low)
    sigma = theta / delta
    inverse = 1.0 / diag
    direction = inverse * rhs / theta
    solution = direction
    remain = rhs
    rho = 1.0 / sigma
    for sweep in range(SWEEPS):
        nodes = assemble(element_term(elem_ops, conn, direction)[None], conn, count)
        remain = remain - share(nodes, faces)[0]
        rho_new = 1.0 / (2.0 * sigma - rho)
        direction = rho_new * rho * direction + 2.0 * rho_new / delta * inverse * remain
        solution = solution + direction
        rho = rho_new
    return prolong(solution[own_conn], interp31)


STRIDE = EX + 1
POINTS = (EX + 1) * (EY + 1)
LANES = (POINTS + 127) // 128 * 128
LINE = EX * EY
BLOCKS = LINE // 128
REACH = SWEEPS + 1
TURNS = ((0, 1), (1, -1), (1, 0), (1, 1))
ROWS = 2 * (len(TURNS) + 1) + 2 * len(TURNS) + 1
MESH = pl.DeviceIdType.MESH
VMEM = pl.BlockSpec(memory_space=pltpu.VMEM)
SMEM = pl.BlockSpec(memory_space=pltpu.SMEM)


def rows_of(shape):
    return lax.broadcasted_iota(jnp.int32, shape, 0)


def spread(row, count=8):
    return jnp.broadcast_to(row, (count, row.shape[1]))


def stack_rows(rows):
    sub = rows_of((8, rows[0].shape[1]))
    out = spread(rows[0])
    for at in range(1, 8):
        out = jnp.where(sub == at, spread(rows[at]), out)
    return out


def parts_of(value):
    hi = value.astype(jnp.bfloat16).astype(jnp.float32)
    left = value - hi
    mid = left.astype(jnp.bfloat16).astype(jnp.float32)
    return jnp.concatenate([hi, mid, left - mid], axis=0).astype(jnp.bfloat16)


def join_parts(value):
    third = value.shape[0] // 3
    return value[:third] + value[third : 2 * third] + value[2 * third :]


def gather_sums(corners):
    sub = rows_of(corners.shape)
    odd, second = ((sub & 1) == 1, (sub & 2) == 2)
    part = jnp.where(odd, pltpu.roll(corners, 1, 1), corners)
    part = part + jnp.where(odd, pltpu.roll(part, 1, 0), pltpu.roll(part, 7, 0))
    part = jnp.where(second, pltpu.roll(part, STRIDE, 1), part)
    return part + jnp.where(second, pltpu.roll(part, 2, 0), pltpu.roll(part, 6, 0))


def aligned(value):
    sub = rows_of(value.shape)
    part = jnp.where((sub & 1) == 1, pltpu.roll(value, 1, 1), value)
    return jnp.where((sub & 2) == 2, pltpu.roll(part, STRIDE, 1), part)


def stencil_rows(columns):
    sub = rows_of(columns[0].shape)
    odd, second = ((sub & 1) == 1, (sub & 2) == 2)

    def over_x(part):
        return part + jnp.where(odd, pltpu.roll(part, 1, 0), pltpu.roll(part, 7, 0))

    def over_y(part):
        return part + jnp.where(second, pltpu.roll(part, 2, 0), pltpu.roll(part, 6, 0))

    c0, c1, c2, c3 = columns
    centre = over_y(over_x(jnp.where(second, jnp.where(odd, c3, c2), jnp.where(odd, c1, c0))))
    along_x = over_y(jnp.where(second, jnp.where(odd, c2, c3), jnp.where(odd, c0, c1)))
    along_y = over_x(jnp.where(second, jnp.where(odd, c1, c0), jnp.where(odd, c3, c2)))
    forward = [(along_x, 0), (c2, 1), (along_y, 0), (c3, 0)]
    backward = [(along_x, 1), (c1, 2), (along_y, 2), (c0, 3)]
    return (centre, 0), forward, backward


def before(ids, mine, theirs):
    column = jnp.broadcast_to(ids[theirs : theirs + 1], (128, LINE)).T
    row = spread(ids[mine : mine + 1])
    place = rows_of((8, LINE)).astype(jnp.float32)
    total = jnp.zeros((8, LINE), jnp.float32)
    for at in range(LINE // 8):
        one = column[8 * at : 8 * at + 8]
        same = jnp.concatenate([one] * BLOCKS, axis=1) == row
        total = total + jnp.where(same, place + (8.0 * at + 1.0), 0.0)
    return jnp.sum(total, axis=0, keepdims=True)


def links(conn):
    ids = conn.astype(jnp.float32)
    own = lax.broadcasted_iota(jnp.int32, (1, LINE), 1)
    rows = []
    for theirs in (1, 2):
        found = before(ids, 0, theirs).astype(jnp.int32)
        packed = jnp.where(found > 0, found - 1 + LINE, own)
        rows += [packed[:, 128 * b : 128 * b + 128] for b in range(BLOCKS)]
    return stack_rows(rows)


def positions(state):
    sub = rows_of((8, 128))
    for _ in range((EX - 1).bit_length()):
        target = state & (LINE - 1)
        lane, block = (target & 127, target >> 7)
        got = jnp.zeros((8, 128), jnp.int32)
        for b in range(BLOCKS):
            table = jnp.where(sub < BLOCKS, spread(state[b : b + 1]), spread(state[BLOCKS + b : BLOCKS + b + 1]))
            got = jnp.where(block == b, jnp.take_along_axis(table, lane, axis=1), got)
        state = got + (state - target)
    steps = state >> (LINE.bit_length() - 1)
    return steps + STRIDE * pltpu.roll(steps, 4, 0)


def one_hot(row):
    return jnp.where(rows_of((LANES, row.shape[1])) == spread(row, LANES), 1.0, 0.0).astype(jnp.bfloat16)


def cycle_kernel(slabs, groups, conn_hbm, ops_hbm, res_hbm, i73_hbm, i31_hbm, out_ref, conn_ref, ops_ref, res_ref, i73_ref, i31_ref, load_sem, sums_ref, coef_ref, stencil_ref, hello, sum_sent, coef_sent, sum_recv, coef_recv, cross_recv):
    slab, group = (lax.axis_index("slab"), lax.axis_index("grp"))
    offsets = [o for o in range(-REACH, REACH + 1) if o != 0]
    below, above = (jnp.minimum(slab, REACH), jnp.minimum(slabs - 1 - slab, REACH))
    every = below + above + 1

    def exists(o):
        return slab >= -o if o < 0 else slab < slabs - o

    loads = [
        pltpu.make_async_copy(source, target, (sum_sent, coef_sent, load_sem.at[0], load_sem.at[1], load_sem.at[2])[at])
        for at, (source, target) in enumerate(((conn_hbm, conn_ref), (i73_hbm, i73_ref), (i31_hbm, i31_ref), (res_hbm, res_ref), (ops_hbm, ops_ref)))
    ]
    for load in loads:
        load.start()
    sums_ref[...] = jnp.zeros(sums_ref.shape, jnp.float32)
    coef_ref[...] = jnp.zeros(coef_ref.shape, jnp.float32)

    def tell(semaphore, first, last, some):
        def visit(z, carry):
            pl.semaphore_signal(semaphore, inc=1, device_id=(slab, z), device_id_type=MESH)
            for o in offsets:

                @pl.when(exists(o))
                def _():
                    pl.semaphore_signal(semaphore, inc=1, device_id=(slab + o, z), device_id_type=MESH)

            return carry

        lax.fori_loop(first, last, visit, 0)
        for o in some:

            @pl.when(exists(o))
            def _():
                pl.semaphore_signal(semaphore, inc=1, device_id=(slab + o, group), device_id_type=MESH)

    barrier = pltpu.get_barrier_semaphore()
    tell(barrier, group + 1, groups, offsets)

    loads[0].wait()
    state = links(conn_ref[...])
    for load in loads[1:]:
        load.wait()
    place = positions(state)
    coef = [[sum(i73_ref[m, i] * i31_ref[a, m] for m in range(4)) for a in range(2)] for i in range(8)]
    along_j = [[None] * 8, [None] * 8]
    for j in range(8):
        for a in range(2):
            along_j[a][j] = sum(coef[i][a] * res_ref[64 * i + 8 * j : 64 * i + 8 * j + 8, :] for i in range(8))
    sub_tile = rows_of((8, 128))
    last = []
    for c in range(2):
        column = jnp.full((8, 128), coef[0][c], jnp.float32)
        for k in range(1, 8):
            column = jnp.where(sub_tile == k, coef[k][c], column)
        last.append(column)
    rows = []
    for a in range(2):
        for b in range(2):
            line = sum(coef[j][b] * along_j[a][j] for j in range(8))
            for c in range(2):
                rows.append(jnp.sum(last[c] * line, axis=0, keepdims=True))
    low_res = stack_rows(rows)

    mine = spread(place[0:1])
    for b in range(1, BLOCKS):
        mine = jnp.where(group == b, spread(place[b : b + 1]), mine)
    own_hot = one_hot(mine[0:1])
    corner = mine + STRIDE * (sub_tile // 2 % 2) + sub_tile % 2
    own_lane, own_tile = (corner & 127, corner >> 7)
    greeted = group * every + below + above

    @pl.when(group > 0)
    def _():
        pl.semaphore_wait(barrier, greeted)

    tell(hello.at[group - 1], 0, jnp.minimum(group, 1), [])
    own = join_parts(lax.dot_general(parts_of(low_res), own_hot, (((1,), (1,)), ((), ())), preferred_element_type=jnp.float32))
    nodes = gather_sums(own)
    for plane in range(2):
        sums_ref[plane, group, REACH : REACH + 1, :] = nodes[4 * plane : 4 * plane + 1]

    def sides(o):
        return pl.ds(0, 2) if abs(o) < REACH else pl.ds(int(o > 0), 1)

    def sum_copy(z, o):
        return pltpu.make_async_remote_copy(
            src_ref=sums_ref.at[sides(o), group, pl.ds(REACH, 1), :],
            dst_ref=sums_ref.at[sides(o), group, pl.ds(REACH - o, 1), :],
            send_sem=sum_sent,
            recv_sem=sum_recv,
            device_id=(slab + o, z),
            device_id_type=MESH,
        )

    def whole(semaphore, rows_at):
        width = next(w for w in range(1, 9) if rows_at % w == 0 and rows_at // w <= stencil_ref.shape[0])
        view = stencil_ref.at[pl.ds(0, rows_at // width), pl.ds(0, width), :]
        return pltpu.make_async_remote_copy(src_ref=view, dst_ref=view, send_sem=semaphore, recv_sem=semaphore, device_id=(slab, group), device_id_type=MESH)

    def for_each_size(rows_of, act):
        sizes = {}
        for at in range(slabs):
            sizes.setdefault(rows_of(at), []).append(at)
        for total, places in sizes.items():
            here = functools.reduce(jnp.logical_or, [slab == at for at in places])

            @pl.when(here)
            def _():
                act(total)

    def sum_rows(at):
        return 2 * (groups - 1) + sum(groups * (2 if abs(o) < REACH else 1) for o in offsets if 0 <= at + o < slabs)

    def coef_rows(distance):
        return {1: ROWS, 2: ROWS - len(TURNS), 3: 1}[distance]

    def coef_got(at):
        crossing = at + (1 if at % 2 else -1)
        return sum(coef_rows(abs(o)) for o in offsets if 0 <= at + o < slabs and at + o != crossing)

    def coef_gone(at):
        outward = 1 if at % 2 else -1
        direct = [o for o in offsets if 0 <= at + o < slabs and o != 2 * outward]
        return sum(coef_rows(abs(o)) for o in direct) + (coef_rows(2) if 0 <= at + outward < slabs else 0)

    def coef_copy(o, arrived, source=0):
        far = abs(o - source)
        first = {1: 0, 2: 0 if o < source else 4, 3: 4 if o < source else 14}[far]
        count = coef_rows(far)
        return pltpu.make_async_remote_copy(
            src_ref=coef_ref.at[pl.ds(first, count), pl.ds(REACH + source, 1), :],
            dst_ref=coef_ref.at[pl.ds(first, count), pl.ds(REACH + source - o, 1), :],
            send_sem=coef_sent,
            recv_sem=arrived,
            device_id=(slab + o, group),
            device_id_type=MESH,
        )

    def send_sums(z, carry):
        sum_copy(z, 0).start()
        for o in offsets:

            @pl.when(exists(o))
            def _():
                sum_copy(z, o).start()

        return carry

    lax.fori_loop(0, jnp.minimum(group, 1), send_sums, 0)
    tell(hello.at[group - 1], 1, group, [])
    lax.fori_loop(1, group, send_sums, 0)
    hot = jnp.concatenate([one_hot(place[b : b + 1]) for b in range(BLOCKS)], axis=1)
    ops = parts_of(ops_ref[...].reshape(64, LINE))
    lex = join_parts(lax.dot_general(ops, hot, (((1,), (1,)), ((), ())), preferred_element_type=jnp.float32))
    moved = [aligned(lex[8 * q : 8 * q + 8]) for q in range(8)]
    sub = rows_of((8, LANES))
    flat, flat_turns, _ = stencil_rows([jnp.where(sub < 4, moved[q], moved[q + 4]) for q in range(4)])
    centre, forward, backward = stencil_rows(moved[4:])
    rows = [(value, row) for value, row in flat_turns] + [flat, centre] + forward + backward
    rows += [(value, row + 4) for value, row in [flat] + flat_turns]
    for at, (value, row) in enumerate(rows):
        coef_ref[at, REACH : REACH + 1, :] = value[row : row + 1]
    even = slab % 2 == 0
    odd = jnp.logical_not(even)
    across = ((jnp.logical_and(even, exists(-1)), -1), (jnp.logical_and(odd, exists(1)), 1))
    @pl.when(jnp.logical_and(group == 0, greeted > 0))
    def _():
        pl.semaphore_wait(barrier, greeted)

    down, up = across
    for here, o, arrived in (
        (*down, cross_recv),
        (jnp.logical_and(odd, exists(-2)), -2, coef_recv),
        (*up, cross_recv),
        (jnp.logical_and(even, exists(2)), 2, coef_recv),
        (odd, -1, coef_recv),
        (even, 1, coef_recv),
        (exists(-3), -3, coef_recv),
        (exists(3), 3, coef_recv),
    ):

        @pl.when(here)
        def _():
            coef_copy(o, arrived).start()

    for o in offsets:

        @pl.when(exists(o))
        def _():
            sum_copy(group, o).start()

    def to_higher(z, carry):
        pl.semaphore_wait(hello.at[z - 1], every)
        return send_sums(z, carry)

    lax.fori_loop(group + 1, groups, to_higher, 0)

    fine = []
    for k in range(2):
        column = jnp.full((8, 128), i31_ref[k, 0], jnp.float32)
        for c in range(1, 4):
            column = jnp.where((sub_tile & 3) == c, i31_ref[k, c], column)
        fine.append(column)
    weights = [jnp.where(sub_tile < 4, i31_ref[j, 2 * h], i31_ref[j, 2 * h + 1]) * fine[k] for h in range(2) for j in range(2) for k in range(2)]

    for here, o in across:

        @pl.when(here)
        def _():
            whole(cross_recv, ROWS).wait_recv()
            coef_copy(-o, coef_recv, source=o).start()

    for_each_size(coef_got, lambda total: whole(coef_recv, total).wait_recv())

    turns = len(TURNS)
    up_first = ROWS - turns
    steps = [STRIDE * dy + dx for dy, dx in TURNS]
    stencil_ref[0] = coef_ref[turns] + pltpu.roll(coef_ref[up_first - 1], 1, 0)
    middle = turns + 1
    stencil_ref[1] = pltpu.roll(coef_ref[middle], 1, 0)
    stencil_ref[2] = coef_ref[middle]
    for at, step in enumerate(steps):
        plane = coef_ref[at] + pltpu.roll(coef_ref[up_first + at], 1, 0)
        ahead, back = (coef_ref[middle + 1 + at], coef_ref[middle + 1 + turns + at])
        stencil_ref[3 + 6 * at] = plane
        stencil_ref[4 + 6 * at] = pltpu.roll(ahead, 1, 0)
        stencil_ref[5 + 6 * at] = pltpu.roll(back, LANES - step, 1)
        stencil_ref[6 + 6 * at] = pltpu.roll(plane, step, 1)
        stencil_ref[7 + 6 * at] = pltpu.roll(back, 1, 0)
        stencil_ref[8 + 6 * at] = pltpu.roll(ahead, step, 1)

    def operate(field):
        total = [stencil_ref[at] * field for at in range(3)]
        for at, step in enumerate(steps):
            for side, shift in enumerate((LANES - step, step)):
                value = pltpu.roll(field, shift, 1)
                for part in range(3):
                    total[part] = total[part] + stencil_ref[3 + 6 * at + 3 * side + part] * value
        return total[0] + pltpu.roll(total[1], 7, 0) + pltpu.roll(total[2], 1, 0)

    diag = stencil_ref[0]
    inverse = 1.0 / jnp.where(diag > 0.0, diag, 1.0)

    for_each_size(sum_rows, lambda total: whole(sum_sent, total).wait_send())
    for_each_size(sum_rows, lambda total: whole(sum_recv, total).wait_recv())

    low, high = (sums_ref[0, 0], sums_ref[1, 0])
    for z in range(1, groups):
        low, high = (low + sums_ref[0, z], high + sums_ref[1, z])
    remain = low + pltpu.roll(high, 1, 0)
    theta = 0.5 * (lam_high + lam_low)
    delta = 0.5 * (lam_high - lam_low)
    sigma = theta / delta
    direction = inverse * remain * (1.0 / theta)
    answer = direction
    rho = 1.0 / sigma
    for sweep in range(SWEEPS):
        remain = remain - operate(direction)
        rho_new = 1.0 / (2.0 * sigma - rho)
        direction = rho_new * rho * direction + 2.0 * rho_new / delta * inverse * remain
        answer = answer + direction
        rho = rho_new

    planes = jnp.where(sub < 4, spread(answer[REACH : REACH + 1]), spread(answer[REACH + 1 : REACH + 2]))
    picked = jnp.take_along_axis(planes[:, :128], own_lane, axis=1)
    for b in range(1, LANES // 128):
        picked = jnp.where(own_tile == b, jnp.take_along_axis(planes[:, 128 * b : 128 * b + 128], own_lane, axis=1), picked)
    values = [spread(picked[p : p + 1]) for p in range(8)]
    for h in range(2):
        ends = [sum(weights[4 * h + q] * values[4 * i + q] for q in range(4)) for i in range(2)]
        for a in range(4):
            out_ref[8 * (2 * a + h) : 8 * (2 * a + h) + 8, :] = i31_ref[0, a] * ends[0] + i31_ref[1, a] * ends[1]

    for_each_size(coef_gone, lambda total: whole(coef_sent, total).wait_send())


def one_layer(resid7, interp73, interp31, elem_ops, conn):
    slabs, groups = (lax.axis_size("slab"), lax.axis_size("grp"))
    dma = pltpu.SemaphoreType.DMA
    return pl.pallas_call(
        functools.partial(cycle_kernel, slabs, groups),
        out_shape=pltpu.VMEM((64, 128), jnp.float32),
        in_specs=[pl.BlockSpec(memory_space=pl.ANY)] * 5,
        out_specs=VMEM,
        scratch_shapes=[
            pltpu.VMEM((8, LINE), jnp.int32),
            pltpu.VMEM((8, 8, LINE), jnp.float32),
            pltpu.VMEM((512, 128), jnp.float32),
            pltpu.SMEM((4, 8), jnp.float32),
            pltpu.SMEM((2, 4), jnp.float32),
            dma((3,)),
            pltpu.VMEM((2, groups, 8, LANES), jnp.float32),
            pltpu.VMEM((ROWS, 8, LANES), jnp.float32),
            pltpu.VMEM((3 + 6 * len(TURNS), 8, LANES), jnp.float32),
            pltpu.SemaphoreType.REGULAR((groups - 1,)),
            dma,
            dma,
            dma,
            dma,
            dma,
        ],
        compiler_params=pltpu.CompilerParams(collective_id=0, has_side_effects=True),
    )(conn, elem_ops, resid7, interp73.T, interp31.T)


def dispatch(resid7, interp73, interp31, elem_ops, conn, faces):
    if conn.shape[1] == LINE and resid7.shape[1] == 128 and lax.axis_size("grp") > 1 and lax.axis_size("slab") % 2 == 0:
        return one_layer(resid7, interp73, interp31, elem_ops, conn)
    return local(resid7, interp73, interp31, elem_ops, conn, faces)


def solution(mesh):
    in_specs = (
        P(None, ("slab", "grp")),
        P(),
        P(),
        P(None, None, "slab"),
        P(None, "slab"),
        P(None, "slab", None),
    )
    out_specs = P(None, ("slab", "grp"))
    return jax.shard_map(dispatch, mesh=mesh, in_specs=in_specs, out_specs=out_specs, check_vma=False)
```

```python
import functools

import jax
import jax.numpy as jnp
from jax import lax
from jax.experimental import pallas as pl
from jax.experimental.pallas import tpu as pltpu
from jax.sharding import PartitionSpec as P

EX = 32
EY = 16
SWEEPS = 2


lam_low = 0.3
lam_high = 1.9


def extended(array, sides, width):
    for axis, dim in sides:
        count, length = (lax.axis_size(axis), array.shape[dim])
        up = [(i, (i + 1) % count) for i in range(count - 1)]
        down = [(j, i) for i, j in up]
        last = lax.slice_in_dim(array, length - width, length, axis=dim)
        first = lax.slice_in_dim(array, 0, width, axis=dim)
        before = lax.ppermute(last, axis, up)
        after = lax.ppermute(first, axis, down)
        array = jnp.concatenate([before, array, after], axis=dim)
    return array


def restrict_high(block, interp73):
    hi = lax.Precision.HIGHEST
    width = block.shape[1]
    cube = block.reshape(8, 8, 8, width)
    cube = jnp.einsum("kc,ijkm->ijcm", interp73, cube, precision=hi)
    cube = jnp.einsum("jb,ijcm->ibcm", interp73, cube, precision=hi)
    cube = jnp.einsum("ia,ibcm->abcm", interp73, cube, precision=hi)
    return cube.reshape(64, width)


def restrict_low(block, interp31):
    hi = lax.Precision.HIGHEST
    width = block.shape[1]
    cube = block.reshape(4, 4, 4, width)
    cube = jnp.einsum("kc,ijkm->ijcm", interp31, cube, precision=hi)
    cube = jnp.einsum("jb,ijcm->ibcm", interp31, cube, precision=hi)
    cube = jnp.einsum("ia,ibcm->abcm", interp31, cube, precision=hi)
    return cube.reshape(8, width)


def prolong(coarse, interp31):
    hi = lax.Precision.HIGHEST
    width = coarse.shape[1]
    cube = coarse.reshape(2, 2, 2, width)
    cube = jnp.einsum("ck,ijkm->ijcm", interp31, cube, precision=hi)
    cube = jnp.einsum("bj,ijcm->ibcm", interp31, cube, precision=hi)
    cube = jnp.einsum("ai,ibcm->abcm", interp31, cube, precision=hi)
    return cube.reshape(64, width)


def assemble(values, conn_ids, count):
    layers = values.shape[0]
    flat = values.reshape(layers, -1).T
    summed = jax.ops.segment_sum(flat, conn_ids.reshape(-1), num_segments=count)
    return summed.T


def element_term(operators, conn_ids, field):
    return jnp.einsum("pqe,qe->pe", operators, field[conn_ids], precision=lax.Precision.HIGHEST)


def share(nodes, faces):
    lower = faces[0, 0]
    upper = faces[1, 0]
    planes = jnp.stack([nodes[:, lower], nodes[:, upper]], axis=1)
    padded = extended(planes, (("slab", 1),), 1)
    return nodes.at[:, lower].add(padded[:, 0]).at[:, upper].add(padded[:, 3])


def local(resid7, interp73, interp31, elem_ops, conn, faces):
    own = resid7.shape[1]
    slab_elems = conn.shape[1]
    layers = slab_elems // (EX * EY)
    count = (EX + 1) * (EY + 1) * (layers + 1)
    start = lax.axis_index("grp") * own
    own_conn = lax.dynamic_slice_in_dim(conn, start, own, 1)
    middle_res = restrict_high(resid7, interp73)
    blocks = lax.all_gather(middle_res, "grp", axis=1, tiled=True)
    slab_res = restrict_low(blocks, interp31)
    pair = jnp.stack([slab_res, jnp.einsum("ppe->pe", elem_ops)])
    both_nodes = assemble(pair, conn, count)
    shared = share(both_nodes, faces)
    rhs = shared[0]
    diag = shared[1]
    theta = 0.5 * (lam_high + lam_low)
    delta = 0.5 * (lam_high - lam_low)
    sigma = theta / delta
    inverse = 1.0 / diag
    direction = inverse * rhs / theta
    solution = direction
    remain = rhs
    rho = 1.0 / sigma
    for sweep in range(SWEEPS):
        nodes = assemble(element_term(elem_ops, conn, direction)[None], conn, count)
        remain = remain - share(nodes, faces)[0]
        rho_new = 1.0 / (2.0 * sigma - rho)
        direction = rho_new * rho * direction + 2.0 * rho_new / delta * inverse * remain
        solution = solution + direction
        rho = rho_new
    return prolong(solution[own_conn], interp31)


STRIDE = EX + 1
POINTS = (EX + 1) * (EY + 1)
LANES = (POINTS + 127) // 128 * 128
LINE = EX * EY
BLOCKS = LINE // 128
REACH = SWEEPS + 1
TURNS = ((0, 1), (1, -1), (1, 0), (1, 1))
ROWS = 2 * (len(TURNS) + 1) + 2 * len(TURNS) + 1
MESH = pl.DeviceIdType.MESH
VMEM = pl.BlockSpec(memory_space=pltpu.VMEM)
SMEM = pl.BlockSpec(memory_space=pltpu.SMEM)


def rows_of(shape):
    return lax.broadcasted_iota(jnp.int32, shape, 0)


def spread(row, count=8):
    return jnp.broadcast_to(row, (count, row.shape[1]))


def stack_rows(rows):
    sub = rows_of((8, rows[0].shape[1]))
    out = spread(rows[0])
    for at in range(1, 8):
        out = jnp.where(sub == at, spread(rows[at]), out)
    return out


def parts_of(value):
    hi = value.astype(jnp.bfloat16).astype(jnp.float32)
    left = value - hi
    mid = left.astype(jnp.bfloat16).astype(jnp.float32)
    return jnp.concatenate([hi, mid, left - mid], axis=0).astype(jnp.bfloat16)


def join_parts(value):
    third = value.shape[0] // 3
    return value[:third] + value[third : 2 * third] + value[2 * third :]


def aligned(value):
    sub = rows_of(value.shape)
    odd, second = ((sub & 1) == 1, (sub & 2) == 2)
    near = jnp.where(odd, pltpu.roll(value, 1, 1), value)
    far = jnp.where(odd, pltpu.roll(value, STRIDE + 1, 1), pltpu.roll(value, STRIDE, 1))
    return jnp.where(second, far, near)


def gather_sums(corners):
    part = aligned(corners)
    part = part + pltpu.roll(part, 7, 0)
    return part + pltpu.roll(part, 6, 0)


def stencil_rows(columns):
    sub = rows_of(columns[0].shape)
    odd, second = ((sub & 1) == 1, (sub & 2) == 2)

    def over_x(part):
        return part + jnp.where(odd, pltpu.roll(part, 1, 0), pltpu.roll(part, 7, 0))

    def over_y(part):
        return part + jnp.where(second, pltpu.roll(part, 2, 0), pltpu.roll(part, 6, 0))

    c0, c1, c2, c3 = columns
    centre = over_y(over_x(jnp.where(second, jnp.where(odd, c3, c2), jnp.where(odd, c1, c0))))
    along_x = over_y(jnp.where(second, jnp.where(odd, c2, c3), jnp.where(odd, c0, c1)))
    along_y = over_x(jnp.where(second, jnp.where(odd, c1, c0), jnp.where(odd, c3, c2)))
    forward = [(along_x, 0), (c2, 1), (along_y, 0), (c3, 0)]
    backward = [(along_x, 1), (c1, 2), (along_y, 2), (c0, 3)]
    return (centre, 0), forward, backward


def coded(number):
    return (128 + (number & 127)) * jnp.left_shift(1, number >> 7)


def before(ids, mine, theirs):
    column = jnp.broadcast_to(ids[theirs : theirs + 1], (128, LINE)).T.astype(jnp.bfloat16)
    row = spread(ids[mine : mine + 1], 16).astype(jnp.bfloat16)
    place = rows_of((16, 128))
    total = jnp.zeros((16, LINE), jnp.bfloat16)
    for at in range(LINE // 16):
        one = column[16 * at : 16 * at + 16]
        same = jnp.concatenate([one] * BLOCKS, axis=1) == row
        value = (place * (1 << (at >> 3)) + ((128 + (16 * at & 127)) << (at >> 3))).astype(jnp.float32).astype(jnp.bfloat16)
        total = jnp.where(same, jnp.concatenate([value] * BLOCKS, axis=1), total)
    return jnp.sum(total.astype(jnp.float32), axis=0, keepdims=True)


def links(conn):
    ids = coded(conn).astype(jnp.float32)
    own = lax.broadcasted_iota(jnp.int32, (1, LINE), 1)
    rows = []
    for theirs in (1, 2):
        code = before(ids, 0, theirs).astype(jnp.int32)
        power = sum((code >= 256 << k).astype(jnp.int32) for k in range((LINE - 1) >> 7))
        found = (code >> power) - 128 + 128 * power
        packed = jnp.where(code > 0, found + LINE, own)
        rows += [packed[:, 128 * b : 128 * b + 128] for b in range(BLOCKS)]
    return stack_rows(rows)


def positions(state):
    sub = rows_of((8, 128))
    for _ in range((EX - 1).bit_length()):
        target = state & (LINE - 1)
        lane, block = (target & 127, target >> 7)
        got = jnp.zeros((8, 128), jnp.int32)
        for b in range(BLOCKS):
            table = jnp.where(sub < BLOCKS, spread(state[b : b + 1]), spread(state[BLOCKS + b : BLOCKS + b + 1]))
            got = jnp.where(block == b, jnp.take_along_axis(table, lane, axis=1), got)
        state = got + (state - target)
    steps = state >> (LINE.bit_length() - 1)
    return steps + STRIDE * pltpu.roll(steps, 4, 0)


def one_hot(row):
    return jnp.where(rows_of((LANES, row.shape[1])) == spread(row, LANES), 1.0, 0.0).astype(jnp.bfloat16)


def cycle_kernel(slabs, groups, conn_hbm, ops_hbm, res_hbm, i73_hbm, i31_hbm, out_ref, conn_ref, ops_ref, res_ref, i73_ref, i31_ref, load_sem, sums_ref, coef_ref, stencil_ref, hello, sum_sent, coef_sent, sum_recv, coef_recv, cross_recv):
    slab, group = (lax.axis_index("slab"), lax.axis_index("grp"))
    offsets = [o for o in range(-REACH, REACH + 1) if o != 0]
    below, above = (jnp.minimum(slab, REACH), jnp.minimum(slabs - 1 - slab, REACH))
    every = below + above + 1

    def exists(o):
        return slab >= -o if o < 0 else slab < slabs - o

    loads = [
        pltpu.make_async_copy(source, target, (sum_sent, coef_sent, load_sem.at[0], load_sem.at[1], load_sem.at[1])[at])
        for at, (source, target) in enumerate(((i73_hbm, i73_ref), (i31_hbm, i31_ref), (conn_hbm, conn_ref), (res_hbm, res_ref), (ops_hbm, ops_ref)))
    ]
    for load in loads:
        load.start()
    sums_ref[...] = jnp.zeros(sums_ref.shape, jnp.float32)
    coef_ref[...] = jnp.zeros(coef_ref.shape, jnp.float32)

    def tell(semaphore, first, last, some):
        def visit(z, carry):
            pl.semaphore_signal(semaphore, inc=1, device_id=(slab, z), device_id_type=MESH)
            for o in offsets:

                @pl.when(exists(o))
                def _():
                    pl.semaphore_signal(semaphore, inc=1, device_id=(slab + o, z), device_id_type=MESH)

            return carry

        lax.fori_loop(first, last, visit, 0)
        for o in some:

            @pl.when(exists(o))
            def _():
                pl.semaphore_signal(semaphore, inc=1, device_id=(slab + o, group), device_id_type=MESH)

    barrier = pltpu.get_barrier_semaphore()
    tell(barrier, group + 1, groups, offsets)

    for load in loads[:3]:
        load.wait()
    coef = [[sum(i73_ref[m, i] * i31_ref[a, m] for m in range(4)) for a in range(2)] for i in range(8)]
    state = links(conn_ref[...])
    both = stencil_ref.at[pl.ds(0, 24), :, pl.ds(0, LINE)]
    pltpu.make_async_copy(both, both, load_sem.at[1]).wait()
    place = positions(state)
    along_j = [[None] * 8, [None] * 8]
    for j in range(8):
        for a in range(2):
            along_j[a][j] = sum(coef[i][a] * res_ref[64 * i + 8 * j : 64 * i + 8 * j + 8, :] for i in range(8))
    sub_tile = rows_of((8, 128))
    last = []
    for c in range(2):
        column = jnp.full((8, 128), coef[0][c], jnp.float32)
        for k in range(1, 8):
            column = jnp.where(sub_tile == k, coef[k][c], column)
        last.append(column)
    rows = []
    for a in range(2):
        for b in range(2):
            line = sum(coef[j][b] * along_j[a][j] for j in range(8))
            for c in range(2):
                rows.append(last[c] * line)
    for bit in (1, 2, 4):
        high = (sub_tile & bit) > 0
        pairs = zip(rows[0::2], rows[1::2])
        rows = [jnp.where(high, one + pltpu.roll(one, bit, 0), zero + pltpu.roll(zero, 8 - bit, 0)) for zero, one in pairs]
    low_res = rows[0]

    mine = spread(place[0:1])
    for b in range(1, BLOCKS):
        mine = jnp.where(group == b, spread(place[b : b + 1]), mine)
    own_hot = one_hot(mine[0:1])
    corner = mine + STRIDE * (sub_tile // 2 % 2) + sub_tile % 2
    own_lane, own_tile = (corner & 127, corner >> 7)
    greeted = group * every + below + above

    @pl.when(group > 0)
    def _():
        pl.semaphore_wait(barrier, greeted)

    tell(hello.at[group - 1], 0, jnp.minimum(group, 1), [])
    own = join_parts(lax.dot_general(parts_of(low_res), own_hot, (((1,), (1,)), ((), ())), preferred_element_type=jnp.float32))
    nodes = gather_sums(own)
    for plane in range(2):
        sums_ref[plane, group, REACH : REACH + 1, :] = nodes[4 * plane : 4 * plane + 1]

    def sides(o):
        return pl.ds(0, 2) if abs(o) < REACH else pl.ds(int(o > 0), 1)

    def sum_copy(z, o):
        return pltpu.make_async_remote_copy(
            src_ref=sums_ref.at[sides(o), group, pl.ds(REACH, 1), :],
            dst_ref=sums_ref.at[sides(o), group, pl.ds(REACH - o, 1), :],
            send_sem=sum_sent,
            recv_sem=sum_recv,
            device_id=(slab + o, z),
            device_id_type=MESH,
        )

    def whole(semaphore, rows_at):
        width = next(w for w in range(1, 9) if rows_at % w == 0 and rows_at // w <= stencil_ref.shape[0])
        view = stencil_ref.at[pl.ds(0, rows_at // width), pl.ds(0, width), :]
        return pltpu.make_async_remote_copy(src_ref=view, dst_ref=view, send_sem=semaphore, recv_sem=semaphore, device_id=(slab, group), device_id_type=MESH)

    def for_each_size(rows_of, act):
        sizes = {}
        for at in range(slabs):
            sizes.setdefault(rows_of(at), []).append(at)
        for total, places in sizes.items():
            here = functools.reduce(jnp.logical_or, [slab == at for at in places])

            @pl.when(here)
            def _():
                act(total)

    def sum_rows(at):
        return 2 * (groups - 1) + sum(groups * (2 if abs(o) < REACH else 1) for o in offsets if 0 <= at + o < slabs)

    def coef_rows(distance):
        return {1: ROWS, 2: ROWS - len(TURNS), 3: 1}[distance]

    def coef_got(at):
        crossing = at + (1 if at % 2 else -1)
        return sum(coef_rows(abs(o)) for o in offsets if 0 <= at + o < slabs and at + o != crossing)

    def coef_gone(at):
        outward = 1 if at % 2 else -1
        direct = [o for o in offsets if 0 <= at + o < slabs and o != 2 * outward]
        return sum(coef_rows(abs(o)) for o in direct) + (coef_rows(2) if 0 <= at + outward < slabs else 0)

    def coef_copy(o, arrived, source=0):
        far = abs(o - source)
        first = {1: 0, 2: 0 if o < source else 4, 3: 4 if o < source else 14}[far]
        count = coef_rows(far)
        return pltpu.make_async_remote_copy(
            src_ref=coef_ref.at[pl.ds(first, count), pl.ds(REACH + source, 1), :],
            dst_ref=coef_ref.at[pl.ds(first, count), pl.ds(REACH + source - o, 1), :],
            send_sem=coef_sent,
            recv_sem=arrived,
            device_id=(slab + o, group),
            device_id_type=MESH,
        )

    def send_sums(z, carry, upward=False):
        for o in sorted([0, *offsets], key=lambda o: (-abs(o), o) if upward else o):

            @pl.when(exists(o))
            def _():
                sum_copy(z, o).start()

        return carry

    lax.fori_loop(0, jnp.minimum(group, 1), send_sums, 0)
    tell(hello.at[group - 1], 1, group, [])
    lax.fori_loop(1, group, send_sums, 0)
    hot = jnp.concatenate([one_hot(place[b : b + 1]) for b in range(BLOCKS)], axis=1)
    ops = parts_of(ops_ref[...].reshape(64, LINE))
    lex = join_parts(lax.dot_general(ops, hot, (((1,), (1,)), ((), ())), preferred_element_type=jnp.float32))
    moved = [aligned(lex[8 * q : 8 * q + 8]) for q in range(8)]
    sub = rows_of((8, LANES))
    flat, flat_turns, _ = stencil_rows([jnp.where(sub < 4, moved[q], moved[q + 4]) for q in range(4)])
    centre, forward, backward = stencil_rows(moved[4:])
    rows = [(value, row) for value, row in flat_turns] + [flat, centre] + forward + backward
    rows += [(value, row + 4) for value, row in [flat] + flat_turns]
    for at, (value, row) in enumerate(rows):
        coef_ref[at, REACH : REACH + 1, :] = value[row : row + 1]
    even = slab % 2 == 0
    odd = jnp.logical_not(even)
    across = ((jnp.logical_and(even, exists(-1)), -1), (jnp.logical_and(odd, exists(1)), 1))
    @pl.when(jnp.logical_and(group == 0, greeted > 0))
    def _():
        pl.semaphore_wait(barrier, greeted)

    down, up = across
    for here, o, arrived in (
        (*down, cross_recv),
        (jnp.logical_and(odd, exists(-2)), -2, coef_recv),
        (*up, cross_recv),
        (jnp.logical_and(even, exists(2)), 2, coef_recv),
        (odd, -1, coef_recv),
        (even, 1, coef_recv),
        (exists(-3), -3, coef_recv),
        (exists(3), 3, coef_recv),
    ):

        @pl.when(here)
        def _():
            coef_copy(o, arrived).start()

    for o in offsets:

        @pl.when(exists(o))
        def _():
            sum_copy(group, o).start()

    def to_higher(z, carry):
        pl.semaphore_wait(hello.at[z - 1], every)
        return send_sums(z, carry, upward=True)

    lax.fori_loop(group + 1, groups, to_higher, 0)

    fine = []
    for k in range(2):
        column = jnp.full((8, 128), i31_ref[k, 0], jnp.float32)
        for c in range(1, 4):
            column = jnp.where((sub_tile & 3) == c, i31_ref[k, c], column)
        fine.append(column)
    weights = [jnp.where(sub_tile < 4, i31_ref[j, 2 * h], i31_ref[j, 2 * h + 1]) * fine[k] for h in range(2) for j in range(2) for k in range(2)]

    for here, o in across:

        @pl.when(here)
        def _():
            whole(cross_recv, ROWS).wait_recv()
            coef_copy(-o, coef_recv, source=o).start()

    for_each_size(coef_got, lambda total: whole(coef_recv, total).wait_recv())

    turns = len(TURNS)
    up_first = ROWS - turns
    steps = [STRIDE * dy + dx for dy, dx in TURNS]
    stencil_ref[0] = coef_ref[turns] + pltpu.roll(coef_ref[up_first - 1], 1, 0)
    middle = turns + 1
    stencil_ref[1] = pltpu.roll(coef_ref[middle], 1, 0)
    stencil_ref[2] = coef_ref[middle]
    for at, step in enumerate(steps):
        plane = coef_ref[at] + pltpu.roll(coef_ref[up_first + at], 1, 0)
        ahead, back = (coef_ref[middle + 1 + at], coef_ref[middle + 1 + turns + at])
        stencil_ref[3 + 6 * at] = plane
        stencil_ref[4 + 6 * at] = pltpu.roll(ahead, 1, 0)
        stencil_ref[5 + 6 * at] = pltpu.roll(back, LANES - step, 1)
        stencil_ref[6 + 6 * at] = pltpu.roll(plane, step, 1)
        stencil_ref[7 + 6 * at] = pltpu.roll(back, 1, 0)
        stencil_ref[8 + 6 * at] = pltpu.roll(ahead, step, 1)

    def operate(field):
        values = [field] + [pltpu.roll(field, shift, 1) for step in steps for shift in (LANES - step, step)]
        total = []
        for part in (1, 2, 0):
            terms = [stencil_ref[3 * at + part] * value for at, value in enumerate(values)]
            while len(terms) > 1:
                terms = [sum(terms[at : at + 2]) for at in range(0, len(terms), 2)]
            total.append(terms[0])
        return total[2] + pltpu.roll(total[0], 7, 0) + pltpu.roll(total[1], 1, 0)

    diag = stencil_ref[0]
    inverse = 1.0 / jnp.where(diag > 0.0, diag, 1.0)

    for_each_size(sum_rows, lambda total: whole(sum_sent, total).wait_send())
    for_each_size(sum_rows, lambda total: whole(sum_recv, total).wait_recv())

    low, high = (sums_ref[0, 0], sums_ref[1, 0])
    for z in range(1, groups):
        low, high = (low + sums_ref[0, z], high + sums_ref[1, z])
    remain = low + pltpu.roll(high, 1, 0)
    theta = 0.5 * (lam_high + lam_low)
    delta = 0.5 * (lam_high - lam_low)
    sigma = theta / delta
    direction = inverse * remain * (1.0 / theta)
    answer = direction
    rho = 1.0 / sigma
    for sweep in range(SWEEPS):
        remain = remain - operate(direction)
        rho_new = 1.0 / (2.0 * sigma - rho)
        direction = rho_new * rho * direction + 2.0 * rho_new / delta * inverse * remain
        answer = answer + direction
        rho = rho_new

    planes = jnp.where(sub < 4, spread(answer[REACH : REACH + 1]), spread(answer[REACH + 1 : REACH + 2]))
    picked = jnp.take_along_axis(planes[:, :128], own_lane, axis=1)
    for b in range(1, LANES // 128):
        picked = jnp.where(own_tile == b, jnp.take_along_axis(planes[:, 128 * b : 128 * b + 128], own_lane, axis=1), picked)
    values = [spread(picked[p : p + 1]) for p in range(8)]
    for h in range(2):
        ends = [sum(weights[4 * h + q] * values[4 * i + q] for q in range(4)) for i in range(2)]
        for a in range(4):
            out_ref[8 * (2 * a + h) : 8 * (2 * a + h) + 8, :] = i31_ref[0, a] * ends[0] + i31_ref[1, a] * ends[1]

    for_each_size(coef_gone, lambda total: whole(coef_sent, total).wait_send())


def one_layer(resid7, interp73, interp31, elem_ops, conn):
    slabs, groups = (lax.axis_size("slab"), lax.axis_size("grp"))
    dma = pltpu.SemaphoreType.DMA
    return pl.pallas_call(
        functools.partial(cycle_kernel, slabs, groups),
        out_shape=pltpu.VMEM((64, 128), jnp.float32),
        in_specs=[pl.BlockSpec(memory_space=pl.ANY)] * 5,
        out_specs=VMEM,
        scratch_shapes=[
            pltpu.VMEM((8, LINE), jnp.int32),
            pltpu.VMEM((8, 8, LINE), jnp.float32),
            pltpu.VMEM((512, 128), jnp.float32),
            pltpu.SMEM((4, 8), jnp.float32),
            pltpu.SMEM((2, 4), jnp.float32),
            dma((2,)),
            pltpu.VMEM((2, groups, 8, LANES), jnp.float32),
            pltpu.VMEM((ROWS, 8, LANES), jnp.float32),
            pltpu.VMEM((3 + 6 * len(TURNS), 8, LANES), jnp.float32),
            pltpu.SemaphoreType.REGULAR((groups - 1,)),
            dma,
            dma,
            dma,
            dma,
            dma,
        ],
        compiler_params=pltpu.CompilerParams(collective_id=0, has_side_effects=True),
    )(conn, elem_ops, resid7, interp73.T, interp31.T)


def dispatch(resid7, interp73, interp31, elem_ops, conn, faces):
    if conn.shape[1] == LINE and resid7.shape[1] == 128 and lax.axis_size("grp") > 1 and lax.axis_size("slab") % 2 == 0:
        return one_layer(resid7, interp73, interp31, elem_ops, conn)
    return local(resid7, interp73, interp31, elem_ops, conn, faces)


def solution(mesh):
    in_specs = (
        P(None, ("slab", "grp")),
        P(),
        P(),
        P(None, None, "slab"),
        P(None, "slab"),
        P(None, "slab", None),
    )
    out_specs = P(None, ("slab", "grp"))
    return jax.shard_map(dispatch, mesh=mesh, in_specs=in_specs, out_specs=out_specs, check_vma=False)
```

```python
import functools

import jax
import jax.numpy as jnp
from jax import lax
from jax.experimental import pallas as pl
from jax.experimental.pallas import tpu as pltpu
from jax.sharding import PartitionSpec as P

EX = 32
EY = 16
SWEEPS = 2


lam_low = 0.3
lam_high = 1.9


def extended(array, sides, width):
    for axis, dim in sides:
        count, length = (lax.axis_size(axis), array.shape[dim])
        up = [(i, (i + 1) % count) for i in range(count - 1)]
        down = [(j, i) for i, j in up]
        last = lax.slice_in_dim(array, length - width, length, axis=dim)
        first = lax.slice_in_dim(array, 0, width, axis=dim)
        before = lax.ppermute(last, axis, up)
        after = lax.ppermute(first, axis, down)
        array = jnp.concatenate([before, array, after], axis=dim)
    return array


def restrict_high(block, interp73):
    hi = lax.Precision.HIGHEST
    width = block.shape[1]
    cube = block.reshape(8, 8, 8, width)
    cube = jnp.einsum("kc,ijkm->ijcm", interp73, cube, precision=hi)
    cube = jnp.einsum("jb,ijcm->ibcm", interp73, cube, precision=hi)
    cube = jnp.einsum("ia,ibcm->abcm", interp73, cube, precision=hi)
    return cube.reshape(64, width)


def restrict_low(block, interp31):
    hi = lax.Precision.HIGHEST
    width = block.shape[1]
    cube = block.reshape(4, 4, 4, width)
    cube = jnp.einsum("kc,ijkm->ijcm", interp31, cube, precision=hi)
    cube = jnp.einsum("jb,ijcm->ibcm", interp31, cube, precision=hi)
    cube = jnp.einsum("ia,ibcm->abcm", interp31, cube, precision=hi)
    return cube.reshape(8, width)


def prolong(coarse, interp31):
    hi = lax.Precision.HIGHEST
    width = coarse.shape[1]
    cube = coarse.reshape(2, 2, 2, width)
    cube = jnp.einsum("ck,ijkm->ijcm", interp31, cube, precision=hi)
    cube = jnp.einsum("bj,ijcm->ibcm", interp31, cube, precision=hi)
    cube = jnp.einsum("ai,ibcm->abcm", interp31, cube, precision=hi)
    return cube.reshape(64, width)


def assemble(values, conn_ids, count):
    layers = values.shape[0]
    flat = values.reshape(layers, -1).T
    summed = jax.ops.segment_sum(flat, conn_ids.reshape(-1), num_segments=count)
    return summed.T


def element_term(operators, conn_ids, field):
    return jnp.einsum("pqe,qe->pe", operators, field[conn_ids], precision=lax.Precision.HIGHEST)


def share(nodes, faces):
    lower = faces[0, 0]
    upper = faces[1, 0]
    planes = jnp.stack([nodes[:, lower], nodes[:, upper]], axis=1)
    padded = extended(planes, (("slab", 1),), 1)
    return nodes.at[:, lower].add(padded[:, 0]).at[:, upper].add(padded[:, 3])


def local(resid7, interp73, interp31, elem_ops, conn, faces):
    own = resid7.shape[1]
    slab_elems = conn.shape[1]
    layers = slab_elems // (EX * EY)
    count = (EX + 1) * (EY + 1) * (layers + 1)
    start = lax.axis_index("grp") * own
    own_conn = lax.dynamic_slice_in_dim(conn, start, own, 1)
    middle_res = restrict_high(resid7, interp73)
    blocks = lax.all_gather(middle_res, "grp", axis=1, tiled=True)
    slab_res = restrict_low(blocks, interp31)
    pair = jnp.stack([slab_res, jnp.einsum("ppe->pe", elem_ops)])
    both_nodes = assemble(pair, conn, count)
    shared = share(both_nodes, faces)
    rhs = shared[0]
    diag = shared[1]
    theta = 0.5 * (lam_high + lam_low)
    delta = 0.5 * (lam_high - lam_low)
    sigma = theta / delta
    inverse = 1.0 / diag
    direction = inverse * rhs / theta
    solution = direction
    remain = rhs
    rho = 1.0 / sigma
    for sweep in range(SWEEPS):
        nodes = assemble(element_term(elem_ops, conn, direction)[None], conn, count)
        remain = remain - share(nodes, faces)[0]
        rho_new = 1.0 / (2.0 * sigma - rho)
        direction = rho_new * rho * direction + 2.0 * rho_new / delta * inverse * remain
        solution = solution + direction
        rho = rho_new
    return prolong(solution[own_conn], interp31)


STRIDE = EX + 1
POINTS = (EX + 1) * (EY + 1)
LANES = (POINTS + 127) // 128 * 128
LINE = EX * EY
BLOCKS = LINE // 128
REACH = SWEEPS + 1
TURNS = ((0, 1), (1, -1), (1, 0), (1, 1))
ROWS = 2 * (len(TURNS) + 1) + 2 * len(TURNS) + 1
MESH = pl.DeviceIdType.MESH
VMEM = pl.BlockSpec(memory_space=pltpu.VMEM)
SMEM = pl.BlockSpec(memory_space=pltpu.SMEM)


def rows_of(shape):
    return lax.broadcasted_iota(jnp.int32, shape, 0)


def spread(row, count=8):
    return jnp.broadcast_to(row, (count, row.shape[1]))


def stack_rows(rows):
    sub = rows_of((8, rows[0].shape[1]))
    out = spread(rows[0])
    for at in range(1, 8):
        out = jnp.where(sub == at, spread(rows[at]), out)
    return out


def parts_of(value):
    hi = value.astype(jnp.bfloat16).astype(jnp.float32)
    left = value - hi
    mid = left.astype(jnp.bfloat16).astype(jnp.float32)
    return jnp.concatenate([hi, mid, left - mid], axis=0).astype(jnp.bfloat16)


def join_parts(value):
    third = value.shape[0] // 3
    return value[:third] + value[third : 2 * third] + value[2 * third :]


def aligned(value):
    sub = rows_of(value.shape)
    odd, second = ((sub & 1) == 1, (sub & 2) == 2)
    near = jnp.where(odd, pltpu.roll(value, 1, 1), value)
    far = jnp.where(odd, pltpu.roll(value, STRIDE + 1, 1), pltpu.roll(value, STRIDE, 1))
    return jnp.where(second, far, near)


def gather_sums(corners):
    part = aligned(corners)
    part = part + pltpu.roll(part, 7, 0)
    return part + pltpu.roll(part, 6, 0)


def stencil_rows(columns):
    sub = rows_of(columns[0].shape)
    odd, second = ((sub & 1) == 1, (sub & 2) == 2)

    def over_x(part):
        return part + jnp.where(odd, pltpu.roll(part, 1, 0), pltpu.roll(part, 7, 0))

    def over_y(part):
        return part + jnp.where(second, pltpu.roll(part, 2, 0), pltpu.roll(part, 6, 0))

    c0, c1, c2, c3 = columns
    centre = over_y(over_x(jnp.where(second, jnp.where(odd, c3, c2), jnp.where(odd, c1, c0))))
    along_x = over_y(jnp.where(second, jnp.where(odd, c2, c3), jnp.where(odd, c0, c1)))
    along_y = over_x(jnp.where(second, jnp.where(odd, c1, c0), jnp.where(odd, c3, c2)))
    forward = [(along_x, 0), (c2, 1), (along_y, 0), (c3, 0)]
    backward = [(along_x, 1), (c1, 2), (along_y, 2), (c0, 3)]
    return (centre, 0), forward, backward


def coded(number):
    return (128 + (number & 127)) * jnp.left_shift(1, number >> 7)


def before(ids, mine, theirs):
    column = jnp.broadcast_to(ids[theirs : theirs + 1], (128, LINE)).T.astype(jnp.bfloat16)
    row = spread(ids[mine : mine + 1], 16).astype(jnp.bfloat16)
    place = rows_of((16, 128))
    total = jnp.zeros((16, LINE), jnp.bfloat16)
    for at in range(LINE // 16):
        one = column[16 * at : 16 * at + 16]
        same = jnp.concatenate([one] * BLOCKS, axis=1) == row
        value = (place * (1 << (at >> 3)) + ((128 + (16 * at & 127)) << (at >> 3))).astype(jnp.float32).astype(jnp.bfloat16)
        total = jnp.where(same, jnp.concatenate([value] * BLOCKS, axis=1), total)
    return jnp.sum(total.astype(jnp.float32), axis=0, keepdims=True)


def links(conn):
    ids = coded(conn).astype(jnp.float32)
    own = lax.broadcasted_iota(jnp.int32, (1, LINE), 1)
    rows = []
    for theirs in (1, 2):
        code = before(ids, 0, theirs).astype(jnp.int32)
        power = sum((code >= 256 << k).astype(jnp.int32) for k in range((LINE - 1) >> 7))
        found = (code >> power) - 128 + 128 * power
        packed = jnp.where(code > 0, found + LINE, own)
        rows += [packed[:, 128 * b : 128 * b + 128] for b in range(BLOCKS)]
    return stack_rows([row for pair in zip(rows[:BLOCKS], rows[BLOCKS:]) for row in pair])


def positions(state):
    block = rows_of((8, 128)) >> 1
    for _ in range((EX - 1).bit_length()):
        target = state & (LINE - 1)
        away = ((target >> 7) - block) & (BLOCKS - 1)
        found = [jnp.take_along_axis(pltpu.roll(state, 8 - 2 * k, 0) if k else state, target & 127, axis=1) for k in range(BLOCKS)]
        bit = 1
        while len(found) > 1:
            high = (away & bit) > 0
            found = [jnp.where(high, two, one) for one, two in zip(found[0::2], found[1::2])]
            bit *= 2
        state = found[0] + (state - target)
    steps = state >> (LINE.bit_length() - 1)
    return steps + STRIDE * pltpu.roll(steps, 7, 0)


def one_hot(row):
    return jnp.where(rows_of((LANES, row.shape[1])) == spread(row, LANES), 1.0, 0.0).astype(jnp.bfloat16)


def cycle_kernel(slabs, groups, conn_hbm, ops_hbm, res_hbm, i73_hbm, i31_hbm, out_ref, conn_ref, ops_ref, res_ref, i73_ref, i31_ref, load_sem, sums_ref, coef_ref, stencil_ref, hello, sum_sent, coef_sent, sum_recv, coef_recv, cross_recv):
    slab, group = (lax.axis_index("slab"), lax.axis_index("grp"))
    offsets = [o for o in range(-REACH, REACH + 1) if o != 0]
    below, above = (jnp.minimum(slab, REACH), jnp.minimum(slabs - 1 - slab, REACH))
    every = below + above + 1

    def exists(o):
        return slab >= -o if o < 0 else slab < slabs - o

    loads = [
        pltpu.make_async_copy(source, target, (sum_sent, coef_sent, load_sem.at[0], load_sem.at[1], load_sem.at[1])[at])
        for at, (source, target) in enumerate(((i73_hbm, i73_ref), (i31_hbm, i31_ref), (conn_hbm, conn_ref), (res_hbm, res_ref), (ops_hbm, ops_ref)))
    ]
    for load in loads:
        load.start()
    sums_ref[...] = jnp.zeros(sums_ref.shape, jnp.float32)
    coef_ref[...] = jnp.zeros(coef_ref.shape, jnp.float32)

    def tell(semaphore, first, last, some):
        def visit(z, carry):
            pl.semaphore_signal(semaphore, inc=1, device_id=(slab, z), device_id_type=MESH)
            for o in offsets:

                @pl.when(exists(o))
                def _():
                    pl.semaphore_signal(semaphore, inc=1, device_id=(slab + o, z), device_id_type=MESH)

            return carry

        lax.fori_loop(first, last, visit, 0)
        for o in some:

            @pl.when(exists(o))
            def _():
                pl.semaphore_signal(semaphore, inc=1, device_id=(slab + o, group), device_id_type=MESH)

    barrier = pltpu.get_barrier_semaphore()
    tell(barrier, group + 1, groups, offsets)

    for load in loads[:3]:
        load.wait()
    coef = [[sum(i73_ref[m, i] * i31_ref[a, m] for m in range(4)) for a in range(2)] for i in range(8)]
    state = links(conn_ref[...])
    both = stencil_ref.at[pl.ds(0, 24), :, pl.ds(0, LINE)]
    pltpu.make_async_copy(both, both, load_sem.at[1]).wait()
    place = positions(state)
    along_j = [[None] * 8, [None] * 8]
    for j in range(8):
        for a in range(2):
            along_j[a][j] = sum(coef[i][a] * res_ref[64 * i + 8 * j : 64 * i + 8 * j + 8, :] for i in range(8))
    sub_tile = rows_of((8, 128))
    last = []
    for c in range(2):
        column = jnp.full((8, 128), coef[0][c], jnp.float32)
        for k in range(1, 8):
            column = jnp.where(sub_tile == k, coef[k][c], column)
        last.append(column)
    rows = []
    for a in range(2):
        for b in range(2):
            line = sum(coef[j][b] * along_j[a][j] for j in range(8))
            for c in range(2):
                rows.append(last[c] * line)
    for bit in (1, 2, 4):
        high = (sub_tile & bit) > 0
        pairs = zip(rows[0::2], rows[1::2])
        rows = [jnp.where(high, one + pltpu.roll(one, bit, 0), zero + pltpu.roll(zero, 8 - bit, 0)) for zero, one in pairs]
    low_res = rows[0]

    mine = spread(place[0:1])
    for b in range(1, BLOCKS):
        mine = jnp.where(group == b, spread(place[2 * b : 2 * b + 1]), mine)
    own_hot = one_hot(mine[0:1])
    corner = mine + STRIDE * (sub_tile // 2 % 2) + sub_tile % 2
    own_lane, own_tile = (corner & 127, corner >> 7)
    greeted = group * every + below + above

    @pl.when(group > 0)
    def _():
        pl.semaphore_wait(barrier, greeted)

    tell(hello.at[jnp.maximum(group - 1, 0)], 0, jnp.minimum(group, 1), [])
    low_parts = parts_of(low_res)
    halves = [lax.dot_general(low_parts, half, (((1,), (1,)), ((), ())), preferred_element_type=jnp.float32) for half in (own_hot[:256], own_hot[256:])]
    own = join_parts(jnp.concatenate(halves, axis=1))
    nodes = gather_sums(own)
    for plane in range(2):
        sums_ref[plane, group, REACH : REACH + 1, :] = nodes[4 * plane : 4 * plane + 1]

    def sides(o):
        return pl.ds(0, 2) if abs(o) < REACH else pl.ds(int(o > 0), 1)

    def sum_copy(z, o):
        return pltpu.make_async_remote_copy(
            src_ref=sums_ref.at[sides(o), group, pl.ds(REACH, 1), :],
            dst_ref=sums_ref.at[sides(o), group, pl.ds(REACH - o, 1), :],
            send_sem=sum_sent,
            recv_sem=sum_recv,
            device_id=(slab + o, z),
            device_id_type=MESH,
        )

    def whole(semaphore, rows_at):
        width = next(w for w in range(1, 9) if rows_at % w == 0 and rows_at // w <= stencil_ref.shape[0])
        view = stencil_ref.at[pl.ds(0, rows_at // width), pl.ds(0, width), :]
        return pltpu.make_async_remote_copy(src_ref=view, dst_ref=view, send_sem=semaphore, recv_sem=semaphore, device_id=(slab, group), device_id_type=MESH)

    def for_each_size(rows_of, act):
        sizes = {}
        for at in range(slabs):
            sizes.setdefault(rows_of(at), []).append(at)
        for total, places in sizes.items():
            here = functools.reduce(jnp.logical_or, [slab == at for at in places])

            @pl.when(here)
            def _():
                act(total)

    def sum_rows(at):
        return 2 * (groups - 1) + sum(groups * (2 if abs(o) < REACH else 1) for o in offsets if 0 <= at + o < slabs)

    def coef_rows(distance):
        return {1: ROWS, 2: ROWS - len(TURNS), 3: 1}[distance]

    def coef_got(at):
        crossing = at + (1 if at % 2 else -1)
        return sum(coef_rows(abs(o)) for o in offsets if 0 <= at + o < slabs and at + o != crossing)

    def coef_gone(at):
        outward = 1 if at % 2 else -1
        direct = [o for o in offsets if 0 <= at + o < slabs and o != 2 * outward]
        return sum(coef_rows(abs(o)) for o in direct) + (coef_rows(2) if 0 <= at + outward < slabs else 0)

    def coef_copy(o, arrived, source=0):
        far = abs(o - source)
        first = {1: 0, 2: 0 if o < source else 4, 3: 4 if o < source else 14}[far]
        count = coef_rows(far)
        return pltpu.make_async_remote_copy(
            src_ref=coef_ref.at[pl.ds(first, count), pl.ds(REACH + source, 1), :],
            dst_ref=coef_ref.at[pl.ds(first, count), pl.ds(REACH + source - o, 1), :],
            send_sem=coef_sent,
            recv_sem=arrived,
            device_id=(slab + o, group),
            device_id_type=MESH,
        )

    def send_sums(z, carry, upward=False):
        for o in sorted([0, *offsets], key=lambda o: (-abs(o), o) if upward else o):

            @pl.when(exists(o))
            def _():
                sum_copy(z, o).start()

        return carry

    lax.fori_loop(0, jnp.minimum(group, 1), send_sums, 0)
    tell(hello.at[jnp.maximum(group - 1, 0)], 1, group, [])
    lax.fori_loop(1, group, send_sums, 0)
    hot = jnp.concatenate([one_hot(place[2 * b : 2 * b + 1]) for b in range(BLOCKS)], axis=1)
    ops = parts_of(ops_ref[...].reshape(64, LINE))
    lex = join_parts(lax.dot_general(ops, hot, (((1,), (1,)), ((), ())), preferred_element_type=jnp.float32))
    moved = [aligned(lex[8 * q : 8 * q + 8]) for q in range(8)]
    sub = rows_of((8, LANES))
    flat, flat_turns, _ = stencil_rows([jnp.where(sub < 4, moved[q], moved[q + 4]) for q in range(4)])
    centre, forward, backward = stencil_rows(moved[4:])
    rows = [(value, row) for value, row in flat_turns] + [flat, centre] + forward + backward
    rows += [(value, row + 4) for value, row in [flat] + flat_turns]
    for at, (value, row) in enumerate(rows):
        coef_ref[at, REACH : REACH + 1, :] = value[row : row + 1]
    even = slab % 2 == 0
    odd = jnp.logical_not(even)
    across = ((jnp.logical_and(even, exists(-1)), -1), (jnp.logical_and(odd, exists(1)), 1))
    @pl.when(jnp.logical_and(group == 0, greeted > 0))
    def _():
        pl.semaphore_wait(barrier, greeted)

    down, up = across
    for here, o, arrived in (
        (*down, cross_recv),
        (jnp.logical_and(odd, exists(-2)), -2, coef_recv),
        (*up, cross_recv),
        (jnp.logical_and(even, exists(2)), 2, coef_recv),
        (odd, -1, coef_recv),
        (even, 1, coef_recv),
        (exists(-3), -3, coef_recv),
        (exists(3), 3, coef_recv),
    ):

        @pl.when(here)
        def _():
            coef_copy(o, arrived).start()

    for o in offsets:

        @pl.when(exists(o))
        def _():
            sum_copy(group, o).start()

    def to_higher(z, carry):
        pl.semaphore_wait(hello.at[z - 1], every)
        return send_sums(z, carry, upward=True)

    lax.fori_loop(group + 1, groups, to_higher, 0)

    fine = []
    for k in range(2):
        column = jnp.full((8, 128), i31_ref[k, 0], jnp.float32)
        for c in range(1, 4):
            column = jnp.where((sub_tile & 3) == c, i31_ref[k, c], column)
        fine.append(column)
    weights = [jnp.where(sub_tile < 4, i31_ref[j, 2 * h], i31_ref[j, 2 * h + 1]) * fine[k] for h in range(2) for j in range(2) for k in range(2)]

    for here, o in across:

        @pl.when(here)
        def _():
            whole(cross_recv, ROWS).wait_recv()
            coef_copy(-o, coef_recv, source=o).start()

    for_each_size(coef_got, lambda total: whole(coef_recv, total).wait_recv())

    turns = len(TURNS)
    up_first = ROWS - turns
    steps = [STRIDE * dy + dx for dy, dx in TURNS]
    stencil_ref[0] = coef_ref[turns] + pltpu.roll(coef_ref[up_first - 1], 1, 0)
    middle = turns + 1
    stencil_ref[1] = pltpu.roll(coef_ref[middle], 1, 0)
    stencil_ref[2] = coef_ref[middle]
    for at, step in enumerate(steps):
        plane = coef_ref[at] + pltpu.roll(coef_ref[up_first + at], 1, 0)
        ahead, back = (coef_ref[middle + 1 + at], coef_ref[middle + 1 + turns + at])
        stencil_ref[3 + 6 * at] = plane
        stencil_ref[4 + 6 * at] = pltpu.roll(ahead, 1, 0)
        stencil_ref[5 + 6 * at] = pltpu.roll(back, LANES - step, 1)
        stencil_ref[6 + 6 * at] = pltpu.roll(plane, step, 1)
        stencil_ref[7 + 6 * at] = pltpu.roll(back, 1, 0)
        stencil_ref[8 + 6 * at] = pltpu.roll(ahead, step, 1)

    def operate(field):
        values = [field] + [pltpu.roll(field, shift, 1) for step in steps for shift in (LANES - step, step)]
        total = []
        for part in (1, 2, 0):
            terms = [stencil_ref[3 * at + part] * value for at, value in enumerate(values)]
            while len(terms) > 1:
                terms = [sum(terms[at : at + 2]) for at in range(0, len(terms), 2)]
            total.append(terms[0])
        return total[2] + pltpu.roll(total[0], 7, 0) + pltpu.roll(total[1], 1, 0)

    diag = stencil_ref[0]
    inverse = 1.0 / jnp.where(diag > 0.0, diag, 1.0)

    for_each_size(sum_rows, lambda total: whole(sum_sent, total).wait_send())
    for_each_size(sum_rows, lambda total: whole(sum_recv, total).wait_recv())

    low, high = (sums_ref[0, 0], sums_ref[1, 0])
    for z in range(1, groups):
        low, high = (low + sums_ref[0, z], high + sums_ref[1, z])
    remain = low + pltpu.roll(high, 1, 0)
    theta = 0.5 * (lam_high + lam_low)
    delta = 0.5 * (lam_high - lam_low)
    sigma = theta / delta
    direction = inverse * remain * (1.0 / theta)
    answer = direction
    rho = 1.0 / sigma
    for sweep in range(SWEEPS):
        remain = remain - operate(direction)
        rho_new = 1.0 / (2.0 * sigma - rho)
        direction = rho_new * rho * direction + 2.0 * rho_new / delta * inverse * remain
        answer = answer + direction
        rho = rho_new

    planes = jnp.where(sub < 4, spread(answer[REACH : REACH + 1]), spread(answer[REACH + 1 : REACH + 2]))
    picked = jnp.take_along_axis(planes[:, :128], own_lane, axis=1)
    for b in range(1, LANES // 128):
        picked = jnp.where(own_tile == b, jnp.take_along_axis(planes[:, 128 * b : 128 * b + 128], own_lane, axis=1), picked)
    values = [spread(picked[p : p + 1]) for p in range(8)]
    for h in range(2):
        ends = [sum(weights[4 * h + q] * values[4 * i + q] for q in range(4)) for i in range(2)]
        for a in range(4):
            out_ref[8 * (2 * a + h) : 8 * (2 * a + h) + 8, :] = i31_ref[0, a] * ends[0] + i31_ref[1, a] * ends[1]

    for_each_size(coef_gone, lambda total: whole(coef_sent, total).wait_send())


def one_layer(resid7, interp73, interp31, elem_ops, conn):
    slabs, groups = (lax.axis_size("slab"), lax.axis_size("grp"))
    dma = pltpu.SemaphoreType.DMA
    return pl.pallas_call(
        functools.partial(cycle_kernel, slabs, groups),
        out_shape=pltpu.VMEM((64, 128), jnp.float32),
        in_specs=[pl.BlockSpec(memory_space=pl.ANY)] * 5,
        out_specs=VMEM,
        scratch_shapes=[
            pltpu.VMEM((8, LINE), jnp.int32),
            pltpu.VMEM((8, 8, LINE), jnp.float32),
            pltpu.VMEM((512, 128), jnp.float32),
            pltpu.SMEM((4, 8), jnp.float32),
            pltpu.SMEM((2, 4), jnp.float32),
            dma((2,)),
            pltpu.VMEM((2, groups, 8, LANES), jnp.float32),
            pltpu.VMEM((ROWS, 8, LANES), jnp.float32),
            pltpu.VMEM((3 + 6 * len(TURNS), 8, LANES), jnp.float32),
            pltpu.SemaphoreType.REGULAR((groups - 1,)),
            dma,
            dma,
            dma,
            dma,
            dma,
        ],
        compiler_params=pltpu.CompilerParams(collective_id=0, has_side_effects=True),
    )(conn, elem_ops, resid7, interp73.T, interp31.T)


def dispatch(resid7, interp73, interp31, elem_ops, conn, faces):
    if conn.shape[1] == LINE and resid7.shape[1] == 128 and lax.axis_size("grp") > 1 and lax.axis_size("slab") % 2 == 0:
        return one_layer(resid7, interp73, interp31, elem_ops, conn)
    return local(resid7, interp73, interp31, elem_ops, conn, faces)


def solution(mesh):
    in_specs = (
        P(None, ("slab", "grp")),
        P(),
        P(),
        P(None, None, "slab"),
        P(None, "slab"),
        P(None, "slab", None),
    )
    out_specs = P(None, ("slab", "grp"))
    return jax.shard_map(dispatch, mesh=mesh, in_specs=in_specs, out_specs=out_specs, check_vma=False)
```

```python
import functools

import jax
import jax.numpy as jnp
from jax import lax
from jax.experimental import pallas as pl
from jax.experimental.pallas import tpu as pltpu
from jax.sharding import PartitionSpec as P

EX = 32
EY = 16
SWEEPS = 2


lam_low = 0.3
lam_high = 1.9


def extended(array, sides, width):
    for axis, dim in sides:
        count, length = (lax.axis_size(axis), array.shape[dim])
        up = [(i, (i + 1) % count) for i in range(count - 1)]
        down = [(j, i) for i, j in up]
        last = lax.slice_in_dim(array, length - width, length, axis=dim)
        first = lax.slice_in_dim(array, 0, width, axis=dim)
        before = lax.ppermute(last, axis, up)
        after = lax.ppermute(first, axis, down)
        array = jnp.concatenate([before, array, after], axis=dim)
    return array


def restrict_high(block, interp73):
    hi = lax.Precision.HIGHEST
    width = block.shape[1]
    cube = block.reshape(8, 8, 8, width)
    cube = jnp.einsum("kc,ijkm->ijcm", interp73, cube, precision=hi)
    cube = jnp.einsum("jb,ijcm->ibcm", interp73, cube, precision=hi)
    cube = jnp.einsum("ia,ibcm->abcm", interp73, cube, precision=hi)
    return cube.reshape(64, width)


def restrict_low(block, interp31):
    hi = lax.Precision.HIGHEST
    width = block.shape[1]
    cube = block.reshape(4, 4, 4, width)
    cube = jnp.einsum("kc,ijkm->ijcm", interp31, cube, precision=hi)
    cube = jnp.einsum("jb,ijcm->ibcm", interp31, cube, precision=hi)
    cube = jnp.einsum("ia,ibcm->abcm", interp31, cube, precision=hi)
    return cube.reshape(8, width)


def prolong(coarse, interp31):
    hi = lax.Precision.HIGHEST
    width = coarse.shape[1]
    cube = coarse.reshape(2, 2, 2, width)
    cube = jnp.einsum("ck,ijkm->ijcm", interp31, cube, precision=hi)
    cube = jnp.einsum("bj,ijcm->ibcm", interp31, cube, precision=hi)
    cube = jnp.einsum("ai,ibcm->abcm", interp31, cube, precision=hi)
    return cube.reshape(64, width)


def assemble(values, conn_ids, count):
    layers = values.shape[0]
    flat = values.reshape(layers, -1).T
    summed = jax.ops.segment_sum(flat, conn_ids.reshape(-1), num_segments=count)
    return summed.T


def element_term(operators, conn_ids, field):
    return jnp.einsum("pqe,qe->pe", operators, field[conn_ids], precision=lax.Precision.HIGHEST)


def share(nodes, faces):
    lower = faces[0, 0]
    upper = faces[1, 0]
    planes = jnp.stack([nodes[:, lower], nodes[:, upper]], axis=1)
    padded = extended(planes, (("slab", 1),), 1)
    return nodes.at[:, lower].add(padded[:, 0]).at[:, upper].add(padded[:, 3])


def local(resid7, interp73, interp31, elem_ops, conn, faces):
    own = resid7.shape[1]
    slab_elems = conn.shape[1]
    layers = slab_elems // (EX * EY)
    count = (EX + 1) * (EY + 1) * (layers + 1)
    start = lax.axis_index("grp") * own
    own_conn = lax.dynamic_slice_in_dim(conn, start, own, 1)
    middle_res = restrict_high(resid7, interp73)
    blocks = lax.all_gather(middle_res, "grp", axis=1, tiled=True)
    slab_res = restrict_low(blocks, interp31)
    pair = jnp.stack([slab_res, jnp.einsum("ppe->pe", elem_ops)])
    both_nodes = assemble(pair, conn, count)
    shared = share(both_nodes, faces)
    rhs = shared[0]
    diag = shared[1]
    theta = 0.5 * (lam_high + lam_low)
    delta = 0.5 * (lam_high - lam_low)
    sigma = theta / delta
    inverse = 1.0 / diag
    direction = inverse * rhs / theta
    solution = direction
    remain = rhs
    rho = 1.0 / sigma
    for sweep in range(SWEEPS):
        nodes = assemble(element_term(elem_ops, conn, direction)[None], conn, count)
        remain = remain - share(nodes, faces)[0]
        rho_new = 1.0 / (2.0 * sigma - rho)
        direction = rho_new * rho * direction + 2.0 * rho_new / delta * inverse * remain
        solution = solution + direction
        rho = rho_new
    return prolong(solution[own_conn], interp31)


STRIDE = EX + 1
POINTS = (EX + 1) * (EY + 1)
LANES = (POINTS + 127) // 128 * 128
LINE = EX * EY
BLOCKS = LINE // 128
REACH = SWEEPS + 1
TURNS = ((0, 1), (1, -1), (1, 0), (1, 1))
ROWS = 2 * (len(TURNS) + 1) + 2 * len(TURNS) + 1
MESH = pl.DeviceIdType.MESH
VMEM = pl.BlockSpec(memory_space=pltpu.VMEM)
SMEM = pl.BlockSpec(memory_space=pltpu.SMEM)


def rows_of(shape):
    return lax.broadcasted_iota(jnp.int32, shape, 0)


def spread(row, count=8):
    return jnp.broadcast_to(row, (count, row.shape[1]))


def stack_rows(rows):
    sub = rows_of((8, rows[0].shape[1]))
    out = spread(rows[0])
    for at in range(1, 8):
        out = jnp.where(sub == at, spread(rows[at]), out)
    return out


def parts_of(value):
    hi = value.astype(jnp.bfloat16).astype(jnp.float32)
    left = value - hi
    mid = left.astype(jnp.bfloat16).astype(jnp.float32)
    return jnp.concatenate([hi, mid, left - mid], axis=0).astype(jnp.bfloat16)


def join_parts(value):
    third = value.shape[0] // 3
    return value[:third] + value[third : 2 * third] + value[2 * third :]


def aligned(value):
    sub = rows_of(value.shape)
    odd, second = ((sub & 1) == 1, (sub & 2) == 2)
    near = jnp.where(odd, pltpu.roll(value, 1, 1), value)
    far = jnp.where(odd, pltpu.roll(value, STRIDE + 1, 1), pltpu.roll(value, STRIDE, 1))
    return jnp.where(second, far, near)


def gather_sums(corners):
    part = aligned(corners)
    part = part + pltpu.roll(part, 7, 0)
    return part + pltpu.roll(part, 6, 0)


def stencil_rows(columns):
    sub = rows_of(columns[0].shape)
    odd, second = ((sub & 1) == 1, (sub & 2) == 2)

    def over_x(part):
        return part + jnp.where(odd, pltpu.roll(part, 1, 0), pltpu.roll(part, 7, 0))

    def over_y(part):
        return part + jnp.where(second, pltpu.roll(part, 2, 0), pltpu.roll(part, 6, 0))

    c0, c1, c2, c3 = columns
    centre = over_y(over_x(jnp.where(second, jnp.where(odd, c3, c2), jnp.where(odd, c1, c0))))
    along_x = over_y(jnp.where(second, jnp.where(odd, c2, c3), jnp.where(odd, c0, c1)))
    along_y = over_x(jnp.where(second, jnp.where(odd, c1, c0), jnp.where(odd, c3, c2)))
    forward = [(along_x, 0), (c2, 1), (along_y, 0), (c3, 0)]
    backward = [(along_x, 1), (c1, 2), (along_y, 2), (c0, 3)]
    return (centre, 0), forward, backward


def coded(number):
    return (128 + (number & 127)) * jnp.left_shift(1, number >> 7)


def before(ids, mine, theirs):
    column = jnp.broadcast_to(ids[theirs : theirs + 1], (128, LINE)).T.astype(jnp.bfloat16)
    row = spread(ids[mine : mine + 1], 16).astype(jnp.bfloat16)
    place = rows_of((16, 128))
    total = jnp.zeros((16, LINE), jnp.bfloat16)
    for at in range(LINE // 16):
        one = column[16 * at : 16 * at + 16]
        same = jnp.concatenate([one] * BLOCKS, axis=1) == row
        value = (place * (1 << (at >> 3)) + ((128 + (16 * at & 127)) << (at >> 3))).astype(jnp.float32).astype(jnp.bfloat16)
        total = jnp.where(same, jnp.concatenate([value] * BLOCKS, axis=1), total)
    return jnp.sum(total.astype(jnp.float32), axis=0, keepdims=True)


def links(conn):
    ids = coded(conn).astype(jnp.float32)
    own = lax.broadcasted_iota(jnp.int32, (1, LINE), 1)
    rows = []
    for theirs in (1, 2):
        code = before(ids, 0, theirs).astype(jnp.int32)
        power = sum((code >= 256 << k).astype(jnp.int32) for k in range((LINE - 1) >> 7))
        found = (code >> power) - 128 + 128 * power
        packed = jnp.where(code > 0, found + LINE, own)
        rows += [packed[:, 128 * b : 128 * b + 128] for b in range(BLOCKS)]
    return stack_rows([row for pair in zip(rows[:BLOCKS], rows[BLOCKS:]) for row in pair])


def positions(state):
    block = rows_of((8, 128)) >> 1
    for _ in range((EX - 1).bit_length()):
        target = state & (LINE - 1)
        away = ((target >> 7) - block) & (BLOCKS - 1)
        found = [jnp.take_along_axis(pltpu.roll(state, 8 - 2 * k, 0) if k else state, target & 127, axis=1) for k in range(BLOCKS)]
        bit = 1
        while len(found) > 1:
            high = (away & bit) > 0
            found = [jnp.where(high, two, one) for one, two in zip(found[0::2], found[1::2])]
            bit *= 2
        state = found[0] + (state - target)
    steps = state >> (LINE.bit_length() - 1)
    return steps + STRIDE * pltpu.roll(steps, 7, 0)


def one_hot(row):
    return jnp.where(rows_of((LANES, row.shape[1])) == spread(row, LANES), 1.0, 0.0).astype(jnp.bfloat16)


def cycle_kernel(slabs, groups, conn_hbm, ops_hbm, res_hbm, i73_hbm, i31_hbm, out_ref, conn_ref, ops_ref, res_ref, i73_ref, i31_ref, load_sem, sums_ref, coef_ref, stencil_ref, hello, sum_sent, coef_sent, sum_recv, coef_recv, cross_recv):
    slab, group = (lax.axis_index("slab"), lax.axis_index("grp"))
    offsets = [o for o in range(-REACH, REACH + 1) if o != 0]
    below, above = (jnp.minimum(slab, REACH), jnp.minimum(slabs - 1 - slab, REACH))
    every = below + above + 1

    def exists(o):
        return slab >= -o if o < 0 else slab < slabs - o

    loads = [
        pltpu.make_async_copy(source, target, (sum_sent, coef_sent, load_sem.at[0], load_sem.at[1], load_sem.at[1])[at])
        for at, (source, target) in enumerate(((i73_hbm, i73_ref), (i31_hbm, i31_ref), (conn_hbm, conn_ref), (res_hbm, res_ref), (ops_hbm, ops_ref)))
    ]
    for load in loads:
        load.start()
    sums_ref[...] = jnp.zeros(sums_ref.shape, jnp.float32)
    coef_ref[...] = jnp.zeros(coef_ref.shape, jnp.float32)

    def tell(semaphore, first, last, some):
        def visit(z, carry):
            pl.semaphore_signal(semaphore, inc=1, device_id=(slab, z), device_id_type=MESH)
            for o in offsets:

                @pl.when(exists(o))
                def _():
                    pl.semaphore_signal(semaphore, inc=1, device_id=(slab + o, z), device_id_type=MESH)

            return carry

        lax.fori_loop(first, last, visit, 0)
        for o in some:

            @pl.when(exists(o))
            def _():
                pl.semaphore_signal(semaphore, inc=1, device_id=(slab + o, group), device_id_type=MESH)

    barrier = pltpu.get_barrier_semaphore()
    tell(barrier, group + 1, groups, offsets)

    for load in loads[:3]:
        load.wait()
    coef = [[sum(i73_ref[m, i] * i31_ref[a, m] for m in range(4)) for a in range(2)] for i in range(8)]
    state = links(conn_ref[...])
    both = stencil_ref.at[pl.ds(0, 24), :, pl.ds(0, LINE)]
    pltpu.make_async_copy(both, both, load_sem.at[1]).wait()
    place = positions(state)
    along_j = [[None] * 8, [None] * 8]
    for j in range(8):
        for a in range(2):
            along_j[a][j] = sum(coef[i][a] * res_ref[64 * i + 8 * j : 64 * i + 8 * j + 8, :] for i in range(8))
    sub_tile = rows_of((8, 128))
    last = []
    for c in range(2):
        column = jnp.full((8, 128), coef[0][c], jnp.float32)
        for k in range(1, 8):
            column = jnp.where(sub_tile == k, coef[k][c], column)
        last.append(column)
    rows = []
    for a in range(2):
        for b in range(2):
            line = sum(coef[j][b] * along_j[a][j] for j in range(8))
            for c in range(2):
                rows.append(last[c] * line)
    for bit in (1, 2, 4):
        high = (sub_tile & bit) > 0
        pairs = zip(rows[0::2], rows[1::2])
        rows = [jnp.where(high, one + pltpu.roll(one, bit, 0), zero + pltpu.roll(zero, 8 - bit, 0)) for zero, one in pairs]
    low_res = rows[0]

    mine = spread(place[0:1])
    for b in range(1, BLOCKS):
        mine = jnp.where(group == b, spread(place[2 * b : 2 * b + 1]), mine)
    own_hot = one_hot(mine[0:1])
    corner = mine + STRIDE * (sub_tile // 2 % 2) + sub_tile % 2
    own_lane, own_tile = (corner & 127, corner >> 7)
    greeted = group * every + below + above

    @pl.when(group > 0)
    def _():
        pl.semaphore_wait(barrier, greeted)

    tell(hello.at[jnp.maximum(group - 1, 0)], 0, jnp.minimum(group, 1), [])
    low_parts = parts_of(low_res)
    halves = [lax.dot_general(low_parts, half, (((1,), (1,)), ((), ())), preferred_element_type=jnp.float32) for half in (own_hot[:256], own_hot[256:])]
    own = join_parts(jnp.concatenate(halves, axis=1))
    nodes = gather_sums(own)
    for plane in range(2):
        sums_ref[plane, group, REACH : REACH + 1, :] = nodes[4 * plane : 4 * plane + 1]

    def sides(o):
        return pl.ds(0, 2) if abs(o) < REACH else pl.ds(int(o > 0), 1)

    def sum_copy(z, o):
        return pltpu.make_async_remote_copy(
            src_ref=sums_ref.at[sides(o), group, pl.ds(REACH, 1), :],
            dst_ref=sums_ref.at[sides(o), group, pl.ds(REACH - o, 1), :],
            send_sem=sum_sent,
            recv_sem=sum_recv,
            device_id=(slab + o, z),
            device_id_type=MESH,
        )

    def whole(semaphore, rows_at):
        width = next(w for w in range(1, 9) if rows_at % w == 0 and rows_at // w <= stencil_ref.shape[0])
        view = stencil_ref.at[pl.ds(0, rows_at // width), pl.ds(0, width), :]
        return pltpu.make_async_remote_copy(src_ref=view, dst_ref=view, send_sem=semaphore, recv_sem=semaphore, device_id=(slab, group), device_id_type=MESH)

    def for_each_size(rows_of, act):
        sizes = {}
        for at in range(slabs):
            sizes.setdefault(rows_of(at), []).append(at)
        for total, places in sizes.items():
            here = functools.reduce(jnp.logical_or, [slab == at for at in places])

            @pl.when(here)
            def _():
                act(total)

    def sum_rows(at):
        return 2 * (groups - 1) + sum(groups * (2 if abs(o) < REACH else 1) for o in offsets if 0 <= at + o < slabs)

    def coef_rows(distance):
        return {1: ROWS, 2: ROWS - len(TURNS), 3: 1}[distance]

    def coef_got(at):
        crossing = at + (1 if at % 2 else -1)
        return sum(coef_rows(abs(o)) for o in offsets if 0 <= at + o < slabs and at + o != crossing)

    def coef_gone(at):
        outward = 1 if at % 2 else -1
        direct = [o for o in offsets if 0 <= at + o < slabs and o != 2 * outward]
        return sum(coef_rows(abs(o)) for o in direct) + (coef_rows(2) if 0 <= at + outward < slabs else 0)

    def coef_copy(o, arrived, source=0):
        far = abs(o - source)
        first = {1: 0, 2: 0 if o < source else 4, 3: 4 if o < source else 14}[far]
        count = coef_rows(far)
        return pltpu.make_async_remote_copy(
            src_ref=coef_ref.at[pl.ds(first, count), pl.ds(REACH + source, 1), :],
            dst_ref=coef_ref.at[pl.ds(first, count), pl.ds(REACH + source - o, 1), :],
            send_sem=coef_sent,
            recv_sem=arrived,
            device_id=(slab + o, group),
            device_id_type=MESH,
        )

    def send_sums(z, carry, upward=False):
        for o in sorted([0, *offsets], key=lambda o: (-abs(o), o) if upward else o):

            @pl.when(exists(o))
            def _():
                sum_copy(z, o).start()

        return carry

    lax.fori_loop(0, jnp.minimum(group, 1), send_sums, 0)
    tell(hello.at[jnp.maximum(group - 1, 0)], 1, group, [])
    lax.fori_loop(1, group, send_sums, 0)
    hot = jnp.concatenate([one_hot(place[2 * b : 2 * b + 1]) for b in range(BLOCKS)], axis=1)
    ops = parts_of(ops_ref[...].reshape(64, LINE))
    lex = join_parts(lax.dot_general(ops, hot, (((1,), (1,)), ((), ())), preferred_element_type=jnp.float32))
    moved = [aligned(lex[8 * q : 8 * q + 8]) for q in range(8)]
    sub = rows_of((8, LANES))
    flat, flat_turns, _ = stencil_rows([jnp.where(sub < 4, moved[q], moved[q + 4]) for q in range(4)])
    centre, forward, backward = stencil_rows(moved[4:])
    rows = [(value, row) for value, row in flat_turns] + [flat, centre] + forward + backward
    rows += [(value, row + 4) for value, row in [flat] + flat_turns]
    for at, (value, row) in enumerate(rows):
        coef_ref[at, REACH : REACH + 1, :] = value[row : row + 1]
    even = slab % 2 == 0
    odd = jnp.logical_not(even)
    across = ((jnp.logical_and(even, exists(-1)), -1), (jnp.logical_and(odd, exists(1)), 1))
    @pl.when(jnp.logical_and(group == 0, greeted > 0))
    def _():
        pl.semaphore_wait(barrier, greeted)

    down, up = across
    for here, o, arrived in (
        (*down, cross_recv),
        (jnp.logical_and(odd, exists(-2)), -2, coef_recv),
        (*up, cross_recv),
        (jnp.logical_and(even, exists(2)), 2, coef_recv),
        (odd, -1, coef_recv),
        (even, 1, coef_recv),
        (exists(-3), -3, coef_recv),
        (exists(3), 3, coef_recv),
    ):

        @pl.when(here)
        def _():
            coef_copy(o, arrived).start()

    for o in offsets:

        @pl.when(exists(o))
        def _():
            sum_copy(group, o).start()

    def to_higher(z, carry):
        pl.semaphore_wait(hello.at[z - 1], every)
        return send_sums(z, carry, upward=True)

    lax.fori_loop(group + 1, groups, to_higher, 0)

    fine = []
    for k in range(2):
        column = jnp.full((8, 128), i31_ref[k, 0], jnp.float32)
        for c in range(1, 4):
            column = jnp.where((sub_tile & 3) == c, i31_ref[k, c], column)
        fine.append(column)
    weights = [jnp.where(sub_tile < 4, i31_ref[j, 2 * h], i31_ref[j, 2 * h + 1]) * fine[k] for h in range(2) for j in range(2) for k in range(2)]

    for here, o in across:

        @pl.when(here)
        def _():
            whole(cross_recv, ROWS).wait_recv()
            coef_copy(-o, coef_recv, source=o).start()

    for_each_size(coef_got, lambda total: whole(coef_recv, total).wait_recv())

    turns = len(TURNS)
    up_first = ROWS - turns
    steps = [STRIDE * dy + dx for dy, dx in TURNS]
    stencil_ref[0] = coef_ref[turns] + pltpu.roll(coef_ref[up_first - 1], 1, 0)
    middle = turns + 1
    stencil_ref[1] = pltpu.roll(coef_ref[middle], 1, 0)
    stencil_ref[2] = coef_ref[middle]
    for at, step in enumerate(steps):
        plane = coef_ref[at] + pltpu.roll(coef_ref[up_first + at], 1, 0)
        ahead, back = (coef_ref[middle + 1 + at], coef_ref[middle + 1 + turns + at])
        stencil_ref[3 + 6 * at] = plane
        stencil_ref[4 + 6 * at] = pltpu.roll(ahead, 1, 0)
        stencil_ref[5 + 6 * at] = pltpu.roll(back, LANES - step, 1)
        stencil_ref[6 + 6 * at] = pltpu.roll(plane, step, 1)
        stencil_ref[7 + 6 * at] = pltpu.roll(back, 1, 0)
        stencil_ref[8 + 6 * at] = pltpu.roll(ahead, step, 1)

    def operate(field):
        values = [field] + [pltpu.roll(field, shift, 1) for step in steps for shift in (LANES - step, step)]
        total = []
        for part in (1, 2, 0):
            terms = [stencil_ref[3 * at + part] * value for at, value in enumerate(values)]
            while len(terms) > 1:
                terms = [sum(terms[at : at + 2]) for at in range(0, len(terms), 2)]
            total.append(terms[0])
        return total[2] + pltpu.roll(total[0], 7, 0) + pltpu.roll(total[1], 1, 0)

    diag = stencil_ref[0]
    inverse = 1.0 / jnp.where(diag > 0.0, diag, 1.0)

    for_each_size(sum_rows, lambda total: whole(sum_sent, total).wait_send())
    for_each_size(sum_rows, lambda total: whole(sum_recv, total).wait_recv())

    low, high = [[sums_ref[plane, z] for z in range(groups)] for plane in range(2)]
    while len(low) > 1:
        low, high = [[sum(part[at : at + 2]) for at in range(0, len(part), 2)] for part in (low, high)]
    low, high = (low[0], high[0])
    remain = low + pltpu.roll(high, 1, 0)
    theta = 0.5 * (lam_high + lam_low)
    delta = 0.5 * (lam_high - lam_low)
    sigma = theta / delta
    direction = inverse * remain * (1.0 / theta)
    answer = direction
    rho = 1.0 / sigma
    for sweep in range(SWEEPS):
        remain = remain - operate(direction)
        rho_new = 1.0 / (2.0 * sigma - rho)
        direction = rho_new * rho * direction + 2.0 * rho_new / delta * inverse * remain
        answer = answer + direction
        rho = rho_new

    planes = jnp.where(sub < 4, spread(answer[REACH : REACH + 1]), spread(answer[REACH + 1 : REACH + 2]))
    found = [jnp.take_along_axis(planes[:, 128 * b : 128 * b + 128], own_lane, axis=1) for b in range(LANES // 128)]
    bit = 1
    while len(found) > 1:
        tall = (own_tile & bit) > 0
        found = [jnp.where(tall, two, one) for one, two in zip(found[0::2], found[1::2])] + found[len(found) // 2 * 2 :]
        bit *= 2
    picked = found[0]
    values = [spread(picked[p : p + 1]) for p in range(8)]
    for h in range(2):
        ends = [sum(weights[4 * h + q] * values[4 * i + q] for q in range(4)) for i in range(2)]
        for a in range(4):
            out_ref[8 * (2 * a + h) : 8 * (2 * a + h) + 8, :] = i31_ref[0, a] * ends[0] + i31_ref[1, a] * ends[1]

    for_each_size(coef_gone, lambda total: whole(coef_sent, total).wait_send())


def one_layer(resid7, interp73, interp31, elem_ops, conn):
    slabs, groups = (lax.axis_size("slab"), lax.axis_size("grp"))
    dma = pltpu.SemaphoreType.DMA
    return pl.pallas_call(
        functools.partial(cycle_kernel, slabs, groups),
        out_shape=pltpu.VMEM((64, 128), jnp.float32),
        in_specs=[pl.BlockSpec(memory_space=pl.ANY)] * 5,
        out_specs=VMEM,
        scratch_shapes=[
            pltpu.VMEM((8, LINE), jnp.int32),
            pltpu.VMEM((8, 8, LINE), jnp.float32),
            pltpu.VMEM((512, 128), jnp.float32),
            pltpu.SMEM((4, 8), jnp.float32),
            pltpu.SMEM((2, 4), jnp.float32),
            dma((2,)),
            pltpu.VMEM((2, groups, 8, LANES), jnp.float32),
            pltpu.VMEM((ROWS, 8, LANES), jnp.float32),
            pltpu.VMEM((3 + 6 * len(TURNS), 8, LANES), jnp.float32),
            pltpu.SemaphoreType.REGULAR((groups - 1,)),
            dma,
            dma,
            dma,
            dma,
            dma,
        ],
        compiler_params=pltpu.CompilerParams(collective_id=0, has_side_effects=True),
    )(conn, elem_ops, resid7, interp73.T, interp31.T)


def dispatch(resid7, interp73, interp31, elem_ops, conn, faces):
    if conn.shape[1] == LINE and resid7.shape[1] == 128 and lax.axis_size("grp") > 1 and lax.axis_size("slab") % 2 == 0:
        return one_layer(resid7, interp73, interp31, elem_ops, conn)
    return local(resid7, interp73, interp31, elem_ops, conn, faces)


def solution(mesh):
    in_specs = (
        P(None, ("slab", "grp")),
        P(),
        P(),
        P(None, None, "slab"),
        P(None, "slab"),
        P(None, "slab", None),
    )
    out_specs = P(None, ("slab", "grp"))
    return jax.shard_map(dispatch, mesh=mesh, in_specs=in_specs, out_specs=out_specs, check_vma=False)
```

```python
import functools

import jax
import jax.numpy as jnp
from jax import lax
from jax.experimental import pallas as pl
from jax.experimental.pallas import tpu as pltpu
from jax.sharding import PartitionSpec as P

EX = 32
EY = 16
SWEEPS = 2


lam_low = 0.3
lam_high = 1.9


def extended(array, sides, width):
    for axis, dim in sides:
        count, length = (lax.axis_size(axis), array.shape[dim])
        up = [(i, (i + 1) % count) for i in range(count - 1)]
        down = [(j, i) for i, j in up]
        last = lax.slice_in_dim(array, length - width, length, axis=dim)
        first = lax.slice_in_dim(array, 0, width, axis=dim)
        before = lax.ppermute(last, axis, up)
        after = lax.ppermute(first, axis, down)
        array = jnp.concatenate([before, array, after], axis=dim)
    return array


def restrict_high(block, interp73):
    hi = lax.Precision.HIGHEST
    width = block.shape[1]
    cube = block.reshape(8, 8, 8, width)
    cube = jnp.einsum("kc,ijkm->ijcm", interp73, cube, precision=hi)
    cube = jnp.einsum("jb,ijcm->ibcm", interp73, cube, precision=hi)
    cube = jnp.einsum("ia,ibcm->abcm", interp73, cube, precision=hi)
    return cube.reshape(64, width)


def restrict_low(block, interp31):
    hi = lax.Precision.HIGHEST
    width = block.shape[1]
    cube = block.reshape(4, 4, 4, width)
    cube = jnp.einsum("kc,ijkm->ijcm", interp31, cube, precision=hi)
    cube = jnp.einsum("jb,ijcm->ibcm", interp31, cube, precision=hi)
    cube = jnp.einsum("ia,ibcm->abcm", interp31, cube, precision=hi)
    return cube.reshape(8, width)


def prolong(coarse, interp31):
    hi = lax.Precision.HIGHEST
    width = coarse.shape[1]
    cube = coarse.reshape(2, 2, 2, width)
    cube = jnp.einsum("ck,ijkm->ijcm", interp31, cube, precision=hi)
    cube = jnp.einsum("bj,ijcm->ibcm", interp31, cube, precision=hi)
    cube = jnp.einsum("ai,ibcm->abcm", interp31, cube, precision=hi)
    return cube.reshape(64, width)


def assemble(values, conn_ids, count):
    layers = values.shape[0]
    flat = values.reshape(layers, -1).T
    summed = jax.ops.segment_sum(flat, conn_ids.reshape(-1), num_segments=count)
    return summed.T


def element_term(operators, conn_ids, field):
    return jnp.einsum("pqe,qe->pe", operators, field[conn_ids], precision=lax.Precision.HIGHEST)


def share(nodes, faces):
    lower = faces[0, 0]
    upper = faces[1, 0]
    planes = jnp.stack([nodes[:, lower], nodes[:, upper]], axis=1)
    padded = extended(planes, (("slab", 1),), 1)
    return nodes.at[:, lower].add(padded[:, 0]).at[:, upper].add(padded[:, 3])


def local(resid7, interp73, interp31, elem_ops, conn, faces):
    own = resid7.shape[1]
    slab_elems = conn.shape[1]
    layers = slab_elems // (EX * EY)
    count = (EX + 1) * (EY + 1) * (layers + 1)
    start = lax.axis_index("grp") * own
    own_conn = lax.dynamic_slice_in_dim(conn, start, own, 1)
    middle_res = restrict_high(resid7, interp73)
    blocks = lax.all_gather(middle_res, "grp", axis=1, tiled=True)
    slab_res = restrict_low(blocks, interp31)
    pair = jnp.stack([slab_res, jnp.einsum("ppe->pe", elem_ops)])
    both_nodes = assemble(pair, conn, count)
    shared = share(both_nodes, faces)
    rhs = shared[0]
    diag = shared[1]
    theta = 0.5 * (lam_high + lam_low)
    delta = 0.5 * (lam_high - lam_low)
    sigma = theta / delta
    inverse = 1.0 / diag
    direction = inverse * rhs / theta
    solution = direction
    remain = rhs
    rho = 1.0 / sigma
    for sweep in range(SWEEPS):
        nodes = assemble(element_term(elem_ops, conn, direction)[None], conn, count)
        remain = remain - share(nodes, faces)[0]
        rho_new = 1.0 / (2.0 * sigma - rho)
        direction = rho_new * rho * direction + 2.0 * rho_new / delta * inverse * remain
        solution = solution + direction
        rho = rho_new
    return prolong(solution[own_conn], interp31)


STRIDE = EX + 1
POINTS = (EX + 1) * (EY + 1)
LANES = (POINTS + 127) // 128 * 128
LINE = EX * EY
BLOCKS = LINE // 128
REACH = SWEEPS + 1
TURNS = ((0, 1), (1, -1), (1, 0), (1, 1))
ROWS = 2 * (len(TURNS) + 1) + 2 * len(TURNS) + 1
MESH = pl.DeviceIdType.MESH
VMEM = pl.BlockSpec(memory_space=pltpu.VMEM)
SMEM = pl.BlockSpec(memory_space=pltpu.SMEM)


def rows_of(shape):
    return lax.broadcasted_iota(jnp.int32, shape, 0)


def spread(row, count=8):
    return jnp.broadcast_to(row, (count, row.shape[1]))


def stack_rows(rows):
    sub = rows_of((8, rows[0].shape[1]))
    out = spread(rows[0])
    for at in range(1, 8):
        out = jnp.where(sub == at, spread(rows[at]), out)
    return out


def parts_of(value):
    hi = value.astype(jnp.bfloat16).astype(jnp.float32)
    left = value - hi
    mid = left.astype(jnp.bfloat16).astype(jnp.float32)
    return jnp.concatenate([hi, mid, left - mid], axis=0).astype(jnp.bfloat16)


def join_parts(value):
    third = value.shape[0] // 3
    return value[:third] + value[third : 2 * third] + value[2 * third :]


def aligned(value):
    sub = rows_of(value.shape)
    odd, second = ((sub & 1) == 1, (sub & 2) == 2)
    near = jnp.where(odd, pltpu.roll(value, 1, 1), value)
    far = jnp.where(odd, pltpu.roll(value, STRIDE + 1, 1), pltpu.roll(value, STRIDE, 1))
    return jnp.where(second, far, near)


def gather_sums(corners):
    part = aligned(corners)
    part = part + pltpu.roll(part, 7, 0)
    return part + pltpu.roll(part, 6, 0)


def stencil_rows(columns):
    sub = rows_of(columns[0].shape)
    odd, second = ((sub & 1) == 1, (sub & 2) == 2)

    def over_x(part):
        return part + jnp.where(odd, pltpu.roll(part, 1, 0), pltpu.roll(part, 7, 0))

    def over_y(part):
        return part + jnp.where(second, pltpu.roll(part, 2, 0), pltpu.roll(part, 6, 0))

    c0, c1, c2, c3 = columns
    centre = over_y(over_x(jnp.where(second, jnp.where(odd, c3, c2), jnp.where(odd, c1, c0))))
    along_x = over_y(jnp.where(second, jnp.where(odd, c2, c3), jnp.where(odd, c0, c1)))
    along_y = over_x(jnp.where(second, jnp.where(odd, c1, c0), jnp.where(odd, c3, c2)))
    forward = [(along_x, 0), (c2, 1), (along_y, 0), (c3, 0)]
    backward = [(along_x, 1), (c1, 2), (along_y, 2), (c0, 3)]
    return (centre, 0), forward, backward


def coded(number):
    return (128 + (number & 127)) * jnp.left_shift(1, number >> 7)


def before(ids, mine, theirs):
    column = jnp.broadcast_to(ids[theirs : theirs + 1], (128, LINE)).T.astype(jnp.bfloat16)
    row = spread(ids[mine : mine + 1], 16).astype(jnp.bfloat16)
    place = rows_of((16, 128))
    total = jnp.zeros((16, LINE), jnp.bfloat16)
    for at in range(LINE // 16):
        one = column[16 * at : 16 * at + 16]
        same = jnp.concatenate([one] * BLOCKS, axis=1) == row
        value = (place * (1 << (at >> 3)) + ((128 + (16 * at & 127)) << (at >> 3))).astype(jnp.float32).astype(jnp.bfloat16)
        total = jnp.where(same, jnp.concatenate([value] * BLOCKS, axis=1), total)
    return jnp.sum(total.astype(jnp.float32), axis=0, keepdims=True)


def links(conn):
    ids = coded(conn).astype(jnp.float32)
    own = lax.broadcasted_iota(jnp.int32, (1, LINE), 1)
    rows = []
    for theirs in (1, 2):
        code = before(ids, 0, theirs).astype(jnp.int32)
        power = sum((code >= 256 << k).astype(jnp.int32) for k in range((LINE - 1) >> 7))
        found = (code >> power) - 128 + 128 * power
        packed = jnp.where(code > 0, found + LINE, own)
        rows += [packed[:, 128 * b : 128 * b + 128] for b in range(BLOCKS)]
    return stack_rows([row for pair in zip(rows[:BLOCKS], rows[BLOCKS:]) for row in pair])


def positions(state):
    block = rows_of((8, 128)) >> 1
    for _ in range((EX - 1).bit_length()):
        target = state & (LINE - 1)
        away = ((target >> 7) - block) & (BLOCKS - 1)
        found = [jnp.take_along_axis(pltpu.roll(state, 8 - 2 * k, 0) if k else state, target & 127, axis=1) for k in range(BLOCKS)]
        bit = 1
        while len(found) > 1:
            high = (away & bit) > 0
            found = [jnp.where(high, two, one) for one, two in zip(found[0::2], found[1::2])]
            bit *= 2
        state = found[0] + (state - target)
    steps = state >> (LINE.bit_length() - 1)
    return steps + STRIDE * pltpu.roll(steps, 7, 0)


def one_hot(row):
    return jnp.where(rows_of((LANES, row.shape[1])) == spread(row, LANES), 1.0, 0.0).astype(jnp.bfloat16)


def cycle_kernel(slabs, groups, conn_hbm, ops_hbm, res_hbm, i73_hbm, i31_hbm, out_ref, conn_ref, ops_ref, res_ref, i73_ref, i31_ref, load_sem, sums_ref, coef_ref, stencil_ref, hello, sum_sent, coef_sent, sum_recv, coef_recv, cross_recv):
    slab, group = (lax.axis_index("slab"), lax.axis_index("grp"))
    offsets = [o for o in range(-REACH, REACH + 1) if o != 0]
    below, above = (jnp.minimum(slab, REACH), jnp.minimum(slabs - 1 - slab, REACH))
    every = below + above + 1

    def exists(o):
        return slab >= -o if o < 0 else slab < slabs - o

    loads = [
        pltpu.make_async_copy(source, target, (sum_sent, coef_sent, load_sem.at[0], load_sem.at[1], load_sem.at[1])[at])
        for at, (source, target) in enumerate(((i73_hbm, i73_ref), (i31_hbm, i31_ref), (conn_hbm, conn_ref), (res_hbm, res_ref), (ops_hbm, ops_ref)))
    ]
    for load in loads:
        load.start()
    sums_ref[...] = jnp.zeros(sums_ref.shape, jnp.float32)
    coef_ref[...] = jnp.zeros(coef_ref.shape, jnp.float32)

    def tell(semaphore, first, last, some):
        def visit(z, carry):
            pl.semaphore_signal(semaphore, inc=1, device_id=(slab, z), device_id_type=MESH)
            for o in offsets:

                @pl.when(exists(o))
                def _():
                    pl.semaphore_signal(semaphore, inc=1, device_id=(slab + o, z), device_id_type=MESH)

            return carry

        lax.fori_loop(first, last, visit, 0)
        for o in some:

            @pl.when(exists(o))
            def _():
                pl.semaphore_signal(semaphore, inc=1, device_id=(slab + o, group), device_id_type=MESH)

    barrier = pltpu.get_barrier_semaphore()
    tell(barrier, group + 1, groups, offsets)

    for load in loads[:3]:
        load.wait()
    coef = [[sum(i73_ref[m, i] * i31_ref[a, m] for m in range(4)) for a in range(2)] for i in range(8)]
    state = links(conn_ref[...])
    both = stencil_ref.at[pl.ds(0, 24), :, pl.ds(0, LINE)]
    pltpu.make_async_copy(both, both, load_sem.at[1]).wait()
    place = positions(state)
    along_j = [[None] * 8, [None] * 8]
    for j in range(8):
        for a in range(2):
            along_j[a][j] = sum(coef[i][a] * res_ref[64 * i + 8 * j : 64 * i + 8 * j + 8, :] for i in range(8))
    sub_tile = rows_of((8, 128))
    last = []
    for c in range(2):
        column = jnp.full((8, 128), coef[0][c], jnp.float32)
        for k in range(1, 8):
            column = jnp.where(sub_tile == k, coef[k][c], column)
        last.append(column)
    rows = []
    for a in range(2):
        for b in range(2):
            line = sum(coef[j][b] * along_j[a][j] for j in range(8))
            for c in range(2):
                rows.append(last[c] * line)
    for bit in (1, 2, 4):
        high = (sub_tile & bit) > 0
        pairs = zip(rows[0::2], rows[1::2])
        rows = [jnp.where(high, one + pltpu.roll(one, bit, 0), zero + pltpu.roll(zero, 8 - bit, 0)) for zero, one in pairs]
    low_res = rows[0]

    mine = spread(place[0:1])
    for b in range(1, BLOCKS):
        mine = jnp.where(group == b, spread(place[2 * b : 2 * b + 1]), mine)
    own_hot = one_hot(mine[0:1])
    corner = mine + STRIDE * (sub_tile // 2 % 2) + sub_tile % 2
    own_lane, own_tile = (corner & 127, corner >> 7)
    greeted = group * every + below + above

    @pl.when(group > 0)
    def _():
        pl.semaphore_wait(barrier, greeted)

    tell(hello.at[jnp.maximum(group - 1, 0)], 0, jnp.minimum(group, 1), [])
    low_parts = parts_of(low_res)
    halves = [lax.dot_general(low_parts, half, (((1,), (1,)), ((), ())), preferred_element_type=jnp.float32) for half in (own_hot[:256], own_hot[256:])]
    own = join_parts(jnp.concatenate(halves, axis=1))
    nodes = gather_sums(own)
    for plane in range(2):
        sums_ref[plane, group, REACH : REACH + 1, :] = nodes[4 * plane : 4 * plane + 1]

    def sides(o):
        return pl.ds(0, 2) if abs(o) < REACH else pl.ds(int(o > 0), 1)

    def sum_copy(z, o):
        return pltpu.make_async_remote_copy(
            src_ref=sums_ref.at[sides(o), group, pl.ds(REACH, 1), :],
            dst_ref=sums_ref.at[sides(o), group, pl.ds(REACH - o, 1), :],
            send_sem=sum_sent,
            recv_sem=sum_recv,
            device_id=(slab + o, z),
            device_id_type=MESH,
        )

    def whole(semaphore, rows_at):
        width = next(w for w in range(1, 9) if rows_at % w == 0 and rows_at // w <= stencil_ref.shape[0])
        view = stencil_ref.at[pl.ds(0, rows_at // width), pl.ds(0, width), :]
        return pltpu.make_async_remote_copy(src_ref=view, dst_ref=view, send_sem=semaphore, recv_sem=semaphore, device_id=(slab, group), device_id_type=MESH)

    def for_each_size(rows_of, act):
        sizes = {}
        for at in range(slabs):
            sizes.setdefault(rows_of(at), []).append(at)
        for total, places in sizes.items():
            here = functools.reduce(jnp.logical_or, [slab == at for at in places])

            @pl.when(here)
            def _():
                act(total)

    def sum_rows(at):
        return 2 * (groups - 1) + sum(groups * (2 if abs(o) < REACH else 1) for o in offsets if 0 <= at + o < slabs)

    def coef_rows(distance):
        return {1: ROWS, 2: ROWS - len(TURNS), 3: 1}[distance]

    def coef_got(at):
        crossing = at + (1 if at % 2 else -1)
        return sum(coef_rows(abs(o)) for o in offsets if 0 <= at + o < slabs and at + o != crossing)

    def coef_gone(at):
        outward = 1 if at % 2 else -1
        direct = [o for o in offsets if 0 <= at + o < slabs and o != 2 * outward]
        return sum(coef_rows(abs(o)) for o in direct) + (coef_rows(2) if 0 <= at + outward < slabs else 0)

    def coef_copy(o, arrived, source=0):
        far = abs(o - source)
        first = {1: 0, 2: 0 if o < source else 4, 3: 4 if o < source else 14}[far]
        count = coef_rows(far)
        return pltpu.make_async_remote_copy(
            src_ref=coef_ref.at[pl.ds(first, count), pl.ds(REACH + source, 1), :],
            dst_ref=coef_ref.at[pl.ds(first, count), pl.ds(REACH + source - o, 1), :],
            send_sem=coef_sent,
            recv_sem=arrived,
            device_id=(slab + o, group),
            device_id_type=MESH,
        )

    def send_sums(z, carry, upward=False):
        for o in sorted([0, *offsets], key=lambda o: (-abs(o), o) if upward else o):

            @pl.when(exists(o))
            def _():
                sum_copy(z, o).start()

        return carry

    lax.fori_loop(0, jnp.minimum(group, 1), send_sums, 0)
    tell(hello.at[jnp.maximum(group - 1, 0)], 1, group, [])
    hot = jnp.concatenate([one_hot(place[2 * b : 2 * b + 1]) for b in range(BLOCKS)], axis=1)
    ops = parts_of(ops_ref[...].reshape(64, LINE))
    lex = join_parts(lax.dot_general(ops, hot, (((1,), (1,)), ((), ())), preferred_element_type=jnp.float32))
    moved = [aligned(lex[8 * q : 8 * q + 8]) for q in range(8)]
    sub = rows_of((8, LANES))
    flat, flat_turns, _ = stencil_rows([jnp.where(sub < 4, moved[q], moved[q + 4]) for q in range(4)])
    centre, forward, backward = stencil_rows(moved[4:])
    rows = [(value, row) for value, row in flat_turns] + [flat, centre] + forward + backward
    rows += [(value, row + 4) for value, row in [flat] + flat_turns]
    for at, (value, row) in enumerate(rows):
        coef_ref[at, REACH : REACH + 1, :] = value[row : row + 1]
    even = slab % 2 == 0
    odd = jnp.logical_not(even)
    across = ((jnp.logical_and(even, exists(-1)), -1), (jnp.logical_and(odd, exists(1)), 1))
    @pl.when(jnp.logical_and(group == 0, greeted > 0))
    def _():
        pl.semaphore_wait(barrier, greeted)

    down, up = across
    for here, o, arrived in (
        (*down, cross_recv),
        (jnp.logical_and(odd, exists(-2)), -2, coef_recv),
        (*up, cross_recv),
        (jnp.logical_and(even, exists(2)), 2, coef_recv),
        (odd, -1, coef_recv),
        (even, 1, coef_recv),
        (exists(-3), -3, coef_recv),
        (exists(3), 3, coef_recv),
    ):

        @pl.when(here)
        def _():
            coef_copy(o, arrived).start()

    for o in offsets:

        @pl.when(exists(o))
        def _():
            sum_copy(group, o).start()

    lax.fori_loop(1, group, send_sums, 0)

    def to_higher(z, carry):
        pl.semaphore_wait(hello.at[z - 1], every)
        return send_sums(z, carry, upward=True)

    lax.fori_loop(group + 1, groups, to_higher, 0)

    fine = []
    for k in range(2):
        column = jnp.full((8, 128), i31_ref[k, 0], jnp.float32)
        for c in range(1, 4):
            column = jnp.where((sub_tile & 3) == c, i31_ref[k, c], column)
        fine.append(column)
    weights = [jnp.where(sub_tile < 4, i31_ref[j, 2 * h], i31_ref[j, 2 * h + 1]) * fine[k] for h in range(2) for j in range(2) for k in range(2)]

    for here, o in across:

        @pl.when(here)
        def _():
            whole(cross_recv, ROWS).wait_recv()
            coef_copy(-o, coef_recv, source=o).start()

    for_each_size(coef_got, lambda total: whole(coef_recv, total).wait_recv())

    turns = len(TURNS)
    up_first = ROWS - turns
    steps = [STRIDE * dy + dx for dy, dx in TURNS]
    stencil_ref[0] = coef_ref[turns] + pltpu.roll(coef_ref[up_first - 1], 1, 0)
    middle = turns + 1
    stencil_ref[1] = pltpu.roll(coef_ref[middle], 1, 0)
    stencil_ref[2] = coef_ref[middle]
    for at, step in enumerate(steps):
        plane = coef_ref[at] + pltpu.roll(coef_ref[up_first + at], 1, 0)
        ahead, back = (coef_ref[middle + 1 + at], coef_ref[middle + 1 + turns + at])
        stencil_ref[3 + 6 * at] = plane
        stencil_ref[4 + 6 * at] = pltpu.roll(ahead, 1, 0)
        stencil_ref[5 + 6 * at] = pltpu.roll(back, LANES - step, 1)
        stencil_ref[6 + 6 * at] = pltpu.roll(plane, step, 1)
        stencil_ref[7 + 6 * at] = pltpu.roll(back, 1, 0)
        stencil_ref[8 + 6 * at] = pltpu.roll(ahead, step, 1)

    def operate(field):
        values = [field] + [pltpu.roll(field, shift, 1) for step in steps for shift in (LANES - step, step)]
        total = []
        for part in (1, 2, 0):
            terms = [stencil_ref[3 * at + part] * value for at, value in enumerate(values)]
            while len(terms) > 1:
                terms = [sum(terms[at : at + 2]) for at in range(0, len(terms), 2)]
            total.append(terms[0])
        return total[2] + pltpu.roll(total[0], 7, 0) + pltpu.roll(total[1], 1, 0)

    diag = stencil_ref[0]
    inverse = 1.0 / jnp.where(diag > 0.0, diag, 1.0)

    for_each_size(sum_rows, lambda total: whole(sum_sent, total).wait_send())
    for_each_size(sum_rows, lambda total: whole(sum_recv, total).wait_recv())

    low, high = [[sums_ref[plane, z] for z in range(groups)] for plane in range(2)]
    while len(low) > 1:
        low, high = [[sum(part[at : at + 2]) for at in range(0, len(part), 2)] for part in (low, high)]
    low, high = (low[0], high[0])
    remain = low + pltpu.roll(high, 1, 0)
    theta = 0.5 * (lam_high + lam_low)
    delta = 0.5 * (lam_high - lam_low)
    sigma = theta / delta
    direction = inverse * remain * (1.0 / theta)
    answer = direction
    rho = 1.0 / sigma
    for sweep in range(SWEEPS):
        remain = remain - operate(direction)
        rho_new = 1.0 / (2.0 * sigma - rho)
        direction = rho_new * rho * direction + 2.0 * rho_new / delta * inverse * remain
        answer = answer + direction
        rho = rho_new

    planes = jnp.where(sub < 4, spread(answer[REACH : REACH + 1]), spread(answer[REACH + 1 : REACH + 2]))
    found = [jnp.take_along_axis(planes[:, 128 * b : 128 * b + 128], own_lane, axis=1) for b in range(LANES // 128)]
    bit = 1
    while len(found) > 1:
        tall = (own_tile & bit) > 0
        found = [jnp.where(tall, two, one) for one, two in zip(found[0::2], found[1::2])] + found[len(found) // 2 * 2 :]
        bit *= 2
    picked = found[0]
    values = [spread(picked[p : p + 1]) for p in range(8)]
    for h in range(2):
        ends = [sum(weights[4 * h + q] * values[4 * i + q] for q in range(4)) for i in range(2)]
        for a in range(4):
            out_ref[8 * (2 * a + h) : 8 * (2 * a + h) + 8, :] = i31_ref[0, a] * ends[0] + i31_ref[1, a] * ends[1]

    for_each_size(coef_gone, lambda total: whole(coef_sent, total).wait_send())


def one_layer(resid7, interp73, interp31, elem_ops, conn):
    slabs, groups = (lax.axis_size("slab"), lax.axis_size("grp"))
    dma = pltpu.SemaphoreType.DMA
    return pl.pallas_call(
        functools.partial(cycle_kernel, slabs, groups),
        out_shape=pltpu.VMEM((64, 128), jnp.float32),
        in_specs=[pl.BlockSpec(memory_space=pl.ANY)] * 5,
        out_specs=VMEM,
        scratch_shapes=[
            pltpu.VMEM((8, LINE), jnp.int32),
            pltpu.VMEM((8, 8, LINE), jnp.float32),
            pltpu.VMEM((512, 128), jnp.float32),
            pltpu.SMEM((4, 8), jnp.float32),
            pltpu.SMEM((2, 4), jnp.float32),
            dma((2,)),
            pltpu.VMEM((2, groups, 8, LANES), jnp.float32),
            pltpu.VMEM((ROWS, 8, LANES), jnp.float32),
            pltpu.VMEM((3 + 6 * len(TURNS), 8, LANES), jnp.float32),
            pltpu.SemaphoreType.REGULAR((groups - 1,)),
            dma,
            dma,
            dma,
            dma,
            dma,
        ],
        compiler_params=pltpu.CompilerParams(collective_id=0, has_side_effects=True),
    )(conn, elem_ops, resid7, interp73.T, interp31.T)


def dispatch(resid7, interp73, interp31, elem_ops, conn, faces):
    if conn.shape[1] == LINE and resid7.shape[1] == 128 and lax.axis_size("grp") > 1 and lax.axis_size("slab") % 2 == 0:
        return one_layer(resid7, interp73, interp31, elem_ops, conn)
    return local(resid7, interp73, interp31, elem_ops, conn, faces)


def solution(mesh):
    in_specs = (
        P(None, ("slab", "grp")),
        P(),
        P(),
        P(None, None, "slab"),
        P(None, "slab"),
        P(None, "slab", None),
    )
    out_specs = P(None, ("slab", "grp"))
    return jax.shard_map(dispatch, mesh=mesh, in_specs=in_specs, out_specs=out_specs, check_vma=False)
```

```python
import functools

import jax
import jax.numpy as jnp
from jax import lax
from jax.experimental import pallas as pl
from jax.experimental.pallas import tpu as pltpu
from jax.sharding import PartitionSpec as P

EX = 32
EY = 16
SWEEPS = 2


lam_low = 0.3
lam_high = 1.9


def extended(array, sides, width):
    for axis, dim in sides:
        count, length = (lax.axis_size(axis), array.shape[dim])
        up = [(i, (i + 1) % count) for i in range(count - 1)]
        down = [(j, i) for i, j in up]
        last = lax.slice_in_dim(array, length - width, length, axis=dim)
        first = lax.slice_in_dim(array, 0, width, axis=dim)
        before = lax.ppermute(last, axis, up)
        after = lax.ppermute(first, axis, down)
        array = jnp.concatenate([before, array, after], axis=dim)
    return array


def restrict_high(block, interp73):
    hi = lax.Precision.HIGHEST
    width = block.shape[1]
    cube = block.reshape(8, 8, 8, width)
    cube = jnp.einsum("kc,ijkm->ijcm", interp73, cube, precision=hi)
    cube = jnp.einsum("jb,ijcm->ibcm", interp73, cube, precision=hi)
    cube = jnp.einsum("ia,ibcm->abcm", interp73, cube, precision=hi)
    return cube.reshape(64, width)


def restrict_low(block, interp31):
    hi = lax.Precision.HIGHEST
    width = block.shape[1]
    cube = block.reshape(4, 4, 4, width)
    cube = jnp.einsum("kc,ijkm->ijcm", interp31, cube, precision=hi)
    cube = jnp.einsum("jb,ijcm->ibcm", interp31, cube, precision=hi)
    cube = jnp.einsum("ia,ibcm->abcm", interp31, cube, precision=hi)
    return cube.reshape(8, width)


def prolong(coarse, interp31):
    hi = lax.Precision.HIGHEST
    width = coarse.shape[1]
    cube = coarse.reshape(2, 2, 2, width)
    cube = jnp.einsum("ck,ijkm->ijcm", interp31, cube, precision=hi)
    cube = jnp.einsum("bj,ijcm->ibcm", interp31, cube, precision=hi)
    cube = jnp.einsum("ai,ibcm->abcm", interp31, cube, precision=hi)
    return cube.reshape(64, width)


def assemble(values, conn_ids, count):
    layers = values.shape[0]
    flat = values.reshape(layers, -1).T
    summed = jax.ops.segment_sum(flat, conn_ids.reshape(-1), num_segments=count)
    return summed.T


def element_term(operators, conn_ids, field):
    return jnp.einsum("pqe,qe->pe", operators, field[conn_ids], precision=lax.Precision.HIGHEST)


def share(nodes, faces):
    lower = faces[0, 0]
    upper = faces[1, 0]
    planes = jnp.stack([nodes[:, lower], nodes[:, upper]], axis=1)
    padded = extended(planes, (("slab", 1),), 1)
    return nodes.at[:, lower].add(padded[:, 0]).at[:, upper].add(padded[:, 3])


def local(resid7, interp73, interp31, elem_ops, conn, faces):
    own = resid7.shape[1]
    slab_elems = conn.shape[1]
    layers = slab_elems // (EX * EY)
    count = (EX + 1) * (EY + 1) * (layers + 1)
    start = lax.axis_index("grp") * own
    own_conn = lax.dynamic_slice_in_dim(conn, start, own, 1)
    middle_res = restrict_high(resid7, interp73)
    blocks = lax.all_gather(middle_res, "grp", axis=1, tiled=True)
    slab_res = restrict_low(blocks, interp31)
    pair = jnp.stack([slab_res, jnp.einsum("ppe->pe", elem_ops)])
    both_nodes = assemble(pair, conn, count)
    shared = share(both_nodes, faces)
    rhs = shared[0]
    diag = shared[1]
    theta = 0.5 * (lam_high + lam_low)
    delta = 0.5 * (lam_high - lam_low)
    sigma = theta / delta
    inverse = 1.0 / diag
    direction = inverse * rhs / theta
    solution = direction
    remain = rhs
    rho = 1.0 / sigma
    for sweep in range(SWEEPS):
        nodes = assemble(element_term(elem_ops, conn, direction)[None], conn, count)
        remain = remain - share(nodes, faces)[0]
        rho_new = 1.0 / (2.0 * sigma - rho)
        direction = rho_new * rho * direction + 2.0 * rho_new / delta * inverse * remain
        solution = solution + direction
        rho = rho_new
    return prolong(solution[own_conn], interp31)


STRIDE = EX + 1
POINTS = (EX + 1) * (EY + 1)
LANES = (POINTS + 127) // 128 * 128
LINE = EX * EY
BLOCKS = LINE // 128
REACH = SWEEPS + 1
TURNS = ((0, 1), (1, -1), (1, 0), (1, 1))
ROWS = 2 * (len(TURNS) + 1) + 2 * len(TURNS) + 1
MESH = pl.DeviceIdType.MESH
VMEM = pl.BlockSpec(memory_space=pltpu.VMEM)
SMEM = pl.BlockSpec(memory_space=pltpu.SMEM)


def rows_of(shape):
    return lax.broadcasted_iota(jnp.int32, shape, 0)


def spread(row, count=8):
    return jnp.broadcast_to(row, (count, row.shape[1]))


def stack_rows(rows):
    sub = rows_of((8, rows[0].shape[1]))
    out = spread(rows[0])
    for at in range(1, 8):
        out = jnp.where(sub == at, spread(rows[at]), out)
    return out


def parts_of(value):
    hi = value.astype(jnp.bfloat16).astype(jnp.float32)
    left = value - hi
    mid = left.astype(jnp.bfloat16).astype(jnp.float32)
    return jnp.concatenate([hi, mid, left - mid], axis=0).astype(jnp.bfloat16)


def join_parts(value):
    third = value.shape[0] // 3
    return value[:third] + value[third : 2 * third] + value[2 * third :]


def aligned(value):
    sub = rows_of(value.shape)
    odd, second = ((sub & 1) == 1, (sub & 2) == 2)
    near = jnp.where(odd, pltpu.roll(value, 1, 1), value)
    far = jnp.where(odd, pltpu.roll(value, STRIDE + 1, 1), pltpu.roll(value, STRIDE, 1))
    return jnp.where(second, far, near)


def gather_sums(corners):
    part = aligned(corners)
    part = part + pltpu.roll(part, 7, 0)
    return part + pltpu.roll(part, 6, 0)


def stencil_rows(columns):
    sub = rows_of(columns[0].shape)
    odd, second = ((sub & 1) == 1, (sub & 2) == 2)

    def over_x(part):
        return part + jnp.where(odd, pltpu.roll(part, 1, 0), pltpu.roll(part, 7, 0))

    def over_y(part):
        return part + jnp.where(second, pltpu.roll(part, 2, 0), pltpu.roll(part, 6, 0))

    c0, c1, c2, c3 = columns
    centre = over_y(over_x(jnp.where(second, jnp.where(odd, c3, c2), jnp.where(odd, c1, c0))))
    along_x = over_y(jnp.where(second, jnp.where(odd, c2, c3), jnp.where(odd, c0, c1)))
    along_y = over_x(jnp.where(second, jnp.where(odd, c1, c0), jnp.where(odd, c3, c2)))
    forward = [(along_x, 0), (c2, 1), (along_y, 0), (c3, 0)]
    backward = [(along_x, 1), (c1, 2), (along_y, 2), (c0, 3)]
    return (centre, 0), forward, backward


def coded(number):
    return (128 + (number & 127)) * jnp.left_shift(1, number >> 7)


def before(ids, mine, theirs):
    column = jnp.broadcast_to(ids[theirs : theirs + 1], (128, LINE)).T.astype(jnp.bfloat16)
    row = spread(ids[mine : mine + 1], 16).astype(jnp.bfloat16)
    place = rows_of((16, 128))
    total = jnp.zeros((16, LINE), jnp.bfloat16)
    for at in range(LINE // 16):
        one = column[16 * at : 16 * at + 16]
        same = jnp.concatenate([one] * BLOCKS, axis=1) == row
        value = (place * (1 << (at >> 3)) + ((128 + (16 * at & 127)) << (at >> 3))).astype(jnp.float32).astype(jnp.bfloat16)
        total = jnp.where(same, jnp.concatenate([value] * BLOCKS, axis=1), total)
    return jnp.sum(total.astype(jnp.float32), axis=0, keepdims=True)


def links(conn):
    ids = coded(conn).astype(jnp.float32)
    own = lax.broadcasted_iota(jnp.int32, (1, LINE), 1)
    rows = []
    for theirs in (1, 2):
        code = before(ids, 0, theirs).astype(jnp.int32)
        power = sum((code >= 256 << k).astype(jnp.int32) for k in range((LINE - 1) >> 7))
        found = (code >> power) - 128 + 128 * power
        packed = jnp.where(code > 0, found + LINE, own)
        rows += [packed[:, 128 * b : 128 * b + 128] for b in range(BLOCKS)]
    return stack_rows([row for pair in zip(rows[:BLOCKS], rows[BLOCKS:]) for row in pair])


def positions(state):
    block = rows_of((8, 128)) >> 1
    for _ in range((EX - 1).bit_length()):
        target = state & (LINE - 1)
        away = ((target >> 7) - block) & (BLOCKS - 1)
        found = [jnp.take_along_axis(pltpu.roll(state, 8 - 2 * k, 0) if k else state, target & 127, axis=1) for k in range(BLOCKS)]
        bit = 1
        while len(found) > 1:
            high = (away & bit) > 0
            found = [jnp.where(high, two, one) for one, two in zip(found[0::2], found[1::2])]
            bit *= 2
        state = found[0] + (state - target)
    steps = state >> (LINE.bit_length() - 1)
    return steps + STRIDE * pltpu.roll(steps, 7, 0)


def one_hot(row):
    return jnp.where(rows_of((LANES, row.shape[1])) == spread(row, LANES), 1.0, 0.0).astype(jnp.bfloat16)


def cycle_kernel(slabs, groups, conn_hbm, ops_hbm, res_hbm, i73_hbm, i31_hbm, out_ref, conn_ref, ops_ref, res_ref, i73_ref, i31_ref, load_sem, sums_ref, coef_ref, stencil_ref, hello, sum_sent, coef_sent, sum_recv, coef_recv, cross_recv):
    slab, group = (lax.axis_index("slab"), lax.axis_index("grp"))
    offsets = [o for o in range(-REACH, REACH + 1) if o != 0]
    below, above = (jnp.minimum(slab, REACH), jnp.minimum(slabs - 1 - slab, REACH))
    every = below + above + 1

    def exists(o):
        return slab >= -o if o < 0 else slab < slabs - o

    loads = [
        pltpu.make_async_copy(source, target, (sum_sent, coef_sent, load_sem.at[0], load_sem.at[1], load_sem.at[1])[at])
        for at, (source, target) in enumerate(((i73_hbm, i73_ref), (i31_hbm, i31_ref), (conn_hbm, conn_ref), (res_hbm, res_ref), (ops_hbm, ops_ref)))
    ]
    for load in loads:
        load.start()
    sums_ref[...] = jnp.zeros(sums_ref.shape, jnp.float32)
    coef_ref[...] = jnp.zeros(coef_ref.shape, jnp.float32)

    def tell(semaphore, first, last, some):
        def visit(z, carry):
            pl.semaphore_signal(semaphore, inc=1, device_id=(slab, z), device_id_type=MESH)
            for o in offsets:

                @pl.when(exists(o))
                def _():
                    pl.semaphore_signal(semaphore, inc=1, device_id=(slab + o, z), device_id_type=MESH)

            return carry

        lax.fori_loop(first, last, visit, 0)
        for o in some:

            @pl.when(exists(o))
            def _():
                pl.semaphore_signal(semaphore, inc=1, device_id=(slab + o, group), device_id_type=MESH)

    barrier = pltpu.get_barrier_semaphore()
    tell(barrier, group + 1, groups, offsets)

    for load in loads[:3]:
        load.wait()
    coef = [[sum(i73_ref[m, i] * i31_ref[a, m] for m in range(4)) for a in range(2)] for i in range(8)]
    state = links(conn_ref[...])
    both = stencil_ref.at[pl.ds(0, 24), :, pl.ds(0, LINE)]
    pltpu.make_async_copy(both, both, load_sem.at[1]).wait()
    place = positions(state)
    along_j = [[None] * 8, [None] * 8]
    for j in range(8):
        for a in range(2):
            along_j[a][j] = sum(coef[i][a] * res_ref[64 * i + 8 * j : 64 * i + 8 * j + 8, :] for i in range(8))
    sub_tile = rows_of((8, 128))
    last = []
    for c in range(2):
        column = jnp.full((8, 128), coef[0][c], jnp.float32)
        for k in range(1, 8):
            column = jnp.where(sub_tile == k, coef[k][c], column)
        last.append(column)
    rows = []
    for a in range(2):
        for b in range(2):
            line = sum(coef[j][b] * along_j[a][j] for j in range(8))
            for c in range(2):
                rows.append(last[c] * line)
    for bit in (1, 2, 4):
        high = (sub_tile & bit) > 0
        pairs = zip(rows[0::2], rows[1::2])
        rows = [jnp.where(high, one + pltpu.roll(one, bit, 0), zero + pltpu.roll(zero, 8 - bit, 0)) for zero, one in pairs]
    low_res = rows[0]

    mine = spread(place[0:1])
    for b in range(1, BLOCKS):
        mine = jnp.where(group == b, spread(place[2 * b : 2 * b + 1]), mine)
    own_hot = one_hot(mine[0:1])
    corner = mine + STRIDE * (sub_tile // 2 % 2) + sub_tile % 2
    own_lane, own_tile = (corner & 127, corner >> 7)
    greeted = group * every + below + above

    @pl.when(group > 0)
    def _():
        pl.semaphore_wait(barrier, greeted)

    tell(hello.at[jnp.maximum(group - 1, 0)], 0, jnp.minimum(group, 1), [])
    low_parts = parts_of(low_res)
    halves = [lax.dot_general(low_parts, half, (((1,), (1,)), ((), ())), preferred_element_type=jnp.float32) for half in (own_hot[:256], own_hot[256:])]
    own = join_parts(jnp.concatenate(halves, axis=1))
    nodes = gather_sums(own)
    for plane in range(2):
        sums_ref[plane, group, REACH : REACH + 1, :] = nodes[4 * plane : 4 * plane + 1]

    def sides(o):
        return pl.ds(0, 2) if abs(o) < REACH else pl.ds(int(o > 0), 1)

    def sum_copy(z, o):
        return pltpu.make_async_remote_copy(
            src_ref=sums_ref.at[sides(o), group, pl.ds(REACH, 1), :],
            dst_ref=sums_ref.at[sides(o), group, pl.ds(REACH - o, 1), :],
            send_sem=sum_sent,
            recv_sem=sum_recv,
            device_id=(slab + o, z),
            device_id_type=MESH,
        )

    def whole(semaphore, rows_at):
        width = next(w for w in range(1, 9) if rows_at % w == 0 and rows_at // w <= stencil_ref.shape[0])
        view = stencil_ref.at[pl.ds(0, rows_at // width), pl.ds(0, width), :]
        return pltpu.make_async_remote_copy(src_ref=view, dst_ref=view, send_sem=semaphore, recv_sem=semaphore, device_id=(slab, group), device_id_type=MESH)

    def for_each_size(rows_of, act):
        sizes = {}
        for at in range(slabs):
            sizes.setdefault(rows_of(at), []).append(at)
        for total, places in sizes.items():
            here = functools.reduce(jnp.logical_or, [slab == at for at in places])

            @pl.when(here)
            def _():
                act(total)

    def sum_rows(at):
        return 2 * (groups - 1) + sum(groups * (2 if abs(o) < REACH else 1) for o in offsets if 0 <= at + o < slabs)

    def coef_rows(distance):
        return {1: ROWS, 2: ROWS - len(TURNS), 3: 1}[distance]

    def coef_got(at):
        crossing = at + (1 if at % 2 else -1)
        return sum(coef_rows(abs(o)) for o in offsets if 0 <= at + o < slabs and at + o != crossing)

    def coef_gone(at):
        outward = 1 if at % 2 else -1
        direct = [o for o in offsets if 0 <= at + o < slabs and o != 2 * outward]
        return sum(coef_rows(abs(o)) for o in direct) + (coef_rows(2) if 0 <= at + outward < slabs else 0)

    def coef_copy(o, arrived, source=0):
        far = abs(o - source)
        first = {1: 0, 2: 0 if o < source else 4, 3: 4 if o < source else 14}[far]
        count = coef_rows(far)
        return pltpu.make_async_remote_copy(
            src_ref=coef_ref.at[pl.ds(first, count), pl.ds(REACH + source, 1), :],
            dst_ref=coef_ref.at[pl.ds(first, count), pl.ds(REACH + source - o, 1), :],
            send_sem=coef_sent,
            recv_sem=arrived,
            device_id=(slab + o, group),
            device_id_type=MESH,
        )

    def send_sums(z, carry, upward=False):
        for o in sorted([0, *offsets], key=lambda o: (-abs(o), o) if upward else o):

            @pl.when(exists(o))
            def _():
                sum_copy(z, o).start()

        return carry

    lax.fori_loop(0, jnp.minimum(group, 1), send_sums, 0)
    tell(hello.at[jnp.maximum(group - 1, 0)], 1, group, [])
    hot = jnp.concatenate([one_hot(place[2 * b : 2 * b + 1]) for b in range(BLOCKS)], axis=1)
    ops = parts_of(ops_ref[...].reshape(64, LINE))
    lex = join_parts(lax.dot_general(ops, hot, (((1,), (1,)), ((), ())), preferred_element_type=jnp.float32))
    moved = [aligned(lex[8 * q : 8 * q + 8]) for q in range(8)]
    sub = rows_of((8, LANES))
    flat, flat_turns, _ = stencil_rows([jnp.where(sub < 4, moved[q], moved[q + 4]) for q in range(4)])
    centre, forward, backward = stencil_rows(moved[4:])
    rows = [(value, row) for value, row in flat_turns] + [flat, centre] + forward + backward
    rows += [(value, row + 4) for value, row in [flat] + flat_turns]
    for at, (value, row) in enumerate(rows):
        coef_ref[at, REACH : REACH + 1, :] = value[row : row + 1]
    even = slab % 2 == 0
    odd = jnp.logical_not(even)
    across = ((jnp.logical_and(even, exists(-1)), -1), (jnp.logical_and(odd, exists(1)), 1))
    @pl.when(jnp.logical_and(group == 0, greeted > 0))
    def _():
        pl.semaphore_wait(barrier, greeted)

    down, up = across
    for here, o, arrived in (
        (*down, cross_recv),
        (jnp.logical_and(odd, exists(-2)), -2, coef_recv),
        (*up, cross_recv),
        (jnp.logical_and(even, exists(2)), 2, coef_recv),
        (odd, -1, coef_recv),
        (even, 1, coef_recv),
        (exists(-3), -3, coef_recv),
        (exists(3), 3, coef_recv),
    ):

        @pl.when(here)
        def _():
            coef_copy(o, arrived).start()

    for o in sorted(offsets, key=lambda o: (-abs(o), o)):

        @pl.when(exists(o))
        def _():
            sum_copy(group, o).start()

    lax.fori_loop(1, group, send_sums, 0)

    def to_higher(z, carry):
        pl.semaphore_wait(hello.at[z - 1], every)
        return send_sums(z, carry, upward=True)

    lax.fori_loop(group + 1, groups, to_higher, 0)

    fine = []
    for k in range(2):
        column = jnp.full((8, 128), i31_ref[k, 0], jnp.float32)
        for c in range(1, 4):
            column = jnp.where((sub_tile & 3) == c, i31_ref[k, c], column)
        fine.append(column)
    weights = [jnp.where(sub_tile < 4, i31_ref[j, 2 * h], i31_ref[j, 2 * h + 1]) * fine[k] for h in range(2) for j in range(2) for k in range(2)]

    for here, o in across:

        @pl.when(here)
        def _():
            whole(cross_recv, ROWS).wait_recv()
            coef_copy(-o, coef_recv, source=o).start()

    for_each_size(coef_got, lambda total: whole(coef_recv, total).wait_recv())

    turns = len(TURNS)
    up_first = ROWS - turns
    steps = [STRIDE * dy + dx for dy, dx in TURNS]
    stencil_ref[0] = coef_ref[turns] + pltpu.roll(coef_ref[up_first - 1], 1, 0)
    middle = turns + 1
    stencil_ref[1] = pltpu.roll(coef_ref[middle], 1, 0)
    stencil_ref[2] = coef_ref[middle]
    for at, step in enumerate(steps):
        plane = coef_ref[at] + pltpu.roll(coef_ref[up_first + at], 1, 0)
        ahead, back = (coef_ref[middle + 1 + at], coef_ref[middle + 1 + turns + at])
        stencil_ref[3 + 6 * at] = plane
        stencil_ref[4 + 6 * at] = pltpu.roll(ahead, 1, 0)
        stencil_ref[5 + 6 * at] = pltpu.roll(back, LANES - step, 1)
        stencil_ref[6 + 6 * at] = pltpu.roll(plane, step, 1)
        stencil_ref[7 + 6 * at] = pltpu.roll(back, 1, 0)
        stencil_ref[8 + 6 * at] = pltpu.roll(ahead, step, 1)

    def operate(field):
        values = [field] + [pltpu.roll(field, shift, 1) for step in steps for shift in (LANES - step, step)]
        total = []
        for part in (1, 2, 0):
            terms = [stencil_ref[3 * at + part] * value for at, value in enumerate(values)]
            while len(terms) > 1:
                terms = [sum(terms[at : at + 2]) for at in range(0, len(terms), 2)]
            total.append(terms[0])
        return total[2] + pltpu.roll(total[0], 7, 0) + pltpu.roll(total[1], 1, 0)

    diag = stencil_ref[0]
    inverse = 1.0 / jnp.where(diag > 0.0, diag, 1.0)

    for_each_size(sum_rows, lambda total: whole(sum_sent, total).wait_send())
    for_each_size(sum_rows, lambda total: whole(sum_recv, total).wait_recv())

    low, high = [[sums_ref[plane, z] for z in range(groups)] for plane in range(2)]
    while len(low) > 1:
        low, high = [[sum(part[at : at + 2]) for at in range(0, len(part), 2)] for part in (low, high)]
    low, high = (low[0], high[0])
    remain = low + pltpu.roll(high, 1, 0)
    theta = 0.5 * (lam_high + lam_low)
    delta = 0.5 * (lam_high - lam_low)
    sigma = theta / delta
    direction = inverse * remain * (1.0 / theta)
    answer = direction
    rho = 1.0 / sigma
    for sweep in range(SWEEPS):
        remain = remain - operate(direction)
        rho_new = 1.0 / (2.0 * sigma - rho)
        direction = rho_new * rho * direction + 2.0 * rho_new / delta * inverse * remain
        answer = answer + direction
        rho = rho_new

    planes = jnp.where(sub < 4, spread(answer[REACH : REACH + 1]), spread(answer[REACH + 1 : REACH + 2]))
    found = [jnp.take_along_axis(planes[:, 128 * b : 128 * b + 128], own_lane, axis=1) for b in range(LANES // 128)]
    bit = 1
    while len(found) > 1:
        tall = (own_tile & bit) > 0
        found = [jnp.where(tall, two, one) for one, two in zip(found[0::2], found[1::2])] + found[len(found) // 2 * 2 :]
        bit *= 2
    picked = found[0]
    values = [spread(picked[p : p + 1]) for p in range(8)]
    for h in range(2):
        ends = [sum(weights[4 * h + q] * values[4 * i + q] for q in range(4)) for i in range(2)]
        for a in range(4):
            out_ref[8 * (2 * a + h) : 8 * (2 * a + h) + 8, :] = i31_ref[0, a] * ends[0] + i31_ref[1, a] * ends[1]

    for_each_size(coef_gone, lambda total: whole(coef_sent, total).wait_send())


def one_layer(resid7, interp73, interp31, elem_ops, conn):
    slabs, groups = (lax.axis_size("slab"), lax.axis_size("grp"))
    dma = pltpu.SemaphoreType.DMA
    return pl.pallas_call(
        functools.partial(cycle_kernel, slabs, groups),
        out_shape=pltpu.VMEM((64, 128), jnp.float32),
        in_specs=[pl.BlockSpec(memory_space=pl.ANY)] * 5,
        out_specs=VMEM,
        scratch_shapes=[
            pltpu.VMEM((8, LINE), jnp.int32),
            pltpu.VMEM((8, 8, LINE), jnp.float32),
            pltpu.VMEM((512, 128), jnp.float32),
            pltpu.SMEM((4, 8), jnp.float32),
            pltpu.SMEM((2, 4), jnp.float32),
            dma((2,)),
            pltpu.VMEM((2, groups, 8, LANES), jnp.float32),
            pltpu.VMEM((ROWS, 8, LANES), jnp.float32),
            pltpu.VMEM((3 + 6 * len(TURNS), 8, LANES), jnp.float32),
            pltpu.SemaphoreType.REGULAR((groups - 1,)),
            dma,
            dma,
            dma,
            dma,
            dma,
        ],
        compiler_params=pltpu.CompilerParams(collective_id=0, has_side_effects=True),
    )(conn, elem_ops, resid7, interp73.T, interp31.T)


def dispatch(resid7, interp73, interp31, elem_ops, conn, faces):
    if conn.shape[1] == LINE and resid7.shape[1] == 128 and lax.axis_size("grp") > 1 and lax.axis_size("slab") % 2 == 0:
        return one_layer(resid7, interp73, interp31, elem_ops, conn)
    return local(resid7, interp73, interp31, elem_ops, conn, faces)


def solution(mesh):
    in_specs = (
        P(None, ("slab", "grp")),
        P(),
        P(),
        P(None, None, "slab"),
        P(None, "slab"),
        P(None, "slab", None),
    )
    out_specs = P(None, ("slab", "grp"))
    return jax.shard_map(dispatch, mesh=mesh, in_specs=in_specs, out_specs=out_specs, check_vma=False)
```
